32 devices in a mesh: dp: 16 (over z, x, core), tensor: 2 (over y).
Axes of the slice: x: 2, y: 2, z: 4, core: 2. Of those that a mesh axis runs over, the one named last changes fastest.
Arguments:
- tokens: bfloat16 [16384, 768], P('dp'), may hold values from -6 to 6
- memory: bfloat16 [128, 256, 768], P('dp'), may hold values from -6 to 6
- groups: int32 [256], P('dp'), may hold values from 0 to 127, as said below
- norm_gains: float32 [3, 768], replicated, may hold values from 0.1 to 1.9
- norm_biases: float32 [3, 768], replicated, may hold values from -1.2 to 1.2
- self_qkv: bfloat16 [3, 768, 768], P(None, None, 'tensor'), may hold values from -0.3125 to 0.3125
- self_out: bfloat16 [768, 768], P('tensor'), may hold values from -0.625 to 0.625
- cross_query: bfloat16 [768, 768], P(None, 'tensor'), may hold values from -0.3125 to 0.3125
- cross_kv: bfloat16 [2, 768, 768], P(None, None, 'tensor'), may hold values from -0.3125 to 0.3125
- cross_out: bfloat16 [768, 768], P('tensor'), may hold values from -0.875 to 0.875
- mlp_up: bfloat16 [768, 3072], P(None, 'tensor'), may hold values from -0.21875 to 0.21875
- mlp_down: bfloat16 [3072, 768], P('tensor'), may hold values from -0.15625 to 0.15625
- cotangent: bfloat16 [16384, 768], P('dp'), may hold values from -6 to 6
Outputs:
- output: bfloat16 [16384, 768], P('dp')
- input_grad: bfloat16 [16384, 768], P('dp')
- memory_grad: bfloat16 [128, 256, 768], P('dp', None, 'tensor')
- norm_gains_grad: float32 [3, 768], replicated
- norm_biases_grad: float32 [3, 768], replicated
- self_qkv_grad: float32 [3, 768, 768], P(None, None, 'tensor')
- self_out_grad: float32 [768, 768], P('tensor')
- cross_query_grad: float32 [768, 768], P(None, 'tensor')
- cross_kv_grad: float32 [2, 768, 768], P(None, None, 'tensor')
- cross_out_grad: float32 [768, 768], P('tensor')
- mlp_up_grad: float32 [768, 3072], P(None, 'tensor')
- mlp_down_grad: float32 [3072, 768], P('tensor')
The draws below stay inside these ranges and needn't reach their ends.
Inputs may be any that keep to these rules, and one draw needn't show every extreme that they name: `groups`: captions of index p of dp read only that index's images, numbers p * 8 to (p + 1) * 8 - 1, and each image is read by exactly two captions.
All inputs are finite; a program needn't handle non-finite values.
Results may differ from the reference program's by a relative error of at most 0.023.
The reference program's roundings to bfloat16 on the way count: a program that leaves them out, or rounds other values in their place, can miss the bound.
Values may be sent and summed in bfloat16 or wider, within the bound.
A program may use at most 192 MiB of HBM per device.

```python
import jax
import jax.numpy as jnp
from jax import lax

D = 768
HEADS = 12
HEAD_DIM = 64
FF = 3072
MEM = 256
LENGTH = 64
CAP_DEV = 16
IMG_DEV = 8
CAPTIONS = 256
IMAGES = 128
TOKENS = 16384
N_DP = 16


def shuffle_block(block_key):
    return jax.random.permutation(block_key, CAP_DEV)


def draw_groups(key, part):
    block_keys = jax.random.split(jax.random.fold_in(key, 17), N_DP)
    orders = jax.vmap(shuffle_block)(block_keys).astype(jnp.int32)
    offsets = jnp.arange(N_DP, dtype=jnp.int32)[:, None] * IMG_DEV
    return (orders // 2 + offsets).reshape(CAPTIONS).astype(jnp.int32)


def steps_of(own_key, extent, shards, smallest, high):
    loudness = 1.0
    for position, parts in shards:
        heights = jax.random.uniform(jax.random.fold_in(jax.random.fold_in(own_key, 6), position), (parts,), jnp.float32, smallest / len(shards), high / len(shards))
        loudness = loudness * jnp.repeat(jnp.exp(heights), extent[position] // parts).reshape((-1,) + (1,) * (len(extent) - 1 - position))
    return loudness


def scatter_about(own_key, extent, deviation, bound, pieces=(), kind=jnp.bfloat16):
    values = jax.random.normal(own_key, extent, jnp.float32) * deviation
    if len(pieces) > 0:
        values = steps_of(own_key, extent, pieces, -0.22, 0.18) * values
    return jnp.clip(values, min=-bound, max=bound).astype(kind)


def setup_inputs(seed: int = 0) -> dict:
    arg_keys = jax.random.split(jax.random.key(seed), 14)
    tokens = scatter_about(arg_keys[0], (TOKENS, D), 1.0, 6.0, ((0, 16),))
    memory = scatter_about(arg_keys[1], (IMAGES, MEM, D), 1.0, 6.0, ((0, 16),))
    groups = draw_groups(jax.random.fold_in(arg_keys[13], 71), 0)
    norm_gains = jnp.clip(1.0 + 0.18 * jax.random.normal(arg_keys[3], (3, D), jnp.float32), 0.1, 1.9)
    norm_biases = scatter_about(arg_keys[4], (3, D), 0.3, 1.2, (), jnp.float32)
    self_qkv = scatter_about(arg_keys[5], (3, D, D), (D // 2) ** -0.5, 0.3125, ((2, 2),))
    self_out = scatter_about(arg_keys[6], (D, D), (D // 8) ** -0.5, 0.625, ((0, 2),))
    cross_query = scatter_about(arg_keys[7], (D, D), (D // 2) ** -0.5, 0.3125, ((1, 2),))
    cross_kv = scatter_about(arg_keys[8], (2, D, D), (D // 2) ** -0.5, 0.3125, ((2, 2),))
    cross_out = scatter_about(arg_keys[9], (D, D), (D // 16) ** -0.5, 0.875, ((0, 2),))
    mlp_up = scatter_about(arg_keys[10], (D, FF), D ** -0.5, 0.21875, ((1, 2),))
    mlp_down = scatter_about(arg_keys[11], (FF, D), (FF // 2) ** -0.5, 0.15625, ((0, 2),))
    cotangent = scatter_about(arg_keys[12], (TOKENS, D), 1.0, 6.0, ((0, 16),))
    return dict(tokens=tokens, memory=memory, groups=groups, norm_gains=norm_gains, norm_biases=norm_biases, self_qkv=self_qkv, self_out=self_out, cross_query=cross_query, cross_kv=cross_kv, cross_out=cross_out, mlp_up=mlp_up, mlp_down=mlp_down, cotangent=cotangent)


@jax.custom_vjp
def low(v):
    return lax.optimization_barrier(v.astype(jnp.bfloat16)).astype(jnp.float32)

@jax.custom_vjp
def low_back(v):
    return v

def low_keep(v):
    return (low(v), None)

def low_pass(kept, grad):
    return (grad,)

def back_keep(v):
    return (v, None)

def back_low(kept, grad):
    return (low(grad),)
low.defvjp(low_keep, low_pass)
low_back.defvjp(back_keep, back_low)
epsilon = 1e-05
highest = lax.Precision.HIGHEST

def lowered_both(values):
    return low_back(low(values))

def matmul(left_side, right_side):
    return jnp.dot(left_side, right_side, precision=highest, preferred_element_type=jnp.float32)

def normalize(values, gain_row, bias_row):
    average = lax.optimization_barrier(jnp.mean(values, axis=-1, keepdims=True))
    centred = values - average
    inverse = lax.rsqrt(lax.optimization_barrier(jnp.mean(centred * centred, axis=-1, keepdims=True)) + epsilon)
    return centred * inverse * gain_row + bias_row

def attend(queries, key_heads, value_heads, causal):
    scores = low_back(jnp.einsum('clhe,ckhe->chlk', queries, key_heads, precision=highest) * HEAD_DIM ** (-0.5))
    if causal:
        allowed = lax.broadcasted_iota(jnp.int32, scores.shape, 2) >= lax.broadcasted_iota(jnp.int32, scores.shape, 3)
        scores = jnp.where(allowed, scores, -1e+30)
    weights = low(jax.nn.softmax(scores, axis=-1))
    return jnp.einsum('chlk,ckhe->clhe', weights, value_heads, precision=highest)

def layer(params, tokens, memory, local_groups):
    norm_gains, norm_biases, self_qkv, self_out, cross_query, cross_kv, cross_out, mlp_up, mlp_down = params
    heads_shape = (CAP_DEV, LENGTH, HEADS, HEAD_DIM)
    row_count = CAP_DEV * LENGTH
    first_norm = low(normalize(tokens, norm_gains[0], norm_biases[0]))
    queries = lowered_both(matmul(first_norm, self_qkv[0])).reshape(heads_shape)
    key_heads = lowered_both(matmul(first_norm, self_qkv[1])).reshape(heads_shape)
    value_heads = lowered_both(matmul(first_norm, self_qkv[2])).reshape(heads_shape)
    mixed_heads = lowered_both(attend(queries, key_heads, value_heads, True).reshape(row_count, D))
    hidden_one = tokens + low_back(matmul(mixed_heads, self_out))
    second = low(normalize(hidden_one, norm_gains[1], norm_biases[1]))
    cross_queries = lowered_both(matmul(second, cross_query)).reshape(heads_shape)
    flat_memory = memory.reshape(IMG_DEV * MEM, D)
    memory_keys = lowered_both(matmul(flat_memory, cross_kv[0])).reshape(IMG_DEV, MEM, HEADS, HEAD_DIM)
    memory_values = lowered_both(matmul(flat_memory, cross_kv[1])).reshape(IMG_DEV, MEM, HEADS, HEAD_DIM)
    caption_keys = jnp.take(memory_keys, local_groups, axis=0)
    caption_values = jnp.take(memory_values, local_groups, axis=0)
    cross_mixed = lowered_both(attend(cross_queries, caption_keys, caption_values, False).reshape(row_count, D))
    hidden_two = hidden_one + low_back(matmul(cross_mixed, cross_out))
    third_norm = low(normalize(hidden_two, norm_gains[2], norm_biases[2]))
    upward = low_back(matmul(third_norm, mlp_up))
    active = low(jax.nn.gelu(upward, approximate=False))
    return hidden_two + low_back(matmul(active, mlp_down))

def add_pair(earlier, later):
    return earlier + later

def reference(tokens, memory, groups, norm_gains, norm_biases, self_qkv, self_out, cross_query, cross_kv, cross_out, mlp_up, mlp_down, cotangent):
    params = (norm_gains.astype(jnp.float32), norm_biases.astype(jnp.float32), self_qkv.astype(jnp.float32), self_out.astype(jnp.float32), cross_query.astype(jnp.float32), cross_kv.astype(jnp.float32), cross_out.astype(jnp.float32), mlp_up.astype(jnp.float32), mlp_down.astype(jnp.float32))
    block_rows = CAP_DEV * LENGTH
    token_blocks = tokens.astype(jnp.float32).reshape(N_DP, block_rows, D)
    memory_blocks = memory.astype(jnp.float32).reshape(N_DP, IMG_DEV, MEM, D)
    group_blocks = groups.reshape(N_DP, CAP_DEV)
    cotangent_blocks = cotangent.astype(jnp.float32).reshape(N_DP, block_rows, D)
    block_numbers = jnp.arange(N_DP, dtype=jnp.int32)

    def one_block(totals, inputs):
        block_index, block_tokens, block_memory, block_groups, block_cotangent = inputs
        local_groups = (block_groups - block_index * IMG_DEV).astype(jnp.int32)

        def forward(pars, token_rows, memory_rows):
            return layer(pars, token_rows, memory_rows, local_groups)
        result, pullback = jax.vjp(forward, params, block_tokens, block_memory)
        weight_grads, token_grad, memory_grad = pullback(block_cotangent)
        totals = jax.tree.map(add_pair, totals, weight_grads)
        return (totals, (result, token_grad, memory_grad))
    zeros = jax.tree.map(jnp.zeros_like, params)
    totals, outputs = lax.scan(one_block, zeros, (block_numbers, token_blocks, memory_blocks, group_blocks, cotangent_blocks))
    results, token_grads, memory_grads = outputs
    output = results.reshape(TOKENS, D).astype(jnp.bfloat16)
    input_grad = token_grads.reshape(TOKENS, D).astype(jnp.bfloat16)
    memory_grad = memory_grads.reshape(IMAGES, MEM, D).astype(jnp.bfloat16)
    return (output, input_grad, memory_grad, totals[0], totals[1], totals[2], totals[3], totals[4], totals[5], totals[6], totals[7], totals[8])
```

```python
import functools

import jax
import jax.numpy as jnp
from jax import lax
from jax.experimental import pallas as pl
from jax.experimental.pallas import tpu as pltpu
from jax.sharding import PartitionSpec as P

HEAD_DIM = 64
SCALE = HEAD_DIM**-0.5
PAIR = 2 * HEAD_DIM
EPSILON = 1e-05
ROOT_HALF = 0.7071067811865476
PDF_SCALE = 0.3989422804014327
MESH = pl.DeviceIdType.MESH
LOW = jnp.bfloat16
F32 = jnp.float32
VMEM_LIMIT = 60 * 1024 * 1024
ANY = pl.BlockSpec(memory_space=pl.ANY)
VMEM = pl.BlockSpec(memory_space=pltpu.VMEM)


def nn(left, right):
    return lax.dot_general(left, right, (((1,), (0,)), ((), ())), preferred_element_type=F32)


def nt(left, right):
    return lax.dot_general(left, right, (((1,), (1,)), ((), ())), preferred_element_type=F32)


def tn(left, right):
    return lax.dot_general(left, right, (((0,), (0,)), ((), ())), preferred_element_type=F32)


def standardize(values):
    average = jnp.mean(values, axis=-1, keepdims=True)
    centred = values - average
    inverse = lax.rsqrt(jnp.mean(centred * centred, axis=-1, keepdims=True) + EPSILON)
    return centred * inverse, inverse


def standardize_back(grad_out, scaled, inverse, gain_row):
    weighted = grad_out * gain_row
    return inverse * (
        weighted
        - jnp.mean(weighted, axis=-1, keepdims=True)
        - scaled * jnp.mean(weighted * scaled, axis=-1, keepdims=True)
    )


def column_sum(values):
    return jnp.sum(values, axis=0, keepdims=True)


def softmax(scores):
    top = jnp.max(scores, axis=-1, keepdims=True)
    weights = jnp.exp(scores - top)
    return weights * (1.0 / jnp.sum(weights, axis=-1, keepdims=True))


def first_lanes():
    return lax.broadcasted_iota(jnp.int32, (1, PAIR), 1) < HEAD_DIM


def split_heads(values):
    zeros = jnp.zeros_like(values)
    first = first_lanes()
    return jnp.where(first, values, zeros), jnp.where(first, zeros, values)


def caption_mask(rows, length):
    query = lax.broadcasted_iota(jnp.int32, (rows, rows), 0)
    key = lax.broadcasted_iota(jnp.int32, (rows, rows), 1)
    return (query // length == key // length) & (query >= key)


def attend(queries, keys, values, allowed):
    mixed = []
    for part in split_heads(queries * jnp.asarray(SCALE, LOW)):
        scores = nt(part, keys)
        if allowed is not None:
            scores = jnp.where(allowed, scores, -1e30)
        mixed.append(nn(softmax(scores).astype(LOW), values))
    return jnp.where(first_lanes(), mixed[0], mixed[1]).astype(LOW)


def attend_back(queries, keys, values, grads, allowed):
    query_grads = []
    key_grad = None
    value_grad = None
    for part, grad in zip(split_heads(queries * jnp.asarray(SCALE, LOW)), split_heads(grads)):
        scores = nt(part, keys)
        if allowed is not None:
            scores = jnp.where(allowed, scores, -1e30)
        probs = softmax(scores)
        prob_grad = nt(grad, values)
        score_grad = probs * (prob_grad - jnp.sum(probs * prob_grad, axis=-1, keepdims=True))
        score_low = score_grad.astype(LOW)
        query_grads.append(nn(score_low, keys))
        more_keys = tn(score_low, part)
        more_values = tn(probs.astype(LOW), grad)
        key_grad = more_keys if key_grad is None else key_grad + more_keys
        value_grad = more_values if value_grad is None else value_grad + more_values
    query_grad = jnp.where(first_lanes(), query_grads[0], query_grads[1]) * SCALE
    return query_grad.astype(LOW), key_grad.astype(LOW), value_grad.astype(LOW)


class Stores:
    def __init__(self, sems):
        self.sems = sems
        self.copies = []

    def __call__(self, source, target):
        copy = pltpu.make_async_copy(source, target, self.sems.at[len(self.copies)])
        copy.start()
        self.copies.append(copy)

    def wait(self):
        for copy in self.copies:
            copy.wait()


def self_forward(length, x, gains, biases, qkv0, qkv1, out0, out1, h1, s0, s1, o0, o1):
    scaled, _ = standardize(x[...].astype(F32))
    low = (scaled * gains[0:1] + biases[0:1]).astype(LOW)
    pair_rows = 2 * length
    for weight, saved in ((qkv0, s0), (qkv1, s1)):
        for j in range(3):
            saved[j] = nn(low, weight[j]).astype(LOW)
    groups = x.shape[0] // pair_rows
    for saved, mixed in ((s0, o0), (s1, o1)):

        @pl.loop(0, groups)
        def _(step):
            rows = pl.ds(pl.multiple_of(step * pair_rows, pair_rows), pair_rows)
            allowed = caption_mask(pair_rows, length)
            for lane in range(0, saved.shape[2], PAIR):
                lanes = slice(lane, lane + PAIR)
                mixed[rows, lanes] = attend(
                    saved[0, rows, lanes], saved[1, rows, lanes], saved[2, rows, lanes], allowed
                )

    h1[...] = x[...].astype(F32) + (nn(o0[...], out0[...]) + nn(o1[...], out1[...]))


def cross_forward(span, h1, memory, gains, biases, q0, q1, kv0, kv1, out0, out1, h2, c, qc0, qc1, m0, m1, o0, o1):
    scaled, _ = standardize(h1[...])
    c[...] = (scaled * gains[1:2] + biases[1:2]).astype(LOW)
    images = memory.shape[0] // span
    pair_rows = h1.shape[0] // images
    for weight, query, kv, saved in ((q0, qc0, kv0, m0), (q1, qc1, kv1, m1)):
        query[...] = nn(c[...], weight[...]).astype(LOW)
        for j in range(2):
            saved[j] = nn(memory[...], kv[j]).astype(LOW)
    for query, saved, mixed in ((qc0, m0, o0), (qc1, m1, o1)):

        @pl.loop(0, images)
        def _(step):
            rows = pl.ds(pl.multiple_of(step * pair_rows, pair_rows), pair_rows)
            keys = pl.ds(pl.multiple_of(step * span, span), span)
            for lane in range(0, saved.shape[2], PAIR):
                lanes = slice(lane, lane + PAIR)
                mixed[rows, lanes] = attend(
                    query[rows, lanes], saved[0, keys, lanes], saved[1, keys, lanes], None
                )

    h2[...] = h1[...] + (nn(o0[...], out0[...]) + nn(o1[...], out1[...]))


def mlp(
    chunk, h2, cot, gains, biases, up0, up1, down0, down1,
    result, dh2, g0, g1, gain_grad, bias_grad, acc, back, low_ref, parts, sems,
):
    width = h2.shape[1]
    scaled, inverse = standardize(h2[...])
    low_ref[...] = (scaled * gains[2:3] + biases[2:3]).astype(LOW)
    acc[...] = h2[...]
    back[...] = jnp.zeros_like(back)
    hidden = up0.shape[1]
    turned = low_ref[...].T
    store = Stores(sems)
    for half, (up, down, grads) in enumerate(((up0, down0, g0), (up1, down1, g1))):
        for start in range(0, hidden, chunk):
            cols = slice(start, start + chunk)
            u = nn(low_ref[...], up[:, cols])
            below = 0.5 + 0.5 * lax.erf(u * ROOT_HALF)
            z = (u * below).astype(LOW)
            acc[...] += nn(z, down[cols, :])
            dz = nt(cot[...], down[cols, :])
            slope = below + u * (PDF_SCALE * jnp.exp(-0.5 * u * u))
            du = (dz * slope).astype(LOW)
            back[...] += nt(du, up[:, cols])
            down_rows = slice(hidden // chunk * width + start, hidden // chunk * width + start + chunk)
            parts[half, down_rows, :] = tn(z, cot[...]).astype(LOW)
            store(parts.at[half, down_rows], grads.at[down_rows])
            up_rows = slice(start // chunk * width, start // chunk * width + width)
            parts[half, up_rows, :] = nn(turned, du).astype(LOW)
            store(parts.at[half, up_rows], grads.at[up_rows])
    result[...] = acc[...].astype(LOW)
    grad = back[...]
    scaled, inverse = standardize(h2[...])
    gain_grad[...] = column_sum(grad * scaled)
    bias_grad[...] = column_sum(grad)
    dh2[...] = cot[...].astype(F32) + standardize_back(grad, scaled, inverse, gains[2:3])
    store.wait()


def cross_back(
    span, dh2, h1, memory, gains, c, q0, q1, kv0, kv1, out0, out1, qc0, qc1, m0, m1, o0, o1,
    dh1, g0, g1, memory_grad, gain_grad, bias_grad, low, dmix, dq, dkv, back, mem_acc, kv_part, query_part, out_part, sems,
):
    store = Stores(sems)
    low[...] = dh2[...].astype(LOW)
    images = memory.shape[0] // span
    pair_rows = h1.shape[0] // images
    local = q0.shape[1]
    width = h1.shape[1]
    for half, (query, kv, out, qc, saved, mixed, grads) in enumerate(
        ((q0, kv0, out0, qc0, m0, o0, g0), (q1, kv1, out1, qc1, m1, o1, g1))
    ):
        out_part[half] = tn(mixed[...], low[...]).astype(LOW)
        store(out_part.at[half], grads.at[3 * width + local : 4 * width])
        dmix[...] = nt(low[...], out[...]).astype(LOW)

        @pl.loop(0, images)
        def _(step):
            rows = pl.ds(pl.multiple_of(step * pair_rows, pair_rows), pair_rows)
            keys = pl.ds(pl.multiple_of(step * span, span), span)
            for lane in range(0, local, PAIR):
                lanes = slice(lane, lane + PAIR)
                a, b, d = attend_back(
                    qc[rows, lanes], saved[0, keys, lanes], saved[1, keys, lanes], dmix[rows, lanes], None
                )
                dq[rows, lanes] = a
                dkv[0, keys, lanes] = b
                dkv[1, keys, lanes] = d

        query_part[half] = tn(c[...], dq[...]).astype(LOW)
        store(query_part.at[half], grads.at[width : 2 * width, local:])
        kv_part[half, :, :local] = tn(memory[...], dkv[0]).astype(LOW)
        kv_part[half, :, local:] = tn(memory[...], dkv[1]).astype(LOW)
        store(kv_part.at[half], grads.at[2 * width : 3 * width])
        more = nt(dq[...], query[...])
        more_memory = nt(dkv[0], kv[0]) + nt(dkv[1], kv[1])
        if half == 0:
            back[...] = more
            mem_acc[...] = more_memory
        else:
            grad = back[...] + more
            total = (mem_acc[...] + more_memory).astype(LOW)
            memory_grad[0] = total[:, :local]
            memory_grad[1] = total[:, local:]
            scaled, inverse = standardize(h1[...])
            gain_grad[...] = column_sum(grad * scaled)
            bias_grad[...] = column_sum(grad)
            dh1[...] = dh2[...] + standardize_back(grad, scaled, inverse, gains[1:2])
    store.wait()


def self_back(
    length, dh1, x, gains, biases, qkv0, qkv1, out0, out1, s0, s1, o0, o1, old0, old1,
    result, g0, g1, gain_grad, bias_grad, low, a_ref, dmix, dqkv, back, pair_part, value_part, out_part, sems,
):
    store = Stores(sems)
    low[...] = dh1[...].astype(LOW)
    scaled, inverse = standardize(x[...].astype(F32))
    a_ref[...] = (scaled * gains[0:1] + biases[0:1]).astype(LOW)
    pair_rows = 2 * length
    groups = x.shape[0] // pair_rows
    local = o0.shape[1]
    width = x.shape[1]
    turned = a_ref[...].T
    for half, (qkv, out, saved, mixed, grads) in enumerate(
        ((qkv0, out0, s0, o0, g0), (qkv1, out1, s1, o1, g1))
    ):
        out_part[half] = tn(mixed[...], low[...]).astype(LOW)
        store(out_part.at[half], grads.at[3 * width : 3 * width + local])
        dmix[...] = nt(low[...], out[...]).astype(LOW)

        @pl.loop(0, groups)
        def _(step):
            rows = pl.ds(pl.multiple_of(step * pair_rows, pair_rows), pair_rows)
            allowed = caption_mask(pair_rows, length)
            for lane in range(0, local, PAIR):
                lanes = slice(lane, lane + PAIR)
                a, b, d = attend_back(
                    saved[0, rows, lanes], saved[1, rows, lanes], saved[2, rows, lanes], dmix[rows, lanes], allowed
                )
                dqkv[0, rows, lanes] = a
                dqkv[1, rows, lanes] = b
                dqkv[2, rows, lanes] = d

        pair_part[half, :, :local] = nn(turned, dqkv[0]).astype(LOW)
        pair_part[half, :, local:] = nn(turned, dqkv[1]).astype(LOW)
        store(pair_part.at[half], grads.at[0:width])
        value_part[half] = nn(turned, dqkv[2]).astype(LOW)
        store(value_part.at[half], grads.at[width : 2 * width, :local])
        more = nt(dqkv[0], qkv[0]) + nt(dqkv[1], qkv[1]) + nt(dqkv[2], qkv[2])
        if half == 0:
            back[...] = more
        else:
            grad = back[...] + more
            scaled, inverse = standardize(x[...].astype(F32))
            gain_grad[...] = column_sum(grad * scaled)
            bias_grad[...] = column_sum(grad)
            result[...] = (dh1[...] + standardize_back(grad, scaled, inverse, gains[0:1])).astype(LOW)
    store.wait()


def partner(axis):
    dp = lax.axis_index("dp")
    side = lax.axis_index("tensor")
    if axis == "y":
        return dp, 1 - side
    if axis == "core":
        return dp + 1 - 2 * (dp % 2), side
    return dp + 2 - 4 * ((dp // 2) % 2), side


def greet(devices):
    barrier = pltpu.get_barrier_semaphore()
    for device in devices:
        pl.semaphore_signal(barrier, inc=1, device_id=device, device_id_type=MESH)
    pl.semaphore_wait(barrier, len(devices))


def remote(source, target, send, recv, device):
    return pltpu.make_async_remote_copy(
        src_ref=source, dst_ref=target, send_sem=send, recv_sem=recv, device_id=device, device_id_type=MESH
    )


def fetch_weights(count, *refs):
    mine, theirs = refs[:count], refs[count : 2 * count]
    sent, got = refs[2 * count :]
    y, x, core = partner("y"), partner("x"), partner("core")
    dp = lax.axis_index("dp")
    here = dp % 4
    there = here + 2 - 4 * (here // 2)
    greet((y, x, core))

    def piece(ref, number):
        size = ref.shape[0] // 4
        return ref.at[pl.ds(pl.multiple_of(number * size, size), size)]

    def move(k, lane, number, device, source=None):
        spot = piece(theirs[k], number)
        return remote(spot if source is None else source, spot, sent.at[lane, k], got.at[lane, k], device)

    first = [move(k, 0, here, y, piece(mine[k], here)) for k in range(count)]
    for copy in first:
        copy.start()
    later = []
    for k in range(count):
        first[k].wait_recv()
        for lane, device in ((1, x), (2, core)):
            copy = move(k, lane, here, device)
            copy.start()
            later.append(copy)
    last = []
    for k in range(count):
        later[2 * k].wait_recv()
        copy = move(k, 3, there, core)
        copy.start()
        last.append(copy)
    for k in range(count):
        later[2 * k + 1].wait_recv()
        last[k].wait_recv()
    for copy in first + later + last:
        copy.wait_send()


def reduce_grads(chips, *refs):
    (m0, m1, a0, a1, out_half, in_half, mem_half, m_sum, a_sum, out_all, in_all, mem_all) = refs[:12]
    (own, other, core_own, core_other, from_y, ring, local_sem, core_sent, core_got, y_sent, y_got,
     ring_sent, ring_got, gather_sent, gather_got, back_sent, back_got, final_sem, act_sem, act_sent, act_got) = refs[12:]
    dp = lax.axis_index("dp")
    side = lax.axis_index("tensor")
    core = dp % 2
    line = dp // 4
    lane = (dp // 2) % 2
    long = chips // 2
    place = line + lane * (chips - 1 - 2 * line)

    def at(position):
        position = (position + chips) % chips
        x = position // long
        z = position + x * (chips - 1 - 2 * position)
        return 4 * z + 2 * x + core, side

    y, mate = partner("y"), partner("core")
    toward = (at(place + 1), at(place - 1))
    greet((y, mate, *toward))
    rows = own.shape[3]
    quarter = chips * rows

    def spot(ref, which, direction, number):
        base = (which * 2 + direction) * quarter + number * rows
        return ref.at[pl.ds(pl.multiple_of(base, rows), rows)]

    def number(direction, step):
        return (place + (2 * chips - step if direction == 0 else step)) % chips

    parts = ((m0, m1, m_sum), (a0, a1, a_sum))
    lanes = [(p, d) for p in range(2) for d in range(2)]

    def acts():
        copies = []
        for i, (half, whole) in enumerate(((out_half, out_all), (in_half, in_all))):
            size = half.shape[0]
            target = whole.at[pl.ds(pl.multiple_of(side * size, size), size)]
            copies.append((half, half, target, i))
        size = mem_half.shape[1]
        target = mem_all.at[pl.ds(pl.multiple_of(side * size, size), size)]
        copies.append((mem_half.at[side], mem_half.at[1 - side], target, 2))
        local = [pltpu.make_async_copy(a, t, act_sem.at[i]) for a, _, t, i in copies]
        away = [remote(b, t, act_sent.at[i], act_got.at[i], y) for _, b, t, i in copies]
        return local, away

    def loads(p, d, s):
        k = number(d, s)
        return (
            pltpu.make_async_copy(spot(parts[p][0], core, d, k), own.at[p, d, s], local_sem.at[0, p, d, s]),
            pltpu.make_async_copy(spot(parts[p][1], core, d, k), other.at[p, d, s], local_sem.at[1, p, d, s]),
        )

    def to_mate(p, d, s):
        k = number(d, s)
        return (
            remote(spot(parts[p][0], 1 - core, d, k), core_own.at[p, d, s], core_sent.at[0, p, d, s],
                   core_got.at[0, p, d, s], mate),
            remote(spot(parts[p][1], 1 - core, d, k), core_other.at[p, d, s], core_sent.at[1, p, d, s],
                   core_got.at[1, p, d, s], mate),
        )

    def to_y(p, d, s):
        return remote(other.at[p, d, s], from_y.at[p, d, s], y_sent.at[p, d, s], y_got.at[p, d, s], y)

    def to_next(p, d, s):
        return remote(own.at[p, d, s], ring.at[p, d, s], ring_sent.at[p, d, s], ring_got.at[p, d, s], toward[d])

    def gather(p, d, s):
        k = number(d, s + chips - 1)
        source = own.at[p, d, chips - 1] if isinstance(s, int) and s == 0 else spot(parts[p][2], core, d, k)
        return remote(source, spot(parts[p][2], core, d, k), gather_sent.at[p, d, s], gather_got.at[p, d, s], toward[d])

    def give_back(p, d, s):
        k = number(d, s + chips - 1)
        source = own.at[p, d, chips - 1] if isinstance(s, int) and s == 0 else spot(parts[p][2], core, d, k)
        return remote(source, spot(parts[p][2], core, d, k), back_sent.at[p, d, s], back_got.at[p, d, s], mate)

    @pl.loop(0, chips)
    def _(s):
        for p, d in lanes:
            for copy in (*loads(p, d, s), *to_mate(p, d, s)):
                copy.start()

    def first(s):
        for p, d in lanes:
            for copy in loads(p, d, s):
                copy.wait()
            for copy in to_mate(p, d, s):
                copy.wait_recv()
            other[p, d, s] = (other[p, d, s].astype(F32) + core_other[p, d, s].astype(F32)).astype(LOW)
            to_y(p, d, s).start()

    def second(s, start):
        for p, d in lanes:
            to_y(p, d, s).wait_recv()
            total = own[p, d, s].astype(F32) + core_own[p, d, s].astype(F32) + from_y[p, d, s].astype(F32)
            if not start:
                to_next(p, d, s - 1).wait_recv()
                total = total + ring[p, d, s - 1].astype(F32)
            own[p, d, s] = total.astype(LOW)

    first(0)
    first(1)
    second(0, True)
    for p, d in lanes:
        to_next(p, d, 0).start()

    @pl.loop(1, chips - 1)
    def _(s):
        first(s + 1)
        second(s, False)
        for p, d in lanes:
            to_next(p, d, s).start()

    local, away = acts()
    for copy in local + away:
        copy.start()
    second(chips - 1, False)
    finals = []
    for p, d in lanes:
        k = number(d, chips - 1)
        copy = pltpu.make_async_copy(own.at[p, d, chips - 1], spot(parts[p][2], core, d, k), final_sem.at[p, d])
        copy.start()
        finals.append(copy)
        gather(p, d, 0).start()
        give_back(p, d, 0).start()

    @pl.loop(1, chips - 1)
    def _(s):
        for p, d in lanes:
            gather(p, d, s - 1).wait_recv()
            gather(p, d, s).start()
            give_back(p, d, s).start()

    for p, d in lanes:
        gather(p, d, chips - 2).wait_recv()
        give_back(p, d, chips - 1).start()

    for copy in finals + local:
        copy.wait()
    for copy in away:
        copy.wait()

    @pl.loop(0, chips)
    def _(s):
        for p, d in lanes:
            for copy in to_mate(p, d, s):
                copy.wait_send()
            to_y(p, d, s).wait_send()
            give_back(p, d, s).wait()

    @pl.loop(0, chips - 1)
    def _(s):
        for p, d in lanes:
            to_next(p, d, s).wait_send()
            gather(p, d, s).wait_send()


def take_rows(order_ref, a_ref, b_ref, a_out, b_out):
    a_out[...] = a_ref[...]
    b_out[...] = b_ref[...]


def take_captions(order, length, first, second):
    width = first.shape[1]
    count = order.shape[0]
    source = pl.BlockSpec((length, width), lambda i, order_ref: (order_ref[i], 0))
    target = pl.BlockSpec((length, width), lambda i, order_ref: (i, 0))
    shape = jax.ShapeDtypeStruct((count * length, width), first.dtype)
    return pl.pallas_call(
        take_rows,
        grid_spec=pltpu.PrefetchScalarGridSpec(
            num_scalar_prefetch=1, grid=(count,), in_specs=[source, source], out_specs=[target, target]
        ),
        out_shape=[shape, shape],
        name="take_captions",
    )(order, first, second)


def put_captions(order, length, first, second):
    width = first.shape[1]
    count = order.shape[0]
    source = pl.BlockSpec((length, width), lambda i, order_ref: (i, 0))
    target = pl.BlockSpec((length, width), lambda i, order_ref: (order_ref[i], 0))
    shape = jax.ShapeDtypeStruct((count * length, width), first.dtype)
    return pl.pallas_call(
        take_rows,
        grid_spec=pltpu.PrefetchScalarGridSpec(
            num_scalar_prefetch=1, grid=(count,), in_specs=[source, source], out_specs=[target, target]
        ),
        out_shape=[shape, shape],
        name="put_captions",
    )(order, first, second)


def shape(dims, kind=LOW):
    return jax.ShapeDtypeStruct(dims, kind)


def call(body, name, args, outs, scratch, specs=None, out_specs=None, **params):
    return pl.pallas_call(
        body,
        out_shape=outs,
        in_specs=specs if specs is not None else [VMEM] * len(args),
        out_specs=out_specs if out_specs is not None else [VMEM] * len(outs),
        scratch_shapes=scratch,
        input_output_aliases=params.pop("aliases", {}),
        compiler_params=pltpu.CompilerParams(vmem_limit_bytes=VMEM_LIMIT, **params),
        name=name,
    )(*args)


def shards(
    chips, tokens, memory, groups, gains, biases, self_qkv, self_out, cross_query, cross_kv,
    cross_out, mlp_up, mlp_down, cotangent,
):
    captions = groups.shape[0]
    length = tokens.shape[0] // captions
    width = tokens.shape[1]
    images, span = memory.shape[:2]
    local = self_qkv.shape[2]
    hidden = mlp_up.shape[1]
    side = lax.axis_index("tensor")
    some = captions // 2 * length
    rows = images // 2 * span

    picked = groups - lax.axis_index("dp") * images
    same = picked[:, None] == picked[None, :]
    number = lax.broadcasted_iota(jnp.int32, (captions, captions), 0)
    other = lax.broadcasted_iota(jnp.int32, (captions, captions), 1)
    rank = 2 * picked + jnp.sum((same & (other < number)).astype(jnp.int32), axis=1)
    order = jnp.sum(jnp.where(rank[None, :] == number, other, 0), axis=1)
    mine = lax.dynamic_slice_in_dim(order, side * (captions // 2), captions // 2)
    x, cot = take_captions(mine, length, tokens, cotangent)
    some_memory = lax.dynamic_slice_in_dim(memory, side * (images // 2), images // 2).reshape(rows, width)

    weights = [
        self_qkv.reshape(3 * width, local), self_out, cross_kv.reshape(2 * width, local), cross_query,
        cross_out, mlp_up, mlp_down,
    ]
    count = len(weights)
    fetched = call(
        functools.partial(fetch_weights, count), "fetch_weights", weights, [shape(w.shape) for w in weights],
        [pltpu.SemaphoreType.DMA((4, count))] * 2, [ANY] * count, [ANY] * count,
        collective_id=0, has_side_effects=True,
    )
    qkv = (self_qkv, fetched[0].reshape(3, width, local))
    out = (self_out, fetched[1])
    kv = (cross_kv, fetched[2].reshape(2, width, local))
    query = (cross_query, fetched[3])
    mix = (cross_out, fetched[4])
    up = (mlp_up, fetched[5])
    down = (mlp_down, fetched[6])

    h1, s0, s1, o0, o1 = call(
        functools.partial(self_forward, length), "self_forward", (x, gains, biases, *qkv, *out),
        [shape((some, width), F32)] + [shape((3, some, local))] * 2 + [shape((some, local))] * 2, [],
    )
    h2, c, qc0, qc1, kv0, kv1, oc0, oc1 = call(
        functools.partial(cross_forward, span), "cross_forward",
        (h1, some_memory, gains, biases, *query, *kv, *mix),
        [shape((some, width), F32), shape((some, width))] + [shape((some, local))] * 2
        + [shape((2, rows, local))] * 2 + [shape((some, local))] * 2, [],
    )
    part = hidden * 2
    row = shape((1, width), F32)
    chunk = min(hidden, width)
    y_half, dh2, gm0, gm1, gain2, bias2 = call(
        functools.partial(mlp, chunk), "mlp", (h2, cot, gains, biases, *up, *down),
        [shape((some, width)), shape((some, width), F32), shape((part, width)), shape((part, width)), row, row],
        [pltpu.VMEM((some, width), F32), pltpu.VMEM((some, width), F32), pltpu.VMEM((some, width), LOW),
         pltpu.VMEM((2, part, width), LOW), pltpu.SemaphoreType.DMA((4 * hidden // chunk,))],
        out_specs=[VMEM, VMEM, ANY, ANY, VMEM, VMEM],
    )
    attn_rows = 4 * width
    dh1, ga0, ga1, mem_half, gain1, bias1 = call(
        functools.partial(cross_back, span), "cross_back",
        (dh2, h1, some_memory, gains, c, *query, *kv, *mix, qc0, qc1, kv0, kv1, oc0, oc1),
        [shape((some, width), F32), shape((attn_rows, width)), shape((attn_rows, width)), shape((2, rows, local)), row, row],
        [pltpu.VMEM((some, width), LOW), pltpu.VMEM((some, local), LOW), pltpu.VMEM((some, local), LOW),
         pltpu.VMEM((2, rows, local), LOW), pltpu.VMEM((some, width), F32), pltpu.VMEM((rows, width), F32),
         pltpu.VMEM((2, width, width), LOW), pltpu.VMEM((2, width, local), LOW), pltpu.VMEM((2, local, width), LOW),
         pltpu.SemaphoreType.DMA((6,))],
        out_specs=[VMEM, ANY, ANY, VMEM, VMEM, VMEM],
    )
    x_half, ga0, ga1, gain0, bias0 = call(
        functools.partial(self_back, length), "self_back",
        (dh1, x, gains, biases, *qkv, *out, s0, s1, o0, o1, ga0, ga1),
        [shape((some, width)), shape((attn_rows, width)), shape((attn_rows, width)), row, row],
        [pltpu.VMEM((some, width), LOW), pltpu.VMEM((some, width), LOW), pltpu.VMEM((some, local), LOW),
         pltpu.VMEM((3, some, local), LOW), pltpu.VMEM((some, width), F32),
         pltpu.VMEM((2, width, width), LOW), pltpu.VMEM((2, width, local), LOW), pltpu.VMEM((2, local, width), LOW),
         pltpu.SemaphoreType.DMA((6,))],
        specs=[VMEM] * 12 + [ANY] * 2, out_specs=[VMEM, ANY, ANY, VMEM, VMEM], aliases={12: 1, 13: 2},
    )
    small = lax.psum(jnp.concatenate([gain0, gain1, gain2, bias0, bias1, bias2], axis=0), ("dp", "tensor"))

    block = part // (4 * chips)
    cube = pltpu.VMEM((2, 2, chips, block, width), LOW)
    dma = pltpu.SemaphoreType.DMA
    full = dma((2, 2, chips))
    m_sum, a_sum, y_all, x_all, mem_all = call(
        functools.partial(reduce_grads, chips), "reduce_grads", (gm0, gm1, ga0, ga1, y_half, x_half, mem_half),
        [shape((part, width)), shape((attn_rows, width)), shape((2 * some, width)), shape((2 * some, width)),
         shape((2 * rows, local))],
        [cube] * 5 + [pltpu.VMEM((2, 2, chips - 1, block, width), LOW)]
        + [dma((2, 2, 2, chips))] * 3 + [full] * 8 + [dma((2, 2))] + [dma((3,))] * 3,
        [ANY] * 7, [ANY] * 5, collective_id=1, has_side_effects=True,
    )
    output, input_grad = put_captions(order, length, y_all, x_all)
    memory_grad = mem_all.reshape(images, span, local)
    wide_m = m_sum.astype(F32)
    blocks = hidden // chunk
    up_grad = jnp.concatenate([wide_m[i * width : (i + 1) * width] for i in range(blocks)], axis=1)
    down_grad = wide_m[blocks * width :]
    wide_a = a_sum.astype(F32)
    qkv_grad = jnp.stack([wide_a[:width, :local], wide_a[:width, local:], wide_a[width : 2 * width, :local]])
    query_grad = wide_a[width : 2 * width, local:]
    kv_grad = jnp.stack([wide_a[2 * width : 3 * width, :local], wide_a[2 * width : 3 * width, local:]])
    out_grad = wide_a[3 * width : 3 * width + local]
    mix_grad = wide_a[3 * width + local :]
    return (
        output, input_grad, memory_grad, small[:3], small[3:], qkv_grad, out_grad, query_grad, kv_grad,
        mix_grad, up_grad, down_grad,
    )


def solution(mesh):
    rows = P("dp", None)
    columns = P(None, "tensor")
    stacked = P(None, None, "tensor")
    halves = P("tensor", None)
    return jax.shard_map(
        functools.partial(shards, mesh.shape["dp"] // 2),
        mesh=mesh,
        in_specs=(rows, P("dp", None, None), P("dp"), P(), P(), stacked, halves, columns, stacked, halves, columns, halves, rows),
        out_specs=(
            rows, rows, P("dp", None, "tensor"), P(), P(), stacked, halves, columns, stacked, halves, columns, halves,
        ),
        check_vma=False,
    )
```

```python
import functools

import jax
import jax.numpy as jnp
from jax import lax
from jax.experimental import pallas as pl
from jax.experimental.pallas import tpu as pltpu
from jax.sharding import PartitionSpec as P

HEAD_DIM = 64
SCALE = HEAD_DIM**-0.5
PAIR = 2 * HEAD_DIM
EPSILON = 1e-05
ROOT_HALF = 0.7071067811865476
PDF_SCALE = 0.3989422804014327
MESH = pl.DeviceIdType.MESH
LOW = jnp.bfloat16
F32 = jnp.float32
VMEM_LIMIT = 60 * 1024 * 1024
ANY = pl.BlockSpec(memory_space=pl.ANY)
VMEM = pl.BlockSpec(memory_space=pltpu.VMEM)


def nn(left, right):
    return lax.dot_general(left, right, (((1,), (0,)), ((), ())), preferred_element_type=F32)


def nt(left, right):
    return lax.dot_general(left, right, (((1,), (1,)), ((), ())), preferred_element_type=F32)


def tn(left, right):
    return lax.dot_general(left, right, (((0,), (0,)), ((), ())), preferred_element_type=F32)


def standardize(values):
    average = jnp.mean(values, axis=-1, keepdims=True)
    centred = values - average
    inverse = lax.rsqrt(jnp.mean(centred * centred, axis=-1, keepdims=True) + EPSILON)
    return centred * inverse, inverse


def standardize_back(grad_out, scaled, inverse, gain_row):
    weighted = grad_out * gain_row
    return inverse * (
        weighted
        - jnp.mean(weighted, axis=-1, keepdims=True)
        - scaled * jnp.mean(weighted * scaled, axis=-1, keepdims=True)
    )


def column_sum(values):
    return jnp.sum(values, axis=0, keepdims=True)


def softmax_down(scores):
    weights = jnp.exp(scores - jnp.max(scores, axis=0, keepdims=True))
    return weights * (1.0 / jnp.sum(weights, axis=0, keepdims=True))


def first_lanes():
    return lax.broadcasted_iota(jnp.int32, (1, PAIR), 1) < HEAD_DIM


def stack_heads(values):
    zeros = jnp.zeros_like(values)
    first = first_lanes()
    return jnp.concatenate([jnp.where(first, values, zeros), jnp.where(first, zeros, values)], axis=0)


def pick_heads(stacked):
    rows = stacked.shape[0] // 2
    return jnp.where(first_lanes(), stacked[:rows], stacked[rows:])


def caption_bias(rows, length):
    key = lax.broadcasted_iota(jnp.int32, (rows, rows), 0)
    query = lax.broadcasted_iota(jnp.int32, (rows, rows), 1)
    allowed = query >= key
    for edge in range(length, rows, length):
        allowed = allowed & ((query < edge) | (key >= edge))
    bias = jnp.where(allowed, 0.0, -1e30)
    return jnp.concatenate([bias, bias], axis=1)


def attend(queries, keys, values, bias):
    scores = nt(keys, stack_heads(queries * jnp.asarray(SCALE, LOW)))
    if bias is not None:
        scores = scores + bias[...]
    return pick_heads(tn(softmax_down(scores).astype(LOW), values)).astype(LOW)


def attend_back(queries, keys, values, grads, bias):
    stacked = stack_heads(queries * jnp.asarray(SCALE, LOW))
    stacked_grads = stack_heads(grads)
    scores = nt(keys, stacked)
    if bias is not None:
        scores = scores + bias[...]
    probs = softmax_down(scores)
    prob_grad = nt(values, stacked_grads)
    score_low = (probs * (prob_grad - jnp.sum(probs * prob_grad, axis=0, keepdims=True))).astype(LOW)
    query_grad = pick_heads(tn(score_low, keys)) * SCALE
    return query_grad.astype(LOW), nn(score_low, stacked).astype(LOW), nn(probs.astype(LOW), stacked_grads).astype(LOW)


class Stores:
    def __init__(self, sems):
        self.sems = sems
        self.copies = []

    def __call__(self, source, target):
        copy = pltpu.make_async_copy(source, target, self.sems.at[len(self.copies)])
        copy.start()
        self.copies.append(copy)

    def wait(self):
        for copy in self.copies:
            copy.wait()


def self_forward(length, x, gains, biases, qkv0, qkv1, out0, out1, h1, s0, s1, o0, o1, bias):
    scaled, _ = standardize(x[...].astype(F32))
    low = (scaled * gains[0:1] + biases[0:1]).astype(LOW)
    pair_rows = bias.shape[0]
    bias[...] = caption_bias(pair_rows, length)
    for weight, saved in ((qkv0, s0), (qkv1, s1)):
        for j in range(3):
            saved[j] = nn(low, weight[j]).astype(LOW)
    groups = x.shape[0] // pair_rows
    for saved, mixed in ((s0, o0), (s1, o1)):

        @pl.loop(0, groups, unroll=True)
        def _(step):
            rows = pl.ds(pl.multiple_of(step * pair_rows, pair_rows), pair_rows)
            for lane in range(0, saved.shape[2], PAIR):
                lanes = slice(lane, lane + PAIR)
                mixed[rows, lanes] = attend(
                    saved[0, rows, lanes], saved[1, rows, lanes], saved[2, rows, lanes], bias
                )

    h1[...] = x[...].astype(F32) + (nn(o0[...], out0[...]) + nn(o1[...], out1[...]))


def cross_forward(span, h1, memory, gains, biases, q0, q1, kv0, kv1, out0, out1, h2, c, qc0, qc1, m0, m1, o0, o1):
    scaled, _ = standardize(h1[...])
    c[...] = (scaled * gains[1:2] + biases[1:2]).astype(LOW)
    images = memory.shape[0] // span
    pair_rows = h1.shape[0] // images
    for weight, query, kv, saved in ((q0, qc0, kv0, m0), (q1, qc1, kv1, m1)):
        query[...] = nn(c[...], weight[...]).astype(LOW)
        for j in range(2):
            saved[j] = nn(memory[...], kv[j]).astype(LOW)
    for query, saved, mixed in ((qc0, m0, o0), (qc1, m1, o1)):

        @pl.loop(0, images, unroll=True)
        def _(step):
            rows = pl.ds(pl.multiple_of(step * pair_rows, pair_rows), pair_rows)
            keys = pl.ds(pl.multiple_of(step * span, span), span)
            for lane in range(0, saved.shape[2], PAIR):
                lanes = slice(lane, lane + PAIR)
                mixed[rows, lanes] = attend(
                    query[rows, lanes], saved[0, keys, lanes], saved[1, keys, lanes], None
                )

    h2[...] = h1[...] + (nn(o0[...], out0[...]) + nn(o1[...], out1[...]))


def mlp(
    chunk, h2, cot, gains, biases, up0, up1, down0, down1,
    result, dh2, g0, g1, gain_grad, bias_grad, acc, back, low_ref, parts, sems,
):
    width = h2.shape[1]
    scaled, inverse = standardize(h2[...])
    low_ref[...] = (scaled * gains[2:3] + biases[2:3]).astype(LOW)
    acc[...] = h2[...]
    back[...] = jnp.zeros_like(back)
    hidden = up0.shape[1]
    turned = low_ref[...].T
    store = Stores(sems)
    for half, (up, down, grads) in enumerate(((up0, down0, g0), (up1, down1, g1))):
        for start in range(0, hidden, chunk):
            cols = slice(start, start + chunk)
            u = nn(low_ref[...], up[:, cols])
            below = 0.5 + 0.5 * lax.erf(u * ROOT_HALF)
            z = (u * below).astype(LOW)
            acc[...] += nn(z, down[cols, :])
            dz = nt(cot[...], down[cols, :])
            slope = below + u * (PDF_SCALE * jnp.exp(-0.5 * u * u))
            du = (dz * slope).astype(LOW)
            back[...] += nt(du, up[:, cols])
            down_rows = slice(hidden // chunk * width + start, hidden // chunk * width + start + chunk)
            parts[half, down_rows, :] = tn(z, cot[...]).astype(LOW)
            store(parts.at[half, down_rows], grads.at[down_rows])
            up_rows = slice(start // chunk * width, start // chunk * width + width)
            parts[half, up_rows, :] = nn(turned, du).astype(LOW)
            store(parts.at[half, up_rows], grads.at[up_rows])
    result[...] = acc[...].astype(LOW)
    grad = back[...]
    scaled, inverse = standardize(h2[...])
    gain_grad[...] = column_sum(grad * scaled)
    bias_grad[...] = column_sum(grad)
    dh2[...] = cot[...].astype(F32) + standardize_back(grad, scaled, inverse, gains[2:3])
    store.wait()


def cross_back(
    span, dh2, h1, memory, gains, c, q0, q1, kv0, kv1, out0, out1, qc0, qc1, m0, m1, o0, o1,
    dh1, g0, g1, memory_grad, gain_grad, bias_grad, low, dmix, dq, dkv, back, mem_acc, kv_part, query_part, out_part, sems,
):
    store = Stores(sems)
    low[...] = dh2[...].astype(LOW)
    images = memory.shape[0] // span
    pair_rows = h1.shape[0] // images
    local = q0.shape[1]
    width = h1.shape[1]
    for half, (query, kv, out, qc, saved, mixed, grads) in enumerate(
        ((q0, kv0, out0, qc0, m0, o0, g0), (q1, kv1, out1, qc1, m1, o1, g1))
    ):
        out_part[half] = tn(mixed[...], low[...]).astype(LOW)
        store(out_part.at[half], grads.at[3 * width + local : 4 * width])
        dmix[...] = nt(low[...], out[...]).astype(LOW)

        @pl.loop(0, images, unroll=True)
        def _(step):
            rows = pl.ds(pl.multiple_of(step * pair_rows, pair_rows), pair_rows)
            keys = pl.ds(pl.multiple_of(step * span, span), span)
            for lane in range(0, local, PAIR):
                lanes = slice(lane, lane + PAIR)
                a, b, d = attend_back(
                    qc[rows, lanes], saved[0, keys, lanes], saved[1, keys, lanes], dmix[rows, lanes], None
                )
                dq[rows, lanes] = a
                dkv[0, keys, lanes] = b
                dkv[1, keys, lanes] = d

        query_part[half] = tn(c[...], dq[...]).astype(LOW)
        store(query_part.at[half], grads.at[width : 2 * width, local:])
        kv_part[half, :, :local] = tn(memory[...], dkv[0]).astype(LOW)
        kv_part[half, :, local:] = tn(memory[...], dkv[1]).astype(LOW)
        store(kv_part.at[half], grads.at[2 * width : 3 * width])
        more = nt(dq[...], query[...])
        more_memory = nt(dkv[0], kv[0]) + nt(dkv[1], kv[1])
        if half == 0:
            back[...] = more
            mem_acc[...] = more_memory
        else:
            grad = back[...] + more
            total = (mem_acc[...] + more_memory).astype(LOW)
            memory_grad[0] = total[:, :local]
            memory_grad[1] = total[:, local:]
            scaled, inverse = standardize(h1[...])
            gain_grad[...] = column_sum(grad * scaled)
            bias_grad[...] = column_sum(grad)
            dh1[...] = dh2[...] + standardize_back(grad, scaled, inverse, gains[1:2])
    store.wait()


def self_back(
    length, dh1, x, gains, biases, qkv0, qkv1, out0, out1, s0, s1, o0, o1, old0, old1,
    result, g0, g1, gain_grad, bias_grad, low, a_ref, dmix, dqkv, back, pair_part, value_part, out_part, bias, sems,
):
    store = Stores(sems)
    low[...] = dh1[...].astype(LOW)
    scaled, inverse = standardize(x[...].astype(F32))
    a_ref[...] = (scaled * gains[0:1] + biases[0:1]).astype(LOW)
    pair_rows = bias.shape[0]
    bias[...] = caption_bias(pair_rows, length)
    groups = x.shape[0] // pair_rows
    local = o0.shape[1]
    width = x.shape[1]
    turned = a_ref[...].T
    for half, (qkv, out, saved, mixed, grads) in enumerate(
        ((qkv0, out0, s0, o0, g0), (qkv1, out1, s1, o1, g1))
    ):
        out_part[half] = tn(mixed[...], low[...]).astype(LOW)
        store(out_part.at[half], grads.at[3 * width : 3 * width + local])
        dmix[...] = nt(low[...], out[...]).astype(LOW)

        @pl.loop(0, groups, unroll=True)
        def _(step):
            rows = pl.ds(pl.multiple_of(step * pair_rows, pair_rows), pair_rows)
            for lane in range(0, local, PAIR):
                lanes = slice(lane, lane + PAIR)
                a, b, d = attend_back(
                    saved[0, rows, lanes], saved[1, rows, lanes], saved[2, rows, lanes], dmix[rows, lanes], bias
                )
                dqkv[0, rows, lanes] = a
                dqkv[1, rows, lanes] = b
                dqkv[2, rows, lanes] = d

        pair_part[half, :, :local] = nn(turned, dqkv[0]).astype(LOW)
        pair_part[half, :, local:] = nn(turned, dqkv[1]).astype(LOW)
        store(pair_part.at[half], grads.at[0:width])
        value_part[half] = nn(turned, dqkv[2]).astype(LOW)
        store(value_part.at[half], grads.at[width : 2 * width, :local])
        more = nt(dqkv[0], qkv[0]) + nt(dqkv[1], qkv[1]) + nt(dqkv[2], qkv[2])
        if half == 0:
            back[...] = more
        else:
            grad = back[...] + more
            scaled, inverse = standardize(x[...].astype(F32))
            gain_grad[...] = column_sum(grad * scaled)
            bias_grad[...] = column_sum(grad)
            result[...] = (dh1[...] + standardize_back(grad, scaled, inverse, gains[0:1])).astype(LOW)
    store.wait()


def partner(axis):
    dp = lax.axis_index("dp")
    side = lax.axis_index("tensor")
    if axis == "y":
        return dp, 1 - side
    if axis == "core":
        return dp + 1 - 2 * (dp % 2), side
    return dp + 2 - 4 * ((dp // 2) % 2), side


def greet(devices):
    barrier = pltpu.get_barrier_semaphore()
    for device in devices:
        pl.semaphore_signal(barrier, inc=1, device_id=device, device_id_type=MESH)
    pl.semaphore_wait(barrier, len(devices))


def remote(source, target, send, recv, device):
    return pltpu.make_async_remote_copy(
        src_ref=source, dst_ref=target, send_sem=send, recv_sem=recv, device_id=device, device_id_type=MESH
    )


def fetch_weights(count, *refs):
    mine, theirs = refs[:count], refs[count : 2 * count]
    sent, got = refs[2 * count :]
    y, x, core = partner("y"), partner("x"), partner("core")
    dp = lax.axis_index("dp")
    here = dp % 4
    there = here + 2 - 4 * (here // 2)
    greet((y, x, core))

    def piece(ref, number):
        size = ref.shape[0] // 4
        return ref.at[pl.ds(pl.multiple_of(number * size, size), size)]

    def move(k, lane, number, device, source=None):
        spot = piece(theirs[k], number)
        return remote(spot if source is None else source, spot, sent.at[lane, k], got.at[lane, k], device)

    first = [move(k, 0, here, y, piece(mine[k], here)) for k in range(count)]
    for copy in first:
        copy.start()
    later = []
    for k in range(count):
        first[k].wait_recv()
        for lane, device in ((1, x), (2, core)):
            copy = move(k, lane, here, device)
            copy.start()
            later.append(copy)
    last = []
    for k in range(count):
        later[2 * k].wait_recv()
        copy = move(k, 3, there, core)
        copy.start()
        last.append(copy)
    for k in range(count):
        later[2 * k + 1].wait_recv()
        last[k].wait_recv()
    for copy in first + later + last:
        copy.wait_send()


def reduce_grads(chips, *refs):
    (m0, m1, a0, a1, out_half, in_half, mem_half, small, m_sum, a_sum, out_all, in_all, mem_all, small_sum) = refs[:14]
    (own, other, core_own, core_other, from_y, ring, local_sem, core_sent, core_got, y_sent, y_got,
     ring_sent, ring_got, gather_sent, gather_got, back_sent, back_got, final_sem, act_sem, act_sent, act_got,
     small_core, small_pair, small_y, small_all, small_sent, small_got, round_sent, round_got) = refs[14:]
    dp = lax.axis_index("dp")
    side = lax.axis_index("tensor")
    core = dp % 2
    line = dp // 4
    lane = (dp // 2) % 2
    long = chips // 2
    place = line + lane * (chips - 1 - 2 * line)

    def at(position):
        position = (position + chips) % chips
        x = position // long
        z = position + x * (chips - 1 - 2 * position)
        return 4 * z + 2 * x + core, side

    y, mate = partner("y"), partner("core")
    toward = (at(place + 1), at(place - 1))
    greet((y, mate, *toward))
    rows = own.shape[3]
    quarter = chips * rows

    def spot(ref, which, direction, number):
        base = (which * 2 + direction) * quarter + number * rows
        return ref.at[pl.ds(pl.multiple_of(base, rows), rows)]

    def number(direction, step):
        return (place + (2 * chips - step if direction == 0 else step)) % chips

    parts = ((m0, m1, m_sum), (a0, a1, a_sum))
    lanes = [(p, d) for p in range(2) for d in range(2)]

    def acts():
        copies = []
        for i, (half, whole) in enumerate(((out_half, out_all), (in_half, in_all))):
            size = half.shape[0]
            target = whole.at[pl.ds(pl.multiple_of(side * size, size), size)]
            copies.append((half, half, target, i))
        size = mem_half.shape[1]
        target = mem_all.at[pl.ds(pl.multiple_of(side * size, size), size)]
        copies.append((mem_half.at[side], mem_half.at[1 - side], target, 2))
        local = [pltpu.make_async_copy(a, t, act_sem.at[i]) for a, _, t, i in copies]
        away = [remote(b, t, act_sent.at[i], act_got.at[i], y) for _, b, t, i in copies]
        return local, away

    def loads(p, d, s):
        k = number(d, s)
        return (
            pltpu.make_async_copy(spot(parts[p][0], core, d, k), own.at[p, d, s], local_sem.at[0, p, d, s]),
            pltpu.make_async_copy(spot(parts[p][1], core, d, k), other.at[p, d, s], local_sem.at[1, p, d, s]),
        )

    def to_mate(p, d, s):
        k = number(d, s)
        return (
            remote(spot(parts[p][0], 1 - core, d, k), core_own.at[p, d, s], core_sent.at[0, p, d, s],
                   core_got.at[0, p, d, s], mate),
            remote(spot(parts[p][1], 1 - core, d, k), core_other.at[p, d, s], core_sent.at[1, p, d, s],
                   core_got.at[1, p, d, s], mate),
        )

    def to_y(p, d, s):
        return remote(other.at[p, d, s], from_y.at[p, d, s], y_sent.at[p, d, s], y_got.at[p, d, s], y)

    def to_next(p, d, s):
        return remote(own.at[p, d, s], ring.at[p, d, s], ring_sent.at[p, d, s], ring_got.at[p, d, s], toward[d])

    def gather(p, d, s):
        k = number(d, s + chips - 1)
        source = own.at[p, d, chips - 1] if isinstance(s, int) and s == 0 else spot(parts[p][2], core, d, k)
        return remote(source, spot(parts[p][2], core, d, k), gather_sent.at[p, d, s], gather_got.at[p, d, s], toward[d])

    def give_back(p, d, s):
        k = number(d, s + chips - 1)
        source = own.at[p, d, chips - 1] if isinstance(s, int) and s == 0 else spot(parts[p][2], core, d, k)
        return remote(source, spot(parts[p][2], core, d, k), back_sent.at[p, d, s], back_got.at[p, d, s], mate)

    @pl.loop(0, chips)
    def _(s):
        for p, d in lanes:
            for copy in (*loads(p, d, s), *to_mate(p, d, s)):
                copy.start()

    def first(s):
        for p, d in lanes:
            for copy in loads(p, d, s):
                copy.wait()
            for copy in to_mate(p, d, s):
                copy.wait_recv()
            other[p, d, s] = (other[p, d, s].astype(F32) + core_other[p, d, s].astype(F32)).astype(LOW)
            to_y(p, d, s).start()

    def second(s, start):
        for p, d in lanes:
            to_y(p, d, s).wait_recv()
            total = own[p, d, s].astype(F32) + core_own[p, d, s].astype(F32) + from_y[p, d, s].astype(F32)
            if not start:
                to_next(p, d, s - 1).wait_recv()
                total = total + ring[p, d, s - 1].astype(F32)
            own[p, d, s] = total.astype(LOW)

    small_mate = remote(small, small_core, small_sent.at[0], small_got.at[0], mate)
    small_mate.start()
    first(0)
    small_mate.wait_recv()
    small_pair[...] = small[...] + small_core[...]
    small_across = remote(small_pair, small_y, small_sent.at[1], small_got.at[1], y)
    small_across.start()
    first(1)
    small_across.wait_recv()
    small_all[place] = small_pair[...] + small_y[...]

    def pass_small(s):
        slot = small_all.at[number(0, s)]
        return remote(slot, slot, round_sent.at[s], round_got.at[s], toward[0])

    pass_small(0).start()
    second(0, True)
    for p, d in lanes:
        to_next(p, d, 0).start()

    @pl.loop(1, chips - 1)
    def _(s):
        first(s + 1)
        second(s, False)
        for p, d in lanes:
            to_next(p, d, s).start()
        pass_small(s - 1).wait_recv()
        pass_small(s).start()

    local, away = acts()
    for copy in local + away:
        copy.start()
    second(chips - 1, False)
    finals = []
    for p, d in lanes:
        k = number(d, chips - 1)
        copy = pltpu.make_async_copy(own.at[p, d, chips - 1], spot(parts[p][2], core, d, k), final_sem.at[p, d])
        copy.start()
        finals.append(copy)
        gather(p, d, 0).start()
        give_back(p, d, 0).start()

    @pl.loop(1, chips - 1)
    def _(s):
        for p, d in lanes:
            gather(p, d, s - 1).wait_recv()
            gather(p, d, s).start()
            give_back(p, d, s).start()

    for p, d in lanes:
        gather(p, d, chips - 2).wait_recv()
        give_back(p, d, chips - 1).start()

    pass_small(chips - 2).wait_recv()
    total = small_all[0]
    for k in range(1, chips):
        total = total + small_all[k]
    small_sum[...] = total
    for copy in finals + local:
        copy.wait()
    small_mate.wait_send()
    small_across.wait_send()
    for copy in away:
        copy.wait()

    @pl.loop(0, chips)
    def _(s):
        for p, d in lanes:
            for copy in to_mate(p, d, s):
                copy.wait_send()
            to_y(p, d, s).wait_send()
            give_back(p, d, s).wait()

    @pl.loop(0, chips - 1)
    def _(s):
        pass_small(s).wait_send()
        for p, d in lanes:
            to_next(p, d, s).wait_send()
            gather(p, d, s).wait_send()


def take_rows(order_ref, a_ref, b_ref, a_out, b_out):
    a_out[...] = a_ref[...]
    b_out[...] = b_ref[...]


def take_captions(order, length, first, second):
    width = first.shape[1]
    count = order.shape[0]
    source = pl.BlockSpec((length, width), lambda i, order_ref: (order_ref[i], 0))
    target = pl.BlockSpec((length, width), lambda i, order_ref: (i, 0))
    shape = jax.ShapeDtypeStruct((count * length, width), first.dtype)
    return pl.pallas_call(
        take_rows,
        grid_spec=pltpu.PrefetchScalarGridSpec(
            num_scalar_prefetch=1, grid=(count,), in_specs=[source, source], out_specs=[target, target]
        ),
        out_shape=[shape, shape],
        name="take_captions",
    )(order, first, second)


def unpack(
    length, order, m_sum, a_sum, y_all, x_all, out, inp, qkv, self_out, query, kv, mix, up, down,
    low, wide, acts, read_sems, write_sems, row_sems, act_sems,
):
    width = up.shape[0]
    local = self_out.shape[0]
    blocks = low.shape[0]
    reads = []
    for i in range(blocks):
        source = m_sum if i < blocks // 2 else a_sum
        row = i % (blocks // 2) * width
        copy = pltpu.make_async_copy(source.at[row : row + width], low.at[i], read_sems.at[i])
        copy.start()
        reads.append(copy)
    whole = [pltpu.make_async_copy(a, acts.at[k], act_sems.at[k]) for k, a in enumerate((y_all, x_all))]
    for copy in whole:
        copy.start()
    moves = []
    for k, target in enumerate((out, inp)):
        whole[k].wait()
        for i in range(order.shape[0]):
            rows = pl.ds(pl.multiple_of(order[i] * length, length), length)
            copy = pltpu.make_async_copy(acts.at[k, i * length : (i + 1) * length], target.at[rows], row_sems.at[k, i])
            copy.start()
            moves.append(copy)
    left, right = slice(0, local), slice(local, width)
    hidden = down.shape[0]
    targets = [[(slice(None), up.at[:, i * width : (i + 1) * width])] for i in range(hidden // width)]
    targets += [[(slice(None), down.at[i * width : (i + 1) * width])] for i in range(hidden // width)]
    targets += [
        [((slice(None), left), qkv.at[0]), ((slice(None), right), qkv.at[1])],
        [((slice(None), left), qkv.at[2]), ((slice(None), right), query)],
        [((slice(None), left), kv.at[0]), ((slice(None), right), kv.at[1])],
        [((left, slice(None)), self_out), ((right, slice(None)), mix)],
    ]
    store = Stores(write_sems)
    for i, places in enumerate(targets):
        reads[i].wait()
        wide[i] = low[i].astype(F32)
        for part, target in places:
            store(wide.at[i] if part == slice(None) else wide.at[(i, *part)], target)
    store.wait()
    for copy in moves:
        copy.wait()


def shape(dims, kind=LOW):
    return jax.ShapeDtypeStruct(dims, kind)


def call(body, name, args, outs, scratch, specs=None, out_specs=None, **params):
    return pl.pallas_call(
        body,
        out_shape=outs,
        in_specs=specs if specs is not None else [VMEM] * len(args),
        out_specs=out_specs if out_specs is not None else [VMEM] * len(outs),
        scratch_shapes=scratch,
        input_output_aliases=params.pop("aliases", {}),
        compiler_params=pltpu.CompilerParams(vmem_limit_bytes=VMEM_LIMIT, **params),
        name=name,
    )(*args)


def shards(
    chips, tokens, memory, groups, gains, biases, self_qkv, self_out, cross_query, cross_kv,
    cross_out, mlp_up, mlp_down, cotangent,
):
    captions = groups.shape[0]
    length = tokens.shape[0] // captions
    width = tokens.shape[1]
    images, span = memory.shape[:2]
    local = self_qkv.shape[2]
    hidden = mlp_up.shape[1]
    side = lax.axis_index("tensor")
    some = captions // 2 * length
    rows = images // 2 * span

    picked = groups - lax.axis_index("dp") * images
    same = picked[:, None] == picked[None, :]
    number = lax.broadcasted_iota(jnp.int32, (captions, captions), 0)
    other = lax.broadcasted_iota(jnp.int32, (captions, captions), 1)
    rank = 2 * picked + jnp.sum((same & (other < number)).astype(jnp.int32), axis=1)
    order = jnp.sum(jnp.where(rank[None, :] == number, other, 0), axis=1)
    mine = lax.dynamic_slice_in_dim(order, side * (captions // 2), captions // 2)
    x, cot = take_captions(mine, length, tokens, cotangent)
    some_memory = lax.dynamic_slice_in_dim(memory, side * (images // 2), images // 2).reshape(rows, width)

    weights = [
        self_qkv.reshape(3 * width, local), self_out, cross_kv.reshape(2 * width, local), cross_query,
        cross_out, mlp_up, mlp_down,
    ]
    count = len(weights)
    fetched = call(
        functools.partial(fetch_weights, count), "fetch_weights", weights, [shape(w.shape) for w in weights],
        [pltpu.SemaphoreType.DMA((4, count))] * 2, [ANY] * count, [ANY] * count,
        collective_id=0, has_side_effects=True,
    )
    qkv = (self_qkv, fetched[0].reshape(3, width, local))
    out = (self_out, fetched[1])
    kv = (cross_kv, fetched[2].reshape(2, width, local))
    query = (cross_query, fetched[3])
    mix = (cross_out, fetched[4])
    up = (mlp_up, fetched[5])
    down = (mlp_down, fetched[6])

    group = min(some, 4 * length)
    mask = pltpu.VMEM((group, 2 * group), F32)
    h1, s0, s1, o0, o1 = call(
        functools.partial(self_forward, length), "self_forward", (x, gains, biases, *qkv, *out),
        [shape((some, width), F32)] + [shape((3, some, local))] * 2 + [shape((some, local))] * 2, [mask],
    )
    h2, c, qc0, qc1, kv0, kv1, oc0, oc1 = call(
        functools.partial(cross_forward, span), "cross_forward",
        (h1, some_memory, gains, biases, *query, *kv, *mix),
        [shape((some, width), F32), shape((some, width))] + [shape((some, local))] * 2
        + [shape((2, rows, local))] * 2 + [shape((some, local))] * 2, [],
    )
    part = hidden * 2
    row = shape((1, width), F32)
    chunk = min(hidden, width)
    y_half, dh2, gm0, gm1, gain2, bias2 = call(
        functools.partial(mlp, chunk), "mlp", (h2, cot, gains, biases, *up, *down),
        [shape((some, width)), shape((some, width), F32), shape((part, width)), shape((part, width)), row, row],
        [pltpu.VMEM((some, width), F32), pltpu.VMEM((some, width), F32), pltpu.VMEM((some, width), LOW),
         pltpu.VMEM((2, part, width), LOW), pltpu.SemaphoreType.DMA((4 * hidden // chunk,))],
        out_specs=[VMEM, VMEM, ANY, ANY, VMEM, VMEM],
    )
    attn_rows = 4 * width
    dh1, ga0, ga1, mem_half, gain1, bias1 = call(
        functools.partial(cross_back, span), "cross_back",
        (dh2, h1, some_memory, gains, c, *query, *kv, *mix, qc0, qc1, kv0, kv1, oc0, oc1),
        [shape((some, width), F32), shape((attn_rows, width)), shape((attn_rows, width)), shape((2, rows, local)), row, row],
        [pltpu.VMEM((some, width), LOW), pltpu.VMEM((some, local), LOW), pltpu.VMEM((some, local), LOW),
         pltpu.VMEM((2, rows, local), LOW), pltpu.VMEM((some, width), F32), pltpu.VMEM((rows, width), F32),
         pltpu.VMEM((2, width, width), LOW), pltpu.VMEM((2, width, local), LOW), pltpu.VMEM((2, local, width), LOW),
         pltpu.SemaphoreType.DMA((6,))],
        out_specs=[VMEM, ANY, ANY, VMEM, VMEM, VMEM],
    )
    x_half, ga0, ga1, gain0, bias0 = call(
        functools.partial(self_back, length), "self_back",
        (dh1, x, gains, biases, *qkv, *out, s0, s1, o0, o1, ga0, ga1),
        [shape((some, width)), shape((attn_rows, width)), shape((attn_rows, width)), row, row],
        [pltpu.VMEM((some, width), LOW), pltpu.VMEM((some, width), LOW), pltpu.VMEM((some, local), LOW),
         pltpu.VMEM((3, some, local), LOW), pltpu.VMEM((some, width), F32),
         pltpu.VMEM((2, width, width), LOW), pltpu.VMEM((2, width, local), LOW), pltpu.VMEM((2, local, width), LOW),
         mask, pltpu.SemaphoreType.DMA((6,))],
        specs=[VMEM] * 12 + [ANY] * 2, out_specs=[VMEM, ANY, ANY, VMEM, VMEM], aliases={12: 1, 13: 2},
    )
    small = jnp.concatenate([gain0, gain1, gain2, bias0, bias1, bias2, gain0, bias0], axis=0)

    block = part // (4 * chips)
    cube = pltpu.VMEM((2, 2, chips, block, width), LOW)
    dma = pltpu.SemaphoreType.DMA
    full = dma((2, 2, chips))
    m_sum, a_sum, y_all, x_all, mem_all, small_sum = call(
        functools.partial(reduce_grads, chips), "reduce_grads", (gm0, gm1, ga0, ga1, y_half, x_half, mem_half, small),
        [shape((part, width)), shape((attn_rows, width)), shape((2 * some, width)), shape((2 * some, width)),
         shape((2 * rows, local)), shape((8, width), F32)],
        [cube] * 5 + [pltpu.VMEM((2, 2, chips - 1, block, width), LOW)]
        + [dma((2, 2, 2, chips))] * 3 + [full] * 8 + [dma((2, 2))] + [dma((3,))] * 3
        + [pltpu.VMEM((8, width), F32)] * 3 + [pltpu.VMEM((chips, 8, width), F32)] + [dma((2,))] * 2 + [dma((chips - 1,))] * 2,
        [ANY] * 7 + [VMEM], [ANY] * 5 + [VMEM], collective_id=1, has_side_effects=True,
    )
    blocks = 2 * hidden // width + 4
    smem = pl.BlockSpec(memory_space=pltpu.SMEM)
    (output, input_grad, qkv_grad, out_grad, query_grad, kv_grad, mix_grad, up_grad, down_grad) = call(
        functools.partial(unpack, length), "unpack", (order, m_sum, a_sum, y_all, x_all),
        [shape(tokens.shape), shape(tokens.shape), shape(self_qkv.shape, F32), shape(self_out.shape, F32),
         shape(cross_query.shape, F32), shape(cross_kv.shape, F32), shape(cross_out.shape, F32),
         shape(mlp_up.shape, F32), shape(mlp_down.shape, F32)],
        [pltpu.VMEM((blocks, width, width), LOW), pltpu.VMEM((blocks, width, width), F32), pltpu.VMEM((2, *tokens.shape), LOW),
         dma((blocks,)),         dma((2 * blocks,)), dma((2, captions)), dma((2,))],
        [smem] + [ANY] * 4, [ANY] * 9,
    )
    return (
        output, input_grad, mem_all.reshape(images, span, local), small_sum[:3], small_sum[3:6], qkv_grad, out_grad,
        query_grad, kv_grad, mix_grad, up_grad, down_grad,
    )


def solution(mesh):
    rows = P("dp", None)
    columns = P(None, "tensor")
    stacked = P(None, None, "tensor")
    halves = P("tensor", None)
    return jax.shard_map(
        functools.partial(shards, mesh.shape["dp"] // 2),
        mesh=mesh,
        in_specs=(rows, P("dp", None, None), P("dp"), P(), P(), stacked, halves, columns, stacked, halves, columns, halves, rows),
        out_specs=(
            rows, rows, P("dp", None, "tensor"), P(), P(), stacked, halves, columns, stacked, halves, columns, halves,
        ),
        check_vma=False,
    )
```

```python
import functools

import jax
import jax.numpy as jnp
from jax import lax
from jax.experimental import pallas as pl
from jax.experimental.pallas import tpu as pltpu
from jax.sharding import PartitionSpec as P

HEAD_DIM = 64
SCALE = HEAD_DIM**-0.5
PAIR = 2 * HEAD_DIM
EPSILON = 1e-05
ROOT_HALF = 0.7071067811865476
PDF_SCALE = 0.3989422804014327
MESH = pl.DeviceIdType.MESH
LOW = jnp.bfloat16
F32 = jnp.float32
FETCH_PACE = ((4.0, 1.7), (6.5, 2.4), (9.0, 2.4))
VMEM_LIMIT = 60 * 1024 * 1024
ANY = pl.BlockSpec(memory_space=pl.ANY)
VMEM = pl.BlockSpec(memory_space=pltpu.VMEM)


def nn(left, right):
    return lax.dot_general(left, right, (((1,), (0,)), ((), ())), preferred_element_type=F32)


def nt(left, right):
    return lax.dot_general(left, right, (((1,), (1,)), ((), ())), preferred_element_type=F32)


def tn(left, right):
    return lax.dot_general(left, right, (((0,), (0,)), ((), ())), preferred_element_type=F32)


def standardize(values):
    average = jnp.mean(values, axis=-1, keepdims=True)
    centred = values - average
    inverse = lax.rsqrt(jnp.mean(centred * centred, axis=-1, keepdims=True) + EPSILON)
    return centred * inverse, inverse


def standardize_back(grad_out, scaled, inverse, gain_row):
    weighted = grad_out * gain_row
    return inverse * (
        weighted
        - jnp.mean(weighted, axis=-1, keepdims=True)
        - scaled * jnp.mean(weighted * scaled, axis=-1, keepdims=True)
    )


def column_sum(values):
    return jnp.sum(values, axis=0, keepdims=True)


def softmax_down(scores):
    weights = jnp.exp(scores - jnp.max(scores, axis=0, keepdims=True))
    return weights * (1.0 / jnp.sum(weights, axis=0, keepdims=True))


def first_lanes():
    return lax.broadcasted_iota(jnp.int32, (1, PAIR), 1) < HEAD_DIM


def stack_heads(values):
    zeros = jnp.zeros_like(values)
    first = first_lanes()
    return jnp.concatenate([jnp.where(first, values, zeros), jnp.where(first, zeros, values)], axis=0)


def pick_heads(stacked):
    rows = stacked.shape[0] // 2
    return jnp.where(first_lanes(), stacked[:rows], stacked[rows:])


def caption_bias(rows, length):
    key = lax.broadcasted_iota(jnp.int32, (rows, rows), 0)
    query = lax.broadcasted_iota(jnp.int32, (rows, rows), 1)
    allowed = query >= key
    for edge in range(length, rows, length):
        allowed = allowed & ((query < edge) | (key >= edge))
    bias = jnp.where(allowed, 0.0, -1e30)
    return jnp.concatenate([bias, bias], axis=1)


def attend(queries, keys, values, bias):
    scores = nt(keys, stack_heads(queries * jnp.asarray(SCALE, LOW)))
    if bias is not None:
        scores = scores + bias[...]
    return pick_heads(tn(softmax_down(scores).astype(LOW), values)).astype(LOW)


def attend_back(queries, keys, values, grads, bias):
    stacked = stack_heads(queries * jnp.asarray(SCALE, LOW))
    stacked_grads = stack_heads(grads)
    scores = nt(keys, stacked)
    if bias is not None:
        scores = scores + bias[...]
    probs = softmax_down(scores)
    prob_grad = nt(values, stacked_grads)
    score_low = (probs * (prob_grad - jnp.sum(probs * prob_grad, axis=0, keepdims=True))).astype(LOW)
    query_grad = pick_heads(tn(score_low, keys)) * SCALE
    return query_grad.astype(LOW), nn(score_low, stacked).astype(LOW), nn(probs.astype(LOW), stacked_grads).astype(LOW)


class Stores:
    def __init__(self, sems):
        self.sems = sems
        self.copies = []

    def __call__(self, source, target):
        copy = pltpu.make_async_copy(source, target, self.sems.at[len(self.copies)])
        copy.start()
        self.copies.append(copy)

    def wait(self):
        for copy in self.copies:
            copy.wait()


def cross_back(
    span, dh2, h1, memory, gains, c, q0, q1, kv0, kv1, out0, out1, qcs, ms, os,
    dh1, g0, g1, memory_grad, gain_grad, bias_grad, low, dmix, dq, dkv, back, mem_acc, kv_part, query_part, out_part, sems,
):
    store = Stores(sems)
    low[...] = dh2[...].astype(LOW)
    images = memory.shape[0] // span
    pair_rows = h1.shape[0] // images
    local = q0.shape[1]
    width = h1.shape[1]
    for half, (query, kv, out, qc, saved, mixed, grads) in enumerate(
        ((q0, kv0, out0, qcs.at[0], ms.at[0], os.at[0], g0), (q1, kv1, out1, qcs.at[1], ms.at[1], os.at[1], g1))
    ):
        out_part[half] = tn(mixed[...], low[...]).astype(LOW)
        store(out_part.at[half], grads.at[3 * width + local : 4 * width])
        dmix[...] = nt(low[...], out[...]).astype(LOW)

        @pl.loop(0, images, unroll=True)
        def _(step):
            rows = pl.ds(pl.multiple_of(step * pair_rows, pair_rows), pair_rows)
            keys = pl.ds(pl.multiple_of(step * span, span), span)
            for lane in range(0, local, PAIR):
                lanes = slice(lane, lane + PAIR)
                a, b, d = attend_back(
                    qc[rows, lanes], saved[0, keys, lanes], saved[1, keys, lanes], dmix[rows, lanes], None
                )
                dq[rows, lanes] = a
                dkv[0, keys, lanes] = b
                dkv[1, keys, lanes] = d

        query_part[half] = tn(c[...], dq[...]).astype(LOW)
        store(query_part.at[half], grads.at[width : 2 * width, local:])
        kv_part[half, :, :local] = tn(memory[...], dkv[0]).astype(LOW)
        kv_part[half, :, local:] = tn(memory[...], dkv[1]).astype(LOW)
        store(kv_part.at[half], grads.at[2 * width : 3 * width])
        more = nt(dq[...], query[...])
        more_memory = nt(dkv[0], kv[0]) + nt(dkv[1], kv[1])
        if half == 0:
            back[...] = more
            mem_acc[...] = more_memory
        else:
            grad = back[...] + more
            total = (mem_acc[...] + more_memory).astype(LOW)
            memory_grad[0] = total[:, :local]
            memory_grad[1] = total[:, local:]
            scaled, inverse = standardize(h1[...])
            gain_grad[...] = column_sum(grad * scaled)
            bias_grad[...] = column_sum(grad)
            dh1[...] = dh2[...] + standardize_back(grad, scaled, inverse, gains[1:2])
    store.wait()


def self_back(
    length, dh1, x, gains, biases, qkv0, qkv1, out0, out1, ss, os, old0, old1,
    result, g0, g1, gain_grad, bias_grad, low, a_ref, dmix, dqkv, back, pair_part, value_part, out_part, bias, sems,
):
    store = Stores(sems)
    low[...] = dh1[...].astype(LOW)
    scaled, inverse = standardize(x[...].astype(F32))
    a_ref[...] = (scaled * gains[0:1] + biases[0:1]).astype(LOW)
    pair_rows = bias.shape[0]
    bias[...] = caption_bias(pair_rows, length)
    groups = x.shape[0] // pair_rows
    local = os.shape[2]
    width = x.shape[1]
    turned = a_ref[...].T
    for half, (qkv, out, saved, mixed, grads) in enumerate(
        ((qkv0, out0, ss.at[0], os.at[0], g0), (qkv1, out1, ss.at[1], os.at[1], g1))
    ):
        out_part[half] = tn(mixed[...], low[...]).astype(LOW)
        store(out_part.at[half], grads.at[3 * width : 3 * width + local])
        dmix[...] = nt(low[...], out[...]).astype(LOW)

        @pl.loop(0, groups, unroll=True)
        def _(step):
            rows = pl.ds(pl.multiple_of(step * pair_rows, pair_rows), pair_rows)
            for lane in range(0, local, PAIR):
                lanes = slice(lane, lane + PAIR)
                a, b, d = attend_back(
                    saved[0, rows, lanes], saved[1, rows, lanes], saved[2, rows, lanes], dmix[rows, lanes], bias
                )
                dqkv[0, rows, lanes] = a
                dqkv[1, rows, lanes] = b
                dqkv[2, rows, lanes] = d

        pair_part[half, :, :local] = nn(turned, dqkv[0]).astype(LOW)
        pair_part[half, :, local:] = nn(turned, dqkv[1]).astype(LOW)
        store(pair_part.at[half], grads.at[0:width])
        value_part[half] = nn(turned, dqkv[2]).astype(LOW)
        store(value_part.at[half], grads.at[width : 2 * width, :local])
        more = nt(dqkv[0], qkv[0]) + nt(dqkv[1], qkv[1]) + nt(dqkv[2], qkv[2])
        if half == 0:
            back[...] = more
        else:
            grad = back[...] + more
            scaled, inverse = standardize(x[...].astype(F32))
            gain_grad[...] = column_sum(grad * scaled)
            bias_grad[...] = column_sum(grad)
            result[...] = (dh1[...] + standardize_back(grad, scaled, inverse, gains[0:1])).astype(LOW)
    store.wait()


def partner(axis):
    dp = lax.axis_index("dp")
    side = lax.axis_index("tensor")
    if axis == "y":
        return dp, 1 - side
    if axis == "core":
        return dp + 1 - 2 * (dp % 2), side
    if axis == "z":
        return dp + 4 - 8 * ((dp // 4) % 2), side
    return dp + 2 - 4 * ((dp // 2) % 2), side


def greet(devices):
    barrier = pltpu.get_barrier_semaphore()
    for device in devices:
        pl.semaphore_signal(barrier, inc=1, device_id=device, device_id_type=MESH)
    pl.semaphore_wait(barrier, len(devices))


def remote(source, target, send, recv, device):
    return pltpu.make_async_remote_copy(
        src_ref=source, dst_ref=target, send_sem=send, recv_sem=recv, device_id=device, device_id_type=MESH
    )


class Fetch:
    def __init__(self, items, sent, got):
        self.items, self.sent, self.got = items, sent, got
        dp = lax.axis_index("dp")
        self.y, self.x, self.z, self.core = (partner(axis) for axis in ("y", "x", "z", "core"))
        self.here = dp % 8
        x, z = (dp // 2) % 2, (dp // 4) % 2
        self.from_x = self.here + 2 - 4 * x
        self.from_z = self.here + 4 - 8 * z
        self.from_both = self.from_x + 4 - 8 * z
        self.steps = [0, 0, 0]
        self.clock = 0.0
        greet((self.y, self.x, self.z, self.core))
        for k in range(len(items)):
            self.across(k).start()

    def piece(self, ref, number, part=None):
        size = ref.shape[0] // 8
        start = pl.multiple_of(number * size, size)
        if part is None:
            return ref.at[pl.ds(start, size)]
        cut = (size // 2 + 15) // 16 * 16
        if part == 0:
            return ref.at[pl.ds(start, cut)]
        return ref.at[pl.ds(pl.multiple_of(start + cut, 16), size - cut)]

    def move(self, k, lane, device, number, part=None):
        spot = self.piece(self.items[k][1], number, part)
        return remote(spot, spot, self.sent.at[lane, k], self.got.at[lane, k], device)

    def across(self, k):
        mine, theirs = self.items[k]
        return remote(
            self.piece(mine, self.here), self.piece(theirs, self.here), self.sent.at[0, k], self.got.at[0, k], self.y
        )

    def copy(self, k, lane):
        if lane == 0:
            return self.across(k)
        device = (None, self.x, self.z, self.x, self.z, self.core, self.core, self.core, self.core)[lane]
        number = (None, self.here, self.here, self.from_z, self.from_x, self.here, self.from_x, self.from_z, self.from_both)
        return self.move(k, lane, device, number[lane], {3: 0, 4: 1}.get(lane))

    def stage(self, which):
        k = self.steps[which]
        self.steps[which] += 1
        if which == 0:
            self.copy(k, 0).wait_recv()
            for lane in (1, 2, 5):
                self.copy(k, lane).start()
        elif which == 1:
            self.copy(k, 1).wait_recv()
            self.copy(k, 4).start()
            self.copy(k, 6).start()
            self.copy(k, 2).wait_recv()
            self.copy(k, 3).start()
            self.copy(k, 7).start()
        else:
            self.copy(k, 3).wait_recv()
            self.copy(k, 4).wait_recv()
            self.copy(k, 8).start()

    def tick(self, amount):
        self.clock += amount
        for which, (first, pace) in enumerate(FETCH_PACE):
            limit = len(self.items) if which == 0 else self.steps[which - 1]
            while self.steps[which] < limit and self.clock >= first + pace * self.steps[which]:
                self.stage(which)

    def need(self, *numbers):
        first, pace = FETCH_PACE[2]
        self.clock = max(self.clock, first + pace * max(numbers))
        self.tick(0)
        for which in range(3):
            while self.steps[which] <= max(numbers):
                self.stage(which)
        for k in numbers:
            for lane in range(5, 9):
                self.copy(k, lane).wait_recv()

    def finish(self):
        for k in range(len(self.items)):
            for lane in range(9):
                self.copy(k, lane).wait_send()


def forward(length, tokens, cotangent, source, memory, gains, biases, *refs):
    (w_qkv, w_out, w_kv, w_query, w_mix, w_up, w_down) = refs[:7]
    (x_o, h1_o, s_o, o_o, c_o, qc_o, kv_o, oc_o, cot_o, y_o, dh2_o, gm0, gm1,
     t_qkv_o, t_out_o, t_kv_o, t_query_o, t_mix_o, gain_grad, bias_grad) = refs[7:27]
    (raw, x, cot, mem, h1, h2, s, o, c, qc, kv, oc, low, turned, acc, back, y, bias, z_ref, du_ref, parts,
     m_qkv, m_out, m_kv, m_query, m_mix, m_up, m_down,
     t_qkv, t_out, t_kv, t_query, t_mix, t_up, t_down,
     load_sem, store_sem, part_sem, sent, got) = refs[27:]
    side = lax.axis_index("tensor")
    images = mem.shape[0]
    span = mem.shape[1]
    width = x.shape[1]
    local = m_out.shape[0]
    hidden = m_down.shape[0]
    rows_all = x.shape[0]

    loads = [
        pltpu.make_async_copy(a, b, load_sem.at[i])
        for i, (a, b) in enumerate((
            (tokens, raw.at[0]), (w_qkv, m_qkv), (memory.at[pl.ds(side * images, images)], mem), (w_kv, m_kv),
            (w_out, m_out), (w_query, m_query), (w_mix, m_mix), (cotangent, raw.at[1]), (w_up, m_up), (w_down, m_down),
        ))
    ]
    for copy in loads:
        copy.start()
    blocks = [slice(i, i + local) for i in range(0, hidden, local)]
    items = [(w_qkv.at[j], t_qkv.at[j]) for j in range(3)] + [(w_out, t_out)]
    items += [(w_kv.at[j], t_kv.at[j]) for j in range(2)] + [(w_query, t_query), (w_mix, t_mix)]
    per = width // local
    starts = []
    for first in range(0, len(blocks), per):
        starts.append(len(items))
        items += [(w_up.at[:, b], t_up.at[:, b]) for b in blocks[first : first + per]]
        items += [(w_down.at[b], t_down.at[b]) for b in blocks[first : first + per]]
    fetch = Fetch(items, sent, got)
    store = Stores(store_sem)

    def select(raw_ref):
        column = lax.broadcasted_iota(jnp.int32, (rows_all, raw_ref.shape[0]), 1)
        chosen = jnp.where(source[...] == column, 1.0, 0.0).astype(LOW)
        return nn(chosen, raw_ref[...]).astype(LOW)

    loads[0].wait()
    x[...] = select(raw.at[0])
    store(x, x_o)
    scaled, _ = standardize(x[...].astype(F32))
    low[...] = (scaled * gains[0:1] + biases[0:1]).astype(LOW)
    pair_rows = bias.shape[0]
    bias[...] = caption_bias(pair_rows, length)

    def self_half(half, weight):
        for j in range(3):
            s[half, j] = nn(low[...], weight[j]).astype(LOW)
            fetch.tick(0.35)
        for start in range(0, rows_all, pair_rows):
            rows = slice(start, start + pair_rows)
            for lane in range(0, local, PAIR):
                lanes = slice(lane, lane + PAIR)
                o[half, rows, lanes] = attend(
                    s[half, 0, rows, lanes], s[half, 1, rows, lanes], s[half, 2, rows, lanes], bias
                )
            fetch.tick(0.8)

    def keys_half(half, weight):
        flat = mem[...].reshape(images * span, width)
        for j in range(2):
            kv[half, j] = nn(flat, weight[j]).astype(LOW)
            fetch.tick(0.7)

    def cross_half(half, weight):
        qc[half] = nn(c[...], weight[...]).astype(LOW)
        some = rows_all // images
        fetch.tick(0.35)
        for step in range(images):
            rows = slice(step * some, (step + 1) * some)
            keys = slice(step * span, (step + 1) * span)
            for lane in range(0, local, PAIR):
                lanes = slice(lane, lane + PAIR)
                oc[half, rows, lanes] = attend(
                    qc[half, rows, lanes], kv[half, 0, keys, lanes], kv[half, 1, keys, lanes], None
                )
            fetch.tick(0.45)

    loads[1].wait()
    fetch.tick(2.5)
    self_half(0, m_qkv)
    loads[2].wait()
    loads[3].wait()
    keys_half(0, m_kv)
    loads[7].wait()
    cot[...] = select(raw.at[1])
    store(cot, cot_o)
    fetch.tick(1.0)
    loads[4].wait()
    fetch.need(0, 1, 2)
    store(t_qkv, t_qkv_o)
    self_half(1, t_qkv)
    store(s, s_o)
    store(o, o_o)
    fetch.need(3)
    store(t_out, t_out_o)
    h1[...] = x[...].astype(F32) + (nn(o[0], m_out[...]) + nn(o[1], t_out[...]))
    store(h1, h1_o)
    scaled, _ = standardize(h1[...])
    c[...] = (scaled * gains[1:2] + biases[1:2]).astype(LOW)
    store(c, c_o)
    fetch.tick(1.5)
    loads[5].wait()
    cross_half(0, m_query)
    fetch.need(4, 5)
    store(t_kv, t_kv_o)
    keys_half(1, t_kv)
    store(kv, kv_o)
    fetch.need(6)
    store(t_query, t_query_o)
    cross_half(1, t_query)
    store(qc, qc_o)
    store(oc, oc_o)
    loads[6].wait()
    fetch.need(7)
    store(t_mix, t_mix_o)
    h2[...] = h1[...] + (nn(oc[0], m_mix[...]) + nn(oc[1], t_mix[...]))
    scaled, _ = standardize(h2[...])
    low[...] = (scaled * gains[2:3] + biases[2:3]).astype(LOW)
    turned[...] = low[...].T
    fetch.tick(1.5)
    loads[8].wait()
    loads[9].wait()
    block = min(256, rows_all)
    open_parts = {}
    number = 0
    for half, (up, down, grads) in enumerate(((m_up, m_down, gm0), (t_up, t_down, gm1))):
        for index, start in enumerate(range(0, hidden, width)):
            if half == 1:
                fetch.need(*range(starts[index], starts[index] + 2 * per))
            cols = slice(start, start + width)

            for first in range(0, rows_all, block):
                rows = slice(first, first + block)
                u = nn(low[rows, :], up[:, cols])
                below = 0.5 + 0.5 * lax.erf(u * ROOT_HALF)
                z = (u * below).astype(LOW)
                z_ref[rows, :] = z
                dz = nt(cot[rows, :], down[cols, :])
                du = (dz * (below + u * (PDF_SCALE * jnp.exp(-0.5 * u * u)))).astype(LOW)
                du_ref[rows, :] = du
                more = nn(z, down[cols, :])
                more_back = nt(du, up[:, cols])
                if number == 0:
                    acc[rows, :] = h2[rows, :] + more
                    back[rows, :] = more_back
                else:
                    acc[rows, :] += more
                    back[rows, :] += more_back
                fetch.tick(1.4)
            slot = number % 2
            for copy in open_parts.pop(slot, ()):
                copy.wait()
            parts[slot, 0] = tn(z_ref[...], cot[...]).astype(LOW)
            fetch.tick(0.7)
            parts[slot, 1] = nn(turned[...], du_ref[...]).astype(LOW)
            fetch.tick(0.7)
            copies = [
                pltpu.make_async_copy(parts.at[slot, 0], grads.at[hidden + start : hidden + start + width], part_sem.at[slot, 0]),
                pltpu.make_async_copy(parts.at[slot, 1], grads.at[start : start + width], part_sem.at[slot, 1]),
            ]
            for copy in copies:
                copy.start()
            open_parts[slot] = copies
            number += 1
    y[...] = acc[...].astype(LOW)
    store(y, y_o)
    grad = back[...]
    scaled, inverse = standardize(h2[...])
    gain_grad[...] = column_sum(grad * scaled)
    bias_grad[...] = column_sum(grad)
    acc[...] = cot[...].astype(F32) + standardize_back(grad, scaled, inverse, gains[2:3])
    store(acc, dh2_o)
    for copies in open_parts.values():
        for copy in copies:
            copy.wait()
    store.wait()
    fetch.finish()


def reduce_grads(chips, *refs):
    (m0, m1, a0, a1, out_half, in_half, mem_half, small, m_sum, a_sum, out_all, in_all, mem_all, small_sum) = refs[:14]
    (own, other, core_own, core_other, from_y, ring, local_sem, core_sent, core_got, y_sent, y_got,
     ring_sent, ring_got, gather_sent, gather_got, back_sent, back_got, final_sem, act_sem, act_sent, act_got,
     small_core, small_pair, small_y, small_all, small_sent, small_got, round_sent, round_got) = refs[14:]
    dp = lax.axis_index("dp")
    side = lax.axis_index("tensor")
    core = dp % 2
    line = dp // 4
    lane = (dp // 2) % 2
    long = chips // 2
    place = line + lane * (chips - 1 - 2 * line)

    def at(position):
        position = (position + chips) % chips
        x = position // long
        z = position + x * (chips - 1 - 2 * position)
        return 4 * z + 2 * x + core, side

    y, mate = partner("y"), partner("core")
    toward = (at(place + 1), at(place - 1))
    greet((y, mate, *toward))
    rows = own.shape[3]
    quarter = chips * rows

    def spot(ref, which, direction, number):
        base = (which * 2 + direction) * quarter + number * rows
        return ref.at[pl.ds(pl.multiple_of(base, rows), rows)]

    def number(direction, step):
        return (place + (2 * chips - step if direction == 0 else step)) % chips

    parts = ((m0, m1, m_sum), (a0, a1, a_sum))
    lanes = [(p, d) for p in range(2) for d in range(2)]

    def acts():
        copies = []
        for i, (half, whole) in enumerate(((out_half, out_all), (in_half, in_all))):
            size = half.shape[0]
            target = whole.at[pl.ds(pl.multiple_of(side * size, size), size)]
            copies.append((half, half, target, i))
        size = mem_half.shape[1]
        target = mem_all.at[pl.ds(pl.multiple_of(side * size, size), size)]
        copies.append((mem_half.at[side], mem_half.at[1 - side], target, 2))
        local = [pltpu.make_async_copy(a, t, act_sem.at[i]) for a, _, t, i in copies]
        away = [remote(b, t, act_sent.at[i], act_got.at[i], y) for _, b, t, i in copies]
        return local, away

    def loads(p, d, s):
        k = number(d, s)
        return (
            pltpu.make_async_copy(spot(parts[p][0], core, d, k), own.at[p, d, s], local_sem.at[0, p, d, s]),
            pltpu.make_async_copy(spot(parts[p][1], core, d, k), other.at[p, d, s], local_sem.at[1, p, d, s]),
        )

    def to_mate(p, d, s):
        k = number(d, s)
        return (
            remote(spot(parts[p][0], 1 - core, d, k), core_own.at[p, d, s], core_sent.at[0, p, d, s],
                   core_got.at[0, p, d, s], mate),
            remote(spot(parts[p][1], 1 - core, d, k), core_other.at[p, d, s], core_sent.at[1, p, d, s],
                   core_got.at[1, p, d, s], mate),
        )

    def to_y(p, d, s):
        return remote(other.at[p, d, s], from_y.at[p, d, s], y_sent.at[p, d, s], y_got.at[p, d, s], y)

    def to_next(p, d, s):
        return remote(own.at[p, d, s], ring.at[p, d, s], ring_sent.at[p, d, s], ring_got.at[p, d, s], toward[d])

    def gather(p, d, s):
        k = number(d, s + chips - 1)
        source = own.at[p, d, chips - 1] if isinstance(s, int) and s == 0 else spot(parts[p][2], core, d, k)
        return remote(source, spot(parts[p][2], core, d, k), gather_sent.at[p, d, s], gather_got.at[p, d, s], toward[d])

    def give_back(p, d, s):
        k = number(d, s + chips - 1)
        source = own.at[p, d, chips - 1] if isinstance(s, int) and s == 0 else spot(parts[p][2], core, d, k)
        return remote(source, spot(parts[p][2], core, d, k), back_sent.at[p, d, s], back_got.at[p, d, s], mate)

    @pl.loop(0, chips)
    def _(s):
        for p, d in lanes:
            for copy in (*loads(p, d, s), *to_mate(p, d, s)):
                copy.start()

    def first(s):
        for p, d in lanes:
            for copy in loads(p, d, s):
                copy.wait()
            for copy in to_mate(p, d, s):
                copy.wait_recv()
            other[p, d, s] = (other[p, d, s].astype(F32) + core_other[p, d, s].astype(F32)).astype(LOW)
            to_y(p, d, s).start()

    def second(s, start):
        for p, d in lanes:
            to_y(p, d, s).wait_recv()
            total = own[p, d, s].astype(F32) + core_own[p, d, s].astype(F32) + from_y[p, d, s].astype(F32)
            if not start:
                to_next(p, d, s - 1).wait_recv()
                total = total + ring[p, d, s - 1].astype(F32)
            own[p, d, s] = total.astype(LOW)

    small_mate = remote(small, small_core, small_sent.at[0], small_got.at[0], mate)
    small_mate.start()
    first(0)
    small_mate.wait_recv()
    small_pair[...] = small[...] + small_core[...]
    small_across = remote(small_pair, small_y, small_sent.at[1], small_got.at[1], y)
    small_across.start()
    first(1)
    small_across.wait_recv()
    small_all[place] = small_pair[...] + small_y[...]

    def pass_small(s):
        slot = small_all.at[number(0, s)]
        return remote(slot, slot, round_sent.at[s], round_got.at[s], toward[0])

    pass_small(0).start()
    second(0, True)
    for p, d in lanes:
        to_next(p, d, 0).start()

    @pl.loop(1, chips - 1)
    def _(s):
        first(s + 1)
        second(s, False)
        for p, d in lanes:
            to_next(p, d, s).start()
        pass_small(s - 1).wait_recv()
        pass_small(s).start()

    local, away = acts()
    for copy in local + away:
        copy.start()
    second(chips - 1, False)
    finals = []
    for p, d in lanes:
        k = number(d, chips - 1)
        copy = pltpu.make_async_copy(own.at[p, d, chips - 1], spot(parts[p][2], core, d, k), final_sem.at[p, d])
        copy.start()
        finals.append(copy)
        gather(p, d, 0).start()
        give_back(p, d, 0).start()

    @pl.loop(1, chips - 1)
    def _(s):
        for p, d in lanes:
            gather(p, d, s - 1).wait_recv()
            gather(p, d, s).start()
            give_back(p, d, s).start()

    for p, d in lanes:
        gather(p, d, chips - 2).wait_recv()
        give_back(p, d, chips - 1).start()

    pass_small(chips - 2).wait_recv()
    total = small_all[0]
    for k in range(1, chips):
        total = total + small_all[k]
    small_sum[...] = total
    for copy in finals + local:
        copy.wait()
    small_mate.wait_send()
    small_across.wait_send()
    for copy in away:
        copy.wait()

    @pl.loop(0, chips)
    def _(s):
        for p, d in lanes:
            for copy in to_mate(p, d, s):
                copy.wait_send()
            to_y(p, d, s).wait_send()
            give_back(p, d, s).wait()

    @pl.loop(0, chips - 1)
    def _(s):
        pass_small(s).wait_send()
        for p, d in lanes:
            to_next(p, d, s).wait_send()
            gather(p, d, s).wait_send()


def unpack(
    length, order, m_sum, a_sum, y_all, x_all, out, inp, qkv, self_out, query, kv, mix, up, down,
    low, wide, acts, read_sems, write_sems, row_sems, act_sems,
):
    width = up.shape[0]
    local = self_out.shape[0]
    blocks = low.shape[0]
    reads = []
    for i in range(blocks):
        source = m_sum if i < blocks // 2 else a_sum
        row = i % (blocks // 2) * width
        copy = pltpu.make_async_copy(source.at[row : row + width], low.at[i], read_sems.at[i])
        copy.start()
        reads.append(copy)
    whole = [pltpu.make_async_copy(a, acts.at[k], act_sems.at[k]) for k, a in enumerate((y_all, x_all))]
    for copy in whole:
        copy.start()
    moves = []
    for k, target in enumerate((out, inp)):
        whole[k].wait()
        for i in range(order.shape[0]):
            rows = pl.ds(pl.multiple_of(order[i] * length, length), length)
            copy = pltpu.make_async_copy(acts.at[k, i * length : (i + 1) * length], target.at[rows], row_sems.at[k, i])
            copy.start()
            moves.append(copy)
    left, right = slice(0, local), slice(local, width)
    hidden = down.shape[0]
    targets = [[(slice(None), up.at[:, i * width : (i + 1) * width])] for i in range(hidden // width)]
    targets += [[(slice(None), down.at[i * width : (i + 1) * width])] for i in range(hidden // width)]
    targets += [
        [((slice(None), left), qkv.at[0]), ((slice(None), right), qkv.at[1])],
        [((slice(None), left), qkv.at[2]), ((slice(None), right), query)],
        [((slice(None), left), kv.at[0]), ((slice(None), right), kv.at[1])],
        [((left, slice(None)), self_out), ((right, slice(None)), mix)],
    ]
    store = Stores(write_sems)
    for i, places in enumerate(targets):
        reads[i].wait()
        wide[i] = low[i].astype(F32)
        for part, target in places:
            store(wide.at[i] if part == slice(None) else wide.at[(i, *part)], target)
    store.wait()
    for copy in moves:
        copy.wait()


def shape(dims, kind=LOW):
    return jax.ShapeDtypeStruct(dims, kind)


def call(body, name, args, outs, scratch, specs=None, out_specs=None, **params):
    return pl.pallas_call(
        body,
        out_shape=outs,
        in_specs=specs if specs is not None else [VMEM] * len(args),
        out_specs=out_specs if out_specs is not None else [VMEM] * len(outs),
        scratch_shapes=scratch,
        input_output_aliases=params.pop("aliases", {}),
        compiler_params=pltpu.CompilerParams(vmem_limit_bytes=VMEM_LIMIT, **params),
        name=name,
    )(*args)


def shards(
    chips, tokens, memory, groups, gains, biases, self_qkv, self_out, cross_query, cross_kv,
    cross_out, mlp_up, mlp_down, cotangent,
):
    captions = groups.shape[0]
    length = tokens.shape[0] // captions
    width = tokens.shape[1]
    images, span = memory.shape[:2]
    local = self_qkv.shape[2]
    hidden = mlp_up.shape[1]
    side = lax.axis_index("tensor")
    some = captions // 2 * length
    rows = images // 2 * span

    picked = groups - lax.axis_index("dp") * images
    same = picked[:, None] == picked[None, :]
    number = lax.broadcasted_iota(jnp.int32, (captions, captions), 0)
    other = lax.broadcasted_iota(jnp.int32, (captions, captions), 1)
    rank = 2 * picked + jnp.sum((same & (other < number)).astype(jnp.int32), axis=1)
    order = jnp.sum(jnp.where(rank[None, :] == number, other, 0), axis=1)
    mine = lax.dynamic_slice_in_dim(order, side * (captions // 2), captions // 2)
    source = (mine[:, None] * length + lax.broadcasted_iota(jnp.int32, (1, length), 1)).reshape(some, 1)
    some_memory = lax.dynamic_slice_in_dim(memory, side * (images // 2), images // 2).reshape(rows, width)

    part = hidden * 2
    row = shape((1, width), F32)
    group = min(some, 4 * length)
    mask = pltpu.VMEM((group, 2 * group), F32)
    dma = pltpu.SemaphoreType.DMA
    vm = pltpu.VMEM
    count = 8 + 2 * (hidden // local)
    weights = (self_qkv, self_out, cross_kv, cross_query, cross_out, mlp_up, mlp_down)
    held = [vm(w.shape, LOW) for w in weights]
    kept = [
        shape((some, width)), shape((some, width), F32), shape((2, 3, some, local)), shape((2, some, local)),
        shape((some, width)), shape((2, some, local)), shape((2, 2, rows, local)), shape((2, some, local)),
        shape((some, width)), shape((some, width)), shape((some, width), F32), shape((part, width)), shape((part, width)),
    ]
    (x, h1, s, o, c, qc, kvs, oc, cot, y_half, dh2, gm0, gm1, t_qkv, t_out, t_kv, t_query, t_mix, gain2, bias2) = call(
        functools.partial(forward, length), "forward",
        (tokens, cotangent, source, memory, gains, biases, *weights),
        kept + [shape(w.shape) for w in weights[:5]] + [row, row],
        [vm((2, *tokens.shape), LOW), vm((some, width), LOW), vm((some, width), LOW), vm((images // 2, span, width), LOW),
         vm((some, width), F32), vm((some, width), F32), vm((2, 3, some, local), LOW), vm((2, some, local), LOW),
         vm((some, width), LOW), vm((2, some, local), LOW), vm((2, 2, rows, local), LOW), vm((2, some, local), LOW),
         vm((some, width), LOW), vm((width, some), LOW), vm((some, width), F32), vm((some, width), F32),
         vm((some, width), LOW), mask, vm((some, width), LOW), vm((some, width), LOW), vm((2, 2, width, width), LOW)]
        + held + held
        + [dma((10,)), dma((16,)), dma((2, 2)), dma((9, count)), dma((9, count))],
        [ANY, ANY, VMEM, ANY, VMEM, VMEM] + [ANY] * 7, [ANY] * 18 + [VMEM] * 2,
        collective_id=0, has_side_effects=True,
    )
    qkv, out, kv = (self_qkv, t_qkv), (self_out, t_out), (cross_kv, t_kv)
    query, mix = (cross_query, t_query), (cross_out, t_mix)
    attn_rows = 4 * width
    dh1, ga0, ga1, mem_half, gain1, bias1 = call(
        functools.partial(cross_back, span), "cross_back",
        (dh2, h1, some_memory, gains, c, *query, *kv, *mix, qc, kvs, oc),
        [shape((some, width), F32), shape((attn_rows, width)), shape((attn_rows, width)), shape((2, rows, local)), row, row],
        [pltpu.VMEM((some, width), LOW), pltpu.VMEM((some, local), LOW), pltpu.VMEM((some, local), LOW),
         pltpu.VMEM((2, rows, local), LOW), pltpu.VMEM((some, width), F32), pltpu.VMEM((rows, width), F32),
         pltpu.VMEM((2, width, width), LOW), pltpu.VMEM((2, width, local), LOW), pltpu.VMEM((2, local, width), LOW),
         pltpu.SemaphoreType.DMA((6,))],
        out_specs=[VMEM, ANY, ANY, VMEM, VMEM, VMEM],
    )
    x_half, ga0, ga1, gain0, bias0 = call(
        functools.partial(self_back, length), "self_back",
        (dh1, x, gains, biases, *qkv, *out, s, o, ga0, ga1),
        [shape((some, width)), shape((attn_rows, width)), shape((attn_rows, width)), row, row],
        [pltpu.VMEM((some, width), LOW), pltpu.VMEM((some, width), LOW), pltpu.VMEM((some, local), LOW),
         pltpu.VMEM((3, some, local), LOW), pltpu.VMEM((some, width), F32),
         pltpu.VMEM((2, width, width), LOW), pltpu.VMEM((2, width, local), LOW), pltpu.VMEM((2, local, width), LOW),
         mask, pltpu.SemaphoreType.DMA((6,))],
        specs=[VMEM] * 10 + [ANY] * 2, out_specs=[VMEM, ANY, ANY, VMEM, VMEM], aliases={10: 1, 11: 2},
    )
    small = jnp.concatenate([gain0, gain1, gain2, bias0, bias1, bias2, gain0, bias0], axis=0)

    block = part // (4 * chips)
    cube = pltpu.VMEM((2, 2, chips, block, width), LOW)
    full = dma((2, 2, chips))
    m_sum, a_sum, y_all, x_all, mem_all, small_sum = call(
        functools.partial(reduce_grads, chips), "reduce_grads", (gm0, gm1, ga0, ga1, y_half, x_half, mem_half, small),
        [shape((part, width)), shape((attn_rows, width)), shape((2 * some, width)), shape((2 * some, width)),
         shape((2 * rows, local)), shape((8, width), F32)],
        [cube] * 5 + [pltpu.VMEM((2, 2, chips - 1, block, width), LOW)]
        + [dma((2, 2, 2, chips))] * 3 + [full] * 8 + [dma((2, 2))] + [dma((3,))] * 3
        + [pltpu.VMEM((8, width), F32)] * 3 + [pltpu.VMEM((chips, 8, width), F32)] + [dma((2,))] * 2 + [dma((chips - 1,))] * 2,
        [ANY] * 7 + [VMEM], [ANY] * 5 + [VMEM], collective_id=1, has_side_effects=True,
    )
    blocks = 2 * hidden // width + 4
    smem = pl.BlockSpec(memory_space=pltpu.SMEM)
    (output, input_grad, qkv_grad, out_grad, query_grad, kv_grad, mix_grad, up_grad, down_grad) = call(
        functools.partial(unpack, length), "unpack", (order, m_sum, a_sum, y_all, x_all),
        [shape(tokens.shape), shape(tokens.shape), shape(self_qkv.shape, F32), shape(self_out.shape, F32),
         shape(cross_query.shape, F32), shape(cross_kv.shape, F32), shape(cross_out.shape, F32),
         shape(mlp_up.shape, F32), shape(mlp_down.shape, F32)],
        [pltpu.VMEM((blocks, width, width), LOW), pltpu.VMEM((blocks, width, width), F32), pltpu.VMEM((2, *tokens.shape), LOW),
         dma((blocks,)),         dma((2 * blocks,)), dma((2, captions)), dma((2,))],
        [smem] + [ANY] * 4, [ANY] * 9,
    )
    return (
        output, input_grad, mem_all.reshape(images, span, local), small_sum[:3], small_sum[3:6], qkv_grad, out_grad,
        query_grad, kv_grad, mix_grad, up_grad, down_grad,
    )


def solution(mesh):
    rows = P("dp", None)
    columns = P(None, "tensor")
    stacked = P(None, None, "tensor")
    halves = P("tensor", None)
    return jax.shard_map(
        functools.partial(shards, mesh.shape["dp"] // 2),
        mesh=mesh,
        in_specs=(rows, P("dp", None, None), P("dp"), P(), P(), stacked, halves, columns, stacked, halves, columns, halves, rows),
        out_specs=(
            rows, rows, P("dp", None, "tensor"), P(), P(), stacked, halves, columns, stacked, halves, columns, halves,
        ),
        check_vma=False,
    )
```

```python
import functools

import jax
import jax.numpy as jnp
from jax import lax
from jax.experimental import pallas as pl
from jax.experimental.pallas import tpu as pltpu
from jax.sharding import PartitionSpec as P

HEAD_DIM = 64
SCALE = HEAD_DIM**-0.5
PAIR = 2 * HEAD_DIM
EPSILON = 1e-05
ROOT_HALF = 0.7071067811865476
PDF_SCALE = 0.3989422804014327
MESH = pl.DeviceIdType.MESH
LOW = jnp.bfloat16
F32 = jnp.float32
BACK_FIRST = 2.0
BACK_STEP = 0.45
FETCH_PACE = ((4.0, 1.7), (6.5, 2.4), (9.0, 2.4))
VMEM_LIMIT = 60 * 1024 * 1024
ANY = pl.BlockSpec(memory_space=pl.ANY)
VMEM = pl.BlockSpec(memory_space=pltpu.VMEM)


def nn(left, right):
    return lax.dot_general(left, right, (((1,), (0,)), ((), ())), preferred_element_type=F32)


def nt(left, right):
    return lax.dot_general(left, right, (((1,), (1,)), ((), ())), preferred_element_type=F32)


def tn(left, right):
    return lax.dot_general(left, right, (((0,), (0,)), ((), ())), preferred_element_type=F32)


def standardize(values):
    average = jnp.mean(values, axis=-1, keepdims=True)
    centred = values - average
    inverse = lax.rsqrt(jnp.mean(centred * centred, axis=-1, keepdims=True) + EPSILON)
    return centred * inverse, inverse


def standardize_back(grad_out, scaled, inverse, gain_row):
    weighted = grad_out * gain_row
    return inverse * (
        weighted
        - jnp.mean(weighted, axis=-1, keepdims=True)
        - scaled * jnp.mean(weighted * scaled, axis=-1, keepdims=True)
    )


def column_sum(values):
    return jnp.sum(values, axis=0, keepdims=True)


def softmax_down(scores):
    weights = jnp.exp(scores - jnp.max(scores, axis=0, keepdims=True))
    return weights * (1.0 / jnp.sum(weights, axis=0, keepdims=True))


def first_lanes():
    return lax.broadcasted_iota(jnp.int32, (1, PAIR), 1) < HEAD_DIM


def stack_heads(values):
    zeros = jnp.zeros_like(values)
    first = first_lanes()
    return jnp.concatenate([jnp.where(first, values, zeros), jnp.where(first, zeros, values)], axis=0)


def pick_heads(stacked):
    rows = stacked.shape[0] // 2
    return jnp.where(first_lanes(), stacked[:rows], stacked[rows:])


def caption_bias(rows, length):
    key = lax.broadcasted_iota(jnp.int32, (rows, rows), 0)
    query = lax.broadcasted_iota(jnp.int32, (rows, rows), 1)
    allowed = query >= key
    for edge in range(length, rows, length):
        allowed = allowed & ((query < edge) | (key >= edge))
    bias = jnp.where(allowed, 0.0, -1e30)
    return jnp.concatenate([bias, bias], axis=1)


def attend(queries, keys, values, bias):
    scores = nt(keys, stack_heads(queries * jnp.asarray(SCALE, LOW)))
    if bias is not None:
        scores = scores + bias[...]
    return pick_heads(tn(softmax_down(scores).astype(LOW), values)).astype(LOW)


def attend_back(queries, keys, values, grads, bias):
    stacked = stack_heads(queries * jnp.asarray(SCALE, LOW))
    stacked_grads = stack_heads(grads)
    scores = nt(keys, stacked)
    if bias is not None:
        scores = scores + bias[...]
    probs = softmax_down(scores)
    prob_grad = nt(values, stacked_grads)
    score_low = (probs * (prob_grad - jnp.sum(probs * prob_grad, axis=0, keepdims=True))).astype(LOW)
    query_grad = pick_heads(tn(score_low, keys)) * SCALE
    return query_grad.astype(LOW), nn(score_low, stacked).astype(LOW), nn(probs.astype(LOW), stacked_grads).astype(LOW)


class Stores:
    def __init__(self, sems):
        self.sems = sems
        self.copies = []

    def __call__(self, source, target):
        copy = pltpu.make_async_copy(source, target, self.sems.at[len(self.copies)])
        copy.start()
        self.copies.append(copy)

    def wait(self):
        for copy in self.copies:
            copy.wait()


def partner(axis):
    dp = lax.axis_index("dp")
    side = lax.axis_index("tensor")
    if axis == "y":
        return dp, 1 - side
    if axis == "core":
        return dp + 1 - 2 * (dp % 2), side
    if axis == "z":
        return dp + 4 - 8 * ((dp // 4) % 2), side
    return dp + 2 - 4 * ((dp // 2) % 2), side


def greet(devices):
    barrier = pltpu.get_barrier_semaphore()
    for device in devices:
        pl.semaphore_signal(barrier, inc=1, device_id=device, device_id_type=MESH)
    pl.semaphore_wait(barrier, len(devices))


def remote(source, target, send, recv, device):
    return pltpu.make_async_remote_copy(
        src_ref=source, dst_ref=target, send_sem=send, recv_sem=recv, device_id=device, device_id_type=MESH
    )


class Fetch:
    def __init__(self, items, sent, got):
        self.items, self.sent, self.got = items, sent, got
        dp = lax.axis_index("dp")
        self.y, self.x, self.z, self.core = (partner(axis) for axis in ("y", "x", "z", "core"))
        self.here = dp % 8
        x, z = (dp // 2) % 2, (dp // 4) % 2
        self.from_x = self.here + 2 - 4 * x
        self.from_z = self.here + 4 - 8 * z
        self.from_both = self.from_x + 4 - 8 * z
        self.steps = [0, 0, 0]
        self.clock = 0.0
        greet((self.y, self.x, self.z, self.core))
        for k in range(len(items)):
            self.across(k).start()

    def piece(self, ref, number, part=None):
        size = ref.shape[0] // 8
        start = pl.multiple_of(number * size, size)
        if part is None:
            return ref.at[pl.ds(start, size)]
        cut = (size // 2 + 15) // 16 * 16
        if part == 0:
            return ref.at[pl.ds(start, cut)]
        return ref.at[pl.ds(pl.multiple_of(start + cut, 16), size - cut)]

    def move(self, k, lane, device, number, part=None):
        spot = self.piece(self.items[k][1], number, part)
        return remote(spot, spot, self.sent.at[lane, k], self.got.at[lane, k], device)

    def across(self, k):
        mine, theirs = self.items[k]
        return remote(
            self.piece(mine, self.here), self.piece(theirs, self.here), self.sent.at[0, k], self.got.at[0, k], self.y
        )

    def copy(self, k, lane):
        if lane == 0:
            return self.across(k)
        device = (None, self.x, self.z, self.x, self.z, self.core, self.core, self.core, self.core)[lane]
        number = (None, self.here, self.here, self.from_z, self.from_x, self.here, self.from_x, self.from_z, self.from_both)
        return self.move(k, lane, device, number[lane], {3: 0, 4: 1}.get(lane))

    def stage(self, which):
        k = self.steps[which]
        self.steps[which] += 1
        if which == 0:
            self.copy(k, 0).wait_recv()
            for lane in (1, 2, 5):
                self.copy(k, lane).start()
        elif which == 1:
            self.copy(k, 1).wait_recv()
            self.copy(k, 4).start()
            self.copy(k, 6).start()
            self.copy(k, 2).wait_recv()
            self.copy(k, 3).start()
            self.copy(k, 7).start()
        else:
            self.copy(k, 3).wait_recv()
            self.copy(k, 4).wait_recv()
            self.copy(k, 8).start()

    def tick(self, amount):
        self.clock += amount
        for which, (first, pace) in enumerate(FETCH_PACE):
            limit = len(self.items) if which == 0 else self.steps[which - 1]
            while self.steps[which] < limit and self.clock >= first + pace * self.steps[which]:
                self.stage(which)

    def need(self, *numbers):
        first, pace = FETCH_PACE[2]
        self.clock = max(self.clock, first + pace * max(numbers))
        self.tick(0)
        for which in range(3):
            while self.steps[which] <= max(numbers):
                self.stage(which)
        for k in numbers:
            for lane in range(5, 9):
                self.copy(k, lane).wait_recv()

    def finish(self):
        for k in range(len(self.items)):
            for lane in range(9):
                self.copy(k, lane).wait_send()


def forward(length, tokens, cotangent, source, memory, gains, biases, *refs):
    (w_qkv, w_out, w_kv, w_query, w_mix, w_up, w_down) = refs[:7]
    (x_o, h1_o, s_o, o_o, c_o, qc_o, kv_o, oc_o, cot_o, y_o, dh2_o, gm0, gm1,
     t_qkv_o, t_out_o, t_kv_o, t_query_o, t_mix_o, gain_grad, bias_grad) = refs[7:27]
    (raw, x, cot, mem, h1, h2, s, o, c, qc, kv, oc, low, turned, acc, back, y, bias, z_ref, du_ref, parts,
     m_qkv, m_out, m_kv, m_query, m_mix, m_up, m_down,
     t_qkv, t_out, t_kv, t_query, t_mix, t_up, t_down,
     load_sem, store_sem, part_sem, sent, got) = refs[27:]
    side = lax.axis_index("tensor")
    images = mem.shape[0]
    span = mem.shape[1]
    width = x.shape[1]
    local = m_out.shape[0]
    hidden = m_down.shape[0]
    rows_all = x.shape[0]

    loads = [
        pltpu.make_async_copy(a, b, load_sem.at[i])
        for i, (a, b) in enumerate((
            (tokens, raw.at[0]), (w_qkv, m_qkv), (memory.at[pl.ds(side * images, images)], mem), (w_kv, m_kv),
            (w_out, m_out), (w_query, m_query), (w_mix, m_mix), (cotangent, raw.at[1]), (w_up, m_up), (w_down, m_down),
        ))
    ]
    for copy in loads:
        copy.start()
    blocks = [slice(i, i + local) for i in range(0, hidden, local)]
    items = [(w_qkv.at[j], t_qkv.at[j]) for j in range(3)] + [(w_out, t_out)]
    items += [(w_kv.at[j], t_kv.at[j]) for j in range(2)] + [(w_query, t_query), (w_mix, t_mix)]
    per = width // local
    starts = []
    for first in range(0, len(blocks), per):
        starts.append(len(items))
        items += [(w_up.at[:, b], t_up.at[:, b]) for b in blocks[first : first + per]]
        items += [(w_down.at[b], t_down.at[b]) for b in blocks[first : first + per]]
    fetch = Fetch(items, sent, got)
    store = Stores(store_sem)

    def select(raw_ref):
        column = lax.broadcasted_iota(jnp.int32, (rows_all, raw_ref.shape[0]), 1)
        chosen = jnp.where(source[...] == column, 1.0, 0.0).astype(LOW)
        return nn(chosen, raw_ref[...]).astype(LOW)

    loads[0].wait()
    x[...] = select(raw.at[0])
    store(x, x_o)
    scaled, _ = standardize(x[...].astype(F32))
    low[...] = (scaled * gains[0:1] + biases[0:1]).astype(LOW)
    pair_rows = bias.shape[0]
    bias[...] = caption_bias(pair_rows, length)

    def self_half(half, weight):
        for j in range(3):
            s[half, j] = nn(low[...], weight[j]).astype(LOW)
            fetch.tick(0.35)
        for start in range(0, rows_all, pair_rows):
            rows = slice(start, start + pair_rows)
            for lane in range(0, local, PAIR):
                lanes = slice(lane, lane + PAIR)
                o[half, rows, lanes] = attend(
                    s[half, 0, rows, lanes], s[half, 1, rows, lanes], s[half, 2, rows, lanes], bias
                )
            fetch.tick(0.8)

    def keys_half(half, weight):
        flat = mem[...].reshape(images * span, width)
        for j in range(2):
            kv[half, j] = nn(flat, weight[j]).astype(LOW)
            fetch.tick(0.7)

    def cross_half(half, weight):
        qc[half] = nn(c[...], weight[...]).astype(LOW)
        some = rows_all // images
        fetch.tick(0.35)
        for step in range(images):
            rows = slice(step * some, (step + 1) * some)
            keys = slice(step * span, (step + 1) * span)
            for lane in range(0, local, PAIR):
                lanes = slice(lane, lane + PAIR)
                oc[half, rows, lanes] = attend(
                    qc[half, rows, lanes], kv[half, 0, keys, lanes], kv[half, 1, keys, lanes], None
                )
            fetch.tick(0.45)

    loads[1].wait()
    fetch.tick(2.5)
    self_half(0, m_qkv)
    loads[2].wait()
    loads[3].wait()
    keys_half(0, m_kv)
    loads[7].wait()
    cot[...] = select(raw.at[1])
    store(cot, cot_o)
    fetch.tick(1.0)
    loads[4].wait()
    fetch.need(0, 1, 2)
    store(t_qkv, t_qkv_o)
    self_half(1, t_qkv)
    store(s, s_o)
    store(o, o_o)
    fetch.need(3)
    store(t_out, t_out_o)
    h1[...] = x[...].astype(F32) + (nn(o[0], m_out[...]) + nn(o[1], t_out[...]))
    store(h1, h1_o)
    scaled, _ = standardize(h1[...])
    c[...] = (scaled * gains[1:2] + biases[1:2]).astype(LOW)
    store(c, c_o)
    fetch.tick(1.5)
    loads[5].wait()
    cross_half(0, m_query)
    fetch.need(4, 5)
    store(t_kv, t_kv_o)
    keys_half(1, t_kv)
    store(kv, kv_o)
    fetch.need(6)
    store(t_query, t_query_o)
    cross_half(1, t_query)
    store(qc, qc_o)
    store(oc, oc_o)
    loads[6].wait()
    fetch.need(7)
    store(t_mix, t_mix_o)
    h2[...] = h1[...] + (nn(oc[0], m_mix[...]) + nn(oc[1], t_mix[...]))
    scaled, _ = standardize(h2[...])
    low[...] = (scaled * gains[2:3] + biases[2:3]).astype(LOW)
    turned[...] = low[...].T
    fetch.tick(1.5)
    loads[8].wait()
    loads[9].wait()
    block = min(256, rows_all)
    open_parts = {}
    number = 0
    for half, (up, down, grads) in enumerate(((m_up, m_down, gm0), (t_up, t_down, gm1))):
        for index, start in enumerate(range(0, hidden, width)):
            if half == 1:
                fetch.need(*range(starts[index], starts[index] + 2 * per))
            cols = slice(start, start + width)

            for first in range(0, rows_all, block):
                rows = slice(first, first + block)
                u = nn(low[rows, :], up[:, cols])
                below = 0.5 + 0.5 * lax.erf(u * ROOT_HALF)
                z = (u * below).astype(LOW)
                z_ref[rows, :] = z
                dz = nt(cot[rows, :], down[cols, :])
                du = (dz * (below + u * (PDF_SCALE * jnp.exp(-0.5 * u * u)))).astype(LOW)
                du_ref[rows, :] = du
                more = nn(z, down[cols, :])
                more_back = nt(du, up[:, cols])
                if number == 0:
                    acc[rows, :] = h2[rows, :] + more
                    back[rows, :] = more_back
                else:
                    acc[rows, :] += more
                    back[rows, :] += more_back
                fetch.tick(1.4)
            slot = number % 2
            for copy in open_parts.pop(slot, ()):
                copy.wait()
            parts[slot, 0] = tn(z_ref[...], cot[...]).astype(LOW)
            fetch.tick(0.7)
            parts[slot, 1] = nn(turned[...], du_ref[...]).astype(LOW)
            fetch.tick(0.7)
            copies = [
                pltpu.make_async_copy(parts.at[slot, 0], grads.at[hidden + start : hidden + start + width], part_sem.at[slot, 0]),
                pltpu.make_async_copy(parts.at[slot, 1], grads.at[start : start + width], part_sem.at[slot, 1]),
            ]
            for copy in copies:
                copy.start()
            open_parts[slot] = copies
            number += 1
    y[...] = acc[...].astype(LOW)
    store(y, y_o)
    grad = back[...]
    scaled, inverse = standardize(h2[...])
    gain_grad[...] = column_sum(grad * scaled)
    bias_grad[...] = column_sum(grad)
    acc[...] = cot[...].astype(F32) + standardize_back(grad, scaled, inverse, gains[2:3])
    store(acc, dh2_o)
    for copies in open_parts.values():
        for copy in copies:
            copy.wait()
    store.wait()
    fetch.finish()


def ring_pieces(block):
    step = max(block // 3, 16)
    return [(start, min(step, block - start)) for start in range(0, block, step)]


def ring_shapes(chips, block, width):
    over = block // 3
    count = len(ring_pieces(block))
    dma = pltpu.SemaphoreType.DMA
    cube = pltpu.VMEM((2, chips, block, width), LOW)
    return [
        cube, cube, cube, cube,
        pltpu.VMEM((2, chips, block - over, width), LOW),
        pltpu.VMEM((2, chips - 1, block + over, width), LOW),
        pltpu.VMEM((2, over, width), LOW),
        dma((2, 2, chips)), dma((2, 2, chips)), dma((2, 2, chips)), dma((2, chips)), dma((2, chips)),
        dma((count + 1, 2, chips - 1)), dma((count + 1, 2, chips - 1)), dma((2,)), dma((2,)),
        dma((count, 2, chips - 1)), dma((count, 2, chips - 1)), dma((2, chips)), dma((2, chips)), dma((2,)),
    ]


RING = 21


class Ring:
    def __init__(self, chips, mine, theirs, total, refs):
        (self.own, self.other, self.core_own, self.core_other, self.from_y, self.ring, self.last,
         self.local, self.core_sent, self.core_got, self.y_sent, self.y_got, self.ring_sent, self.ring_got,
         self.last_sent, self.last_got, self.gather_sent, self.gather_got, self.back_sent, self.back_got,
         self.final_sem) = refs
        self.chips, self.mine, self.theirs, self.total = chips, mine, theirs, total
        dp = lax.axis_index("dp")
        side = lax.axis_index("tensor")
        self.core = dp % 2
        line, lane = dp // 4, (dp // 2) % 2
        self.place = line + lane * (chips - 1 - 2 * line)
        long = chips // 2

        def at(position):
            position = (position + chips) % chips
            x = position // long
            z = position + x * (chips - 1 - 2 * position)
            return 4 * z + 2 * x + self.core, side

        self.y, self.mate = partner("y"), partner("core")
        self.toward = (at(self.place + 1), at(self.place - 1))
        self.rows = self.own.shape[2]
        self.cut = self.from_y.shape[2]
        self.pieces = ring_pieces(self.rows)

    def greet(self):
        greet((self.y, self.mate, *self.toward))

    def number(self, d, step):
        return (self.place + (2 * self.chips - step if d == 0 else step)) % self.chips

    def spot(self, ref, which, d, number):
        base = (which * 2 + d) * (self.chips * self.rows) + number * self.rows
        return ref.at[pl.ds(pl.multiple_of(base, self.rows), self.rows)]

    def load(self, w, d, s):
        source = (self.mine, self.theirs)[w]
        target = (self.own, self.other)[w]
        return pltpu.make_async_copy(
            self.spot(source, self.core, d, self.number(d, s)), target.at[d, s], self.local.at[w, d, s]
        )

    def to_mate(self, w, d, s):
        source = (self.mine, self.theirs)[w]
        target = (self.core_own, self.core_other)[w]
        return remote(
            self.spot(source, 1 - self.core, d, self.number(d, s)), target.at[d, s],
            self.core_sent.at[w, d, s], self.core_got.at[w, d, s], self.mate,
        )

    def to_y(self, d, s):
        return remote(
            self.other.at[d, s, pl.ds(0, self.cut)], self.from_y.at[d, s], self.y_sent.at[d, s], self.y_got.at[d, s], self.y
        )

    def to_next(self, w, d, s):
        if w < len(self.pieces):
            start, size = self.pieces[w]
            source, target = self.own.at[d, s, pl.ds(start, size)], self.ring.at[d, s, pl.ds(start, size)]
        else:
            over = self.rows - self.cut
            source, target = self.other.at[d, s, pl.ds(self.cut, over)], self.ring.at[d, s, pl.ds(self.rows, over)]
        return remote(source, target, self.ring_sent.at[w, d, s], self.ring_got.at[w, d, s], self.toward[d])

    def to_y_last(self, d):
        source = self.other.at[d, self.chips - 1, pl.ds(self.cut, self.rows - self.cut)]
        return remote(source, self.last.at[d], self.last_sent.at[d], self.last_got.at[d], self.y)

    def done(self, d, s, start=0, size=None):
        size = self.rows if size is None else size
        k = self.number(d, s + self.chips - 1)
        base = (self.core * 2 + d) * (self.chips * self.rows) + k * self.rows + start
        spot = self.total.at[pl.ds(pl.multiple_of(base, 8), size)]
        return (self.own.at[d, self.chips - 1, pl.ds(start, size)] if s == 0 else spot), spot

    def gather(self, w, d, s):
        source, spot = self.done(d, s, *self.pieces[w])
        return remote(source, spot, self.gather_sent.at[w, d, s], self.gather_got.at[w, d, s], self.toward[d])

    def give_back(self, d, s):
        source, spot = self.done(d, s)
        return remote(source, spot, self.back_sent.at[d, s], self.back_got.at[d, s], self.mate)

    def keep(self, d):
        return pltpu.make_async_copy(*self.done(d, 0), self.final_sem.at[d])

    def begin(self):
        for s in range(self.chips):
            for d in range(2):
                for w in (1, 0):
                    self.load(w, d, s).start()
                    self.to_mate(w, d, s).start()

    def first(self, s, d):
        self.load(1, d, s).wait()
        self.to_mate(1, d, s).wait_recv()
        self.other[d, s] = (self.other[d, s].astype(F32) + self.core_other[d, s].astype(F32)).astype(LOW)
        self.to_y(d, s).start()

    def second(self, s, w):
        end = s == self.chips - 1
        if w == len(self.pieces):
            high = slice(self.cut, self.rows)
            for d in range(2):
                if s > 0:
                    self.to_next(w, d, s - 1).wait_recv()
                    more = self.ring[d, s - 1, self.rows :].astype(F32)
                    self.other[d, s, high] = (self.other[d, s, high].astype(F32) + more).astype(LOW)
                if end:
                    self.to_y_last(d).start()
                else:
                    self.to_next(w, d, s).start()
            return
        start, size = self.pieces[w]
        rows = slice(start, start + size)
        for d in range(2):
            if w == 0:
                self.load(0, d, s).wait()
                self.to_mate(0, d, s).wait_recv()
                self.to_y(d, s).wait_recv()
            total = self.own[d, s, rows].astype(F32) + self.core_own[d, s, rows].astype(F32)
            if start < self.cut:
                total = total + self.from_y[d, s, rows].astype(F32)
            if s > 0:
                self.to_next(w, d, s - 1).wait_recv()
                total = total + self.ring[d, s - 1, rows].astype(F32)
            self.own[d, s, rows] = total.astype(LOW)
            if not end:
                self.to_next(w, d, s).start()

    def turn(self, w):
        high = slice(self.cut, self.rows)
        s = self.chips - 1
        for d in range(2):
            if self.pieces[w][0] == self.cut:
                self.to_y_last(d).wait_recv()
                self.own[d, s, high] = (self.own[d, s, high].astype(F32) + self.last[d].astype(F32)).astype(LOW)
            self.gather(w, d, 0).start()
            if w == len(self.pieces) - 1:
                self.give_back(d, 0).start()
                self.keep(d).start()

    def spread(self, s, w):
        for d in range(2):
            self.gather(w, d, s - 1).wait_recv()
            if s < self.chips - 1:
                self.gather(w, d, s).start()
            if w == len(self.pieces) - 1:
                self.give_back(d, s).start()

    def steps(self):
        part = functools.partial
        early = [part(self.first, s, d) for s in range(self.chips) for d in range(2)]
        sums, early = early[:4], early[4:]
        for s in range(self.chips):
            for w in range(len(self.pieces) + 1):
                sums.append(part(self.second, s, w))
                if early and w < 2:
                    sums.append(early.pop(0))
        count = len(self.pieces)
        return sums, [part(self.turn, w) for w in range(count)] + [
            part(self.spread, s, w) for s in range(1, self.chips) for w in range(count)
        ]

    def finish(self):
        for d in range(2):
            self.keep(d).wait()
            self.to_y_last(d).wait_send()
            for s in range(self.chips):
                for w in range(2):
                    self.to_mate(w, d, s).wait_send()
                self.to_y(d, s).wait_send()
                self.give_back(d, s).wait()
                if s < self.chips - 1:
                    for w in range(len(self.pieces) + 1):
                        self.to_next(w, d, s).wait_send()
                    for w in range(len(self.pieces)):
                        self.gather(w, d, s).wait_send()


class Share:
    def __init__(self, here, there, whole, sems):
        side = lax.axis_index("tensor")
        size = here.shape[0]
        target = whole.at[pl.ds(pl.multiple_of(side * size, size), size)]
        self.near = pltpu.make_async_copy(here, target, sems[0].at[0])
        self.far = remote(there, target, sems[1].at[0], sems[2].at[0], partner("y"))
        self.near.start()
        self.far.start()

    def finish(self):
        self.near.wait()
        self.far.wait()


def backward(
    length, chips, gm0, gm1, y_half, dh2_h, h1_h, memory, gains, biases, gain2, bias2, c_h, x_h, s_h, o_h, qc_h, kv_h, oc_h,
    w_qkv, w_out, w_kv, w_query, w_mix, t_qkv, t_out, t_kv, t_query, t_mix, *refs
):
    (ga0, ga1, m_sum, out_all, mem_all, x_o, small) = refs[:7]
    ring = Ring(chips, gm0, gm1, m_sum, refs[7 : 7 + RING])
    (dh, h1, mem, c, x, s, o, qc, kv, oc, wx, wo, low, a_ref, turned, dmix, dqkv, dkv, back, mem_acc, mem_half,
     wide_part, thin_part, out_part, bias, result, load_sem, weight_sem, store_sem, *share_sems) = refs[7 + RING :]
    side = lax.axis_index("tensor")
    images, span, width = mem.shape
    local = wo.shape[1]
    rows_all = x.shape[0]

    ring.greet()
    ring.begin()
    loads = {}
    for i, (name, source, target) in enumerate((
        ("dh", dh2_h, dh), ("oc", oc_h, oc), ("qc", qc_h, qc), ("kv", kv_h, kv), ("c", c_h, c),
        ("mem", memory.at[pl.ds(side * images, images)], mem), ("h1", h1_h, h1), ("x", x_h, x), ("s", s_h, s), ("o", o_h, o),
    )):
        loads[name] = pltpu.make_async_copy(source, target, load_sem.at[i])
        loads[name].start()

    def weights(half, cross):
        keys, q, out = ((w_kv, w_query, w_mix), (t_kv, t_query, t_mix))[half]
        big, end = ((w_qkv, w_out), (t_qkv, t_out))[half]
        pairs = ((keys, wx.at[half, 0:2]), (q, wx.at[half, 2]), (out, wo.at[half])) if cross else (
            (big, wx.at[half]), (end, wo.at[half]))
        copies = [
            pltpu.make_async_copy(source, target, weight_sem.at[0 if cross else 1, half, i])
            for i, (source, target) in enumerate(pairs)
        ]
        for copy in copies:
            copy.start()
        return copies

    held = [weights(0, True), weights(1, True)]
    sums, spread = ring.steps()
    shares = []

    def share_out():
        shares.append(Share(y_half, y_half, out_all, share_sems[:3]))

    todo = sums + [share_out] + spread
    clock = [0.0, 0]

    def tick(amount):
        clock[0] += amount
        while clock[1] < len(todo) and clock[0] >= BACK_FIRST + BACK_STEP * clock[1]:
            todo[clock[1]]()
            clock[1] += 1

    open_parts = {}
    count = [0]

    def put(slot, source, target):
        copy = pltpu.make_async_copy(source, target, store_sem.at[count[0]])
        count[0] += 1
        copy.start()
        open_parts.setdefault(slot, []).append(copy)

    def free(slot):
        for copy in open_parts.pop(slot, ()):
            copy.wait()

    def wait(*names):
        for name in names:
            loads[name].wait()

    wait("dh", "oc")
    low[...] = dh[...].astype(LOW)
    some = rows_all // images
    for half, grads in enumerate((ga0, ga1)):
        for copy in held[half]:
            copy.wait()
        out_part[half] = tn(oc[half], low[...]).astype(LOW)
        put(("out", half), out_part.at[half], grads.at[3 * width + local : 4 * width])
        tick(0.6)
        dmix[...] = nt(low[...], wo[half]).astype(LOW)
        tick(0.5)
        if half == 0:
            wait("qc", "kv")
        for step in range(images):
            rows = slice(step * some, (step + 1) * some)
            keys = slice(step * span, (step + 1) * span)
            for lane in range(0, local, PAIR):
                lanes = slice(lane, lane + PAIR)
                dqkv[0, rows, lanes], dkv[0, keys, lanes], dkv[1, keys, lanes] = attend_back(
                    qc[half, rows, lanes], kv[half, 0, keys, lanes], kv[half, 1, keys, lanes], dmix[rows, lanes], None
                )
                tick(0.45)
        if half == 0:
            wait("c", "mem")
        flat = mem[...].reshape(images * span, width)
        thin_part[half] = tn(c[...], dqkv[0]).astype(LOW)
        put(("thin", half), thin_part.at[half], grads.at[width : 2 * width, local:])
        tick(0.6)
        wide_part[half, :, :local] = tn(flat, dkv[0]).astype(LOW)
        tick(0.9)
        wide_part[half, :, local:] = tn(flat, dkv[1]).astype(LOW)
        put(("wide", half), wide_part.at[half], grads.at[2 * width : 3 * width])
        tick(1.0)
        more = nt(dqkv[0], wx[half, 2])
        if half == 0:
            back[...] = more
        else:
            back[...] += more
        tick(0.4)
        more_memory = nt(dkv[0], wx[half, 0]) + nt(dkv[1], wx[half, 1])
        if half == 0:
            mem_acc[...] = more_memory
        else:
            total = (mem_acc[...] + more_memory).astype(LOW)
            mem_half[0] = total[:, :local]
            mem_half[1] = total[:, local:]
            todo.insert(max(clock[1], len(sums) + 1), lambda: shares.append(Share(mem_half.at[side], mem_half.at[1 - side], mem_all, share_sems[3:6])))
        held[half] = weights(half, False)
        tick(1.4)
    wait("h1")
    grad = back[...]
    scaled, inverse = standardize(h1[...])
    small[1:2] = column_sum(grad * scaled)
    small[4:5] = column_sum(grad)
    dh[...] += standardize_back(grad, scaled, inverse, gains[1:2])
    small[2:3] = gain2[...]
    small[5:6] = bias2[...]
    small[6:8] = jnp.zeros((2, width), F32)
    low[...] = dh[...].astype(LOW)
    wait("x")
    scaled, _ = standardize(x[...].astype(F32))
    a_ref[...] = (scaled * gains[0:1] + biases[0:1]).astype(LOW)
    turned[...] = a_ref[...].T
    bias[...] = caption_bias(bias.shape[0], length)
    tick(2.5)
    group = bias.shape[0]
    wait("s", "o")
    for half, grads in enumerate((ga0, ga1)):
        for copy in held[half]:
            copy.wait()
        free(("out", half))
        out_part[half] = tn(o[half], low[...]).astype(LOW)
        put(("out", half), out_part.at[half], grads.at[3 * width : 3 * width + local])
        tick(0.5)
        dmix[...] = nt(low[...], wo[half]).astype(LOW)
        tick(0.5)
        for first in range(0, rows_all, group):
            rows = slice(first, first + group)
            for lane in range(0, local, PAIR):
                lanes = slice(lane, lane + PAIR)
                dqkv[0, rows, lanes], dqkv[1, rows, lanes], dqkv[2, rows, lanes] = attend_back(
                    s[half, 0, rows, lanes], s[half, 1, rows, lanes], s[half, 2, rows, lanes], dmix[rows, lanes], bias
                )
                tick(0.7)
        free(("wide", half))
        wide_part[half, :, :local] = nn(turned[...], dqkv[0]).astype(LOW)
        tick(0.5)
        wide_part[half, :, local:] = nn(turned[...], dqkv[1]).astype(LOW)
        put(("wide", half), wide_part.at[half], grads.at[0:width])
        tick(0.5)
        free(("thin", half))
        thin_part[half] = nn(turned[...], dqkv[2]).astype(LOW)
        put(("thin", half), thin_part.at[half], grads.at[width : 2 * width, :local])
        tick(0.5)
        more = nt(dqkv[0], wx[half, 0]) + nt(dqkv[1], wx[half, 1]) + nt(dqkv[2], wx[half, 2])
        if half == 0:
            back[...] = more
        else:
            back[...] += more
        tick(1.2)
    grad = back[...]
    scaled, inverse = standardize(x[...].astype(F32))
    small[0:1] = column_sum(grad * scaled)
    small[3:4] = column_sum(grad)
    result[...] = (dh[...] + standardize_back(grad, scaled, inverse, gains[0:1])).astype(LOW)
    put("result", result, x_o)
    while clock[1] < len(todo):
        todo[clock[1]]()
        clock[1] += 1
    for slot in list(open_parts):
        free(slot)
    ring.finish()
    for share in shares:
        share.finish()


def reduce_rest(chips, ga0, ga1, in_half, small, *refs):
    a_sum, in_all, small_sum = refs[:3]
    ring = Ring(chips, ga0, ga1, a_sum, refs[3 : 3 + RING])
    (small_core, small_pair, small_y, small_all, small_sent, small_got, round_sent, round_got, *share_sems) = refs[3 + RING :]
    ring.greet()
    ring.begin()
    small_mate = remote(small, small_core, small_sent.at[0], small_got.at[0], ring.mate)
    small_mate.start()
    small_across = remote(small_pair, small_y, small_sent.at[1], small_got.at[1], ring.y)

    def pass_small(s):
        slot = small_all.at[ring.number(0, s)]
        return remote(slot, slot, round_sent.at[s], round_got.at[s], ring.toward[0])

    shares = []
    sums, spread = ring.steps()
    for i, step in enumerate(sums + spread):
        step()
        small_turn, rest = divmod(i, 4)
        if rest:
            pass
        elif small_turn == 0:
            small_mate.wait_recv()
            small_pair[...] = small[...] + small_core[...]
            small_across.start()
        elif small_turn == 1:
            small_across.wait_recv()
            small_all[ring.place] = small_pair[...] + small_y[...]
            pass_small(0).start()
        elif 2 <= small_turn < chips:
            pass_small(small_turn - 2).wait_recv()
            pass_small(small_turn - 1).start()
        if i == len(sums) - 1:
            shares.append(Share(in_half, in_half, in_all, share_sems))
    pass_small(chips - 2).wait_recv()
    total = small_all[0]
    for k in range(1, chips):
        total = total + small_all[k]
    small_sum[...] = total
    small_mate.wait_send()
    small_across.wait_send()
    for s in range(chips - 1):
        pass_small(s).wait_send()
    ring.finish()
    for share in shares:
        share.finish()


def unpack(
    length, order, m_sum, a_sum, y_all, x_all, out, inp, qkv, self_out, query, kv, mix, up, down,
    low, wide, acts, read_sems, write_sems, row_sems, act_sems,
):
    width = up.shape[0]
    local = self_out.shape[0]
    blocks = low.shape[0]
    reads = []
    for i in range(blocks):
        source = m_sum if i < blocks // 2 else a_sum
        row = i % (blocks // 2) * width
        copy = pltpu.make_async_copy(source.at[row : row + width], low.at[i], read_sems.at[i])
        copy.start()
        reads.append(copy)
    whole = [pltpu.make_async_copy(a, acts.at[k], act_sems.at[k]) for k, a in enumerate((y_all, x_all))]
    for copy in whole:
        copy.start()
    moves = []
    for k, target in enumerate((out, inp)):
        whole[k].wait()
        for i in range(order.shape[0]):
            rows = pl.ds(pl.multiple_of(order[i] * length, length), length)
            copy = pltpu.make_async_copy(acts.at[k, i * length : (i + 1) * length], target.at[rows], row_sems.at[k, i])
            copy.start()
            moves.append(copy)
    left, right = slice(0, local), slice(local, width)
    hidden = down.shape[0]
    targets = [[(slice(None), up.at[:, i * width : (i + 1) * width])] for i in range(hidden // width)]
    targets += [[(slice(None), down.at[i * width : (i + 1) * width])] for i in range(hidden // width)]
    targets += [
        [((slice(None), left), qkv.at[0]), ((slice(None), right), qkv.at[1])],
        [((slice(None), left), qkv.at[2]), ((slice(None), right), query)],
        [((slice(None), left), kv.at[0]), ((slice(None), right), kv.at[1])],
        [((left, slice(None)), self_out), ((right, slice(None)), mix)],
    ]
    store = Stores(write_sems)
    for i, places in enumerate(targets):
        reads[i].wait()
        wide[i] = low[i].astype(F32)
        for part, target in places:
            store(wide.at[i] if part == slice(None) else wide.at[(i, *part)], target)
    store.wait()
    for copy in moves:
        copy.wait()


def shape(dims, kind=LOW):
    return jax.ShapeDtypeStruct(dims, kind)


def call(body, name, args, outs, scratch, specs=None, out_specs=None, **params):
    return pl.pallas_call(
        body,
        out_shape=outs,
        in_specs=specs if specs is not None else [VMEM] * len(args),
        out_specs=out_specs if out_specs is not None else [VMEM] * len(outs),
        scratch_shapes=scratch,
        input_output_aliases=params.pop("aliases", {}),
        compiler_params=pltpu.CompilerParams(vmem_limit_bytes=VMEM_LIMIT, **params),
        name=name,
    )(*args)


def shards(
    chips, tokens, memory, groups, gains, biases, self_qkv, self_out, cross_query, cross_kv,
    cross_out, mlp_up, mlp_down, cotangent,
):
    captions = groups.shape[0]
    length = tokens.shape[0] // captions
    width = tokens.shape[1]
    images, span = memory.shape[:2]
    local = self_qkv.shape[2]
    hidden = mlp_up.shape[1]
    side = lax.axis_index("tensor")
    some = captions // 2 * length
    rows = images // 2 * span

    picked = groups - lax.axis_index("dp") * images
    same = picked[:, None] == picked[None, :]
    number = lax.broadcasted_iota(jnp.int32, (captions, captions), 0)
    other = lax.broadcasted_iota(jnp.int32, (captions, captions), 1)
    rank = 2 * picked + jnp.sum((same & (other < number)).astype(jnp.int32), axis=1)
    order = jnp.sum(jnp.where(rank[None, :] == number, other, 0), axis=1)
    mine = lax.dynamic_slice_in_dim(order, side * (captions // 2), captions // 2)
    source = (mine[:, None] * length + lax.broadcasted_iota(jnp.int32, (1, length), 1)).reshape(some, 1)

    part = hidden * 2
    row = shape((1, width), F32)
    group = min(some, 4 * length)
    mask = pltpu.VMEM((group, 2 * group), F32)
    dma = pltpu.SemaphoreType.DMA
    vm = pltpu.VMEM
    count = 8 + 2 * (hidden // local)
    weights = (self_qkv, self_out, cross_kv, cross_query, cross_out, mlp_up, mlp_down)
    held = [vm(w.shape, LOW) for w in weights]
    kept = [
        shape((some, width)), shape((some, width), F32), shape((2, 3, some, local)), shape((2, some, local)),
        shape((some, width)), shape((2, some, local)), shape((2, 2, rows, local)), shape((2, some, local)),
        shape((some, width)), shape((some, width)), shape((some, width), F32), shape((part, width)), shape((part, width)),
    ]
    (x, h1, s, o, c, qc, kvs, oc, cot, y_half, dh2, gm0, gm1, t_qkv, t_out, t_kv, t_query, t_mix, gain2, bias2) = call(
        functools.partial(forward, length), "forward",
        (tokens, cotangent, source, memory, gains, biases, *weights),
        kept + [shape(w.shape) for w in weights[:5]] + [row, row],
        [vm((2, *tokens.shape), LOW), vm((some, width), LOW), vm((some, width), LOW), vm((images // 2, span, width), LOW),
         vm((some, width), F32), vm((some, width), F32), vm((2, 3, some, local), LOW), vm((2, some, local), LOW),
         vm((some, width), LOW), vm((2, some, local), LOW), vm((2, 2, rows, local), LOW), vm((2, some, local), LOW),
         vm((some, width), LOW), vm((width, some), LOW), vm((some, width), F32), vm((some, width), F32),
         vm((some, width), LOW), mask, vm((some, width), LOW), vm((some, width), LOW), vm((2, 2, width, width), LOW)]
        + held + held
        + [dma((10,)), dma((16,)), dma((2, 2)), dma((9, count)), dma((9, count))],
        [ANY, ANY, VMEM, ANY, VMEM, VMEM] + [ANY] * 7, [ANY] * 18 + [VMEM] * 2,
        collective_id=0, has_side_effects=True,
    )
    attn_rows = 4 * width
    block = part // (4 * chips)
    ring = ring_shapes(chips, block, width)
    one = [dma((1,))] * 3
    ga0, ga1, m_sum, y_all, mem_all, x_half, small = call(
        functools.partial(backward, length, chips), "backward",
        (gm0, gm1, y_half, dh2, h1, memory, gains, biases, gain2, bias2, c, x, s, o, qc, kvs, oc, *weights[:5],
         t_qkv, t_out, t_kv, t_query, t_mix),
        [shape((attn_rows, width)), shape((attn_rows, width)), shape((part, width)), shape((2 * some, width)),
         shape((2 * rows, local)), shape((some, width)), shape((8, width), F32)],
        ring
        + [vm((some, width), F32), vm((some, width), F32), vm((images // 2, span, width), LOW), vm((some, width), LOW),
           vm((some, width), LOW), vm((2, 3, some, local), LOW), vm((2, some, local), LOW), vm((2, some, local), LOW),
           vm((2, 2, rows, local), LOW), vm((2, some, local), LOW), vm((2, 3, width, local), LOW), vm((2, local, width), LOW),
           vm((some, width), LOW), vm((some, width), LOW), vm((width, some), LOW), vm((some, local), LOW),
           vm((3, some, local), LOW), vm((2, rows, local), LOW), vm((some, width), F32), vm((rows, width), F32),
           vm((2, rows, local), LOW), vm((2, width, width), LOW), vm((2, width, local), LOW), vm((2, local, width), LOW),
           mask, vm((some, width), LOW), dma((10,)), dma((2, 2, 3)), dma((16,))]
        + one + one,
        [ANY] * 6 + [VMEM] * 4 + [ANY] * 17, [ANY] * 6 + [VMEM],
        collective_id=1, has_side_effects=True,
    )
    a_sum, x_all, small_sum = call(
        functools.partial(reduce_rest, chips), "reduce_rest", (ga0, ga1, x_half, small),
        [shape((attn_rows, width)), shape((2 * some, width)), shape((8, width), F32)],
        ring + [vm((8, width), F32)] * 3 + [vm((chips, 8, width), F32)] + [dma((2,))] * 2 + [dma((chips - 1,))] * 2 + one,
        [ANY] * 3 + [VMEM], [ANY, ANY, VMEM], collective_id=2, has_side_effects=True,
    )
    blocks = 2 * hidden // width + 4
    smem = pl.BlockSpec(memory_space=pltpu.SMEM)
    (output, input_grad, qkv_grad, out_grad, query_grad, kv_grad, mix_grad, up_grad, down_grad) = call(
        functools.partial(unpack, length), "unpack", (order, m_sum, a_sum, y_all, x_all),
        [shape(tokens.shape), shape(tokens.shape), shape(self_qkv.shape, F32), shape(self_out.shape, F32),
         shape(cross_query.shape, F32), shape(cross_kv.shape, F32), shape(cross_out.shape, F32),
         shape(mlp_up.shape, F32), shape(mlp_down.shape, F32)],
        [pltpu.VMEM((blocks, width, width), LOW), pltpu.VMEM((blocks, width, width), F32), pltpu.VMEM((2, *tokens.shape), LOW),
         dma((blocks,)),         dma((2 * blocks,)), dma((2, captions)), dma((2,))],
        [smem] + [ANY] * 4, [ANY] * 9,
    )
    return (
        output, input_grad, mem_all.reshape(images, span, local), small_sum[:3], small_sum[3:6], qkv_grad, out_grad,
        query_grad, kv_grad, mix_grad, up_grad, down_grad,
    )


def solution(mesh):
    rows = P("dp", None)
    columns = P(None, "tensor")
    stacked = P(None, None, "tensor")
    halves = P("tensor", None)
    return jax.shard_map(
        functools.partial(shards, mesh.shape["dp"] // 2),
        mesh=mesh,
        in_specs=(rows, P("dp", None, None), P("dp"), P(), P(), stacked, halves, columns, stacked, halves, columns, halves, rows),
        out_specs=(
            rows, rows, P("dp", None, "tensor"), P(), P(), stacked, halves, columns, stacked, halves, columns, halves,
        ),
        check_vma=False,
    )
```

```python
import functools

import jax
import jax.numpy as jnp
from jax import lax
from jax.experimental import pallas as pl
from jax.experimental.pallas import tpu as pltpu
from jax.sharding import PartitionSpec as P

HEAD_DIM = 64
SCALE = HEAD_DIM**-0.5
PAIR = 2 * HEAD_DIM
EPSILON = 1e-05
ROOT_HALF = 0.7071067811865476
PDF_SCALE = 0.3989422804014327
MESH = pl.DeviceIdType.MESH
LOW = jnp.bfloat16
F32 = jnp.float32
BACK_FIRST = 2.0
BACK_STEP = 0.45
FETCH_PACE = ((4.0, 1.7), (6.5, 2.4), (9.0, 2.4))
VMEM_LIMIT = 60 * 1024 * 1024
ANY = pl.BlockSpec(memory_space=pl.ANY)
VMEM = pl.BlockSpec(memory_space=pltpu.VMEM)


def nn(left, right):
    return lax.dot_general(left, right, (((1,), (0,)), ((), ())), preferred_element_type=F32)


def nt(left, right):
    return lax.dot_general(left, right, (((1,), (1,)), ((), ())), preferred_element_type=F32)


def tn(left, right):
    return lax.dot_general(left, right, (((0,), (0,)), ((), ())), preferred_element_type=F32)


def standardize(values):
    average = jnp.mean(values, axis=-1, keepdims=True)
    centred = values - average
    inverse = lax.rsqrt(jnp.mean(centred * centred, axis=-1, keepdims=True) + EPSILON)
    return centred * inverse, inverse


def standardize_back(grad_out, scaled, inverse, gain_row):
    weighted = grad_out * gain_row
    return inverse * (
        weighted
        - jnp.mean(weighted, axis=-1, keepdims=True)
        - scaled * jnp.mean(weighted * scaled, axis=-1, keepdims=True)
    )


def column_sum(values):
    return jnp.sum(values, axis=0, keepdims=True)


def softmax_down(scores):
    weights = jnp.exp(scores - jnp.max(scores, axis=0, keepdims=True))
    return weights * (1.0 / jnp.sum(weights, axis=0, keepdims=True))


def first_lanes():
    return lax.broadcasted_iota(jnp.int32, (1, PAIR), 1) < HEAD_DIM


def stack_heads(values):
    zeros = jnp.zeros_like(values)
    first = first_lanes()
    return jnp.concatenate([jnp.where(first, values, zeros), jnp.where(first, zeros, values)], axis=0)


def pick_heads(stacked):
    rows = stacked.shape[0] // 2
    return jnp.where(first_lanes(), stacked[:rows], stacked[rows:])


def caption_bias(rows, length):
    key = lax.broadcasted_iota(jnp.int32, (rows, rows), 0)
    query = lax.broadcasted_iota(jnp.int32, (rows, rows), 1)
    allowed = query >= key
    for edge in range(length, rows, length):
        allowed = allowed & ((query < edge) | (key >= edge))
    bias = jnp.where(allowed, 0.0, -1e30)
    return jnp.concatenate([bias, bias], axis=1)


def attend(queries, keys, values, bias):
    scores = nt(keys, stack_heads(queries * jnp.asarray(SCALE, LOW)))
    if bias is not None:
        scores = scores + bias[...]
    return pick_heads(tn(softmax_down(scores).astype(LOW), values)).astype(LOW)


def attend_back(queries, keys, values, grads, bias):
    stacked = stack_heads(queries * jnp.asarray(SCALE, LOW))
    stacked_grads = stack_heads(grads)
    scores = nt(keys, stacked)
    if bias is not None:
        scores = scores + bias[...]
    probs = softmax_down(scores)
    prob_grad = nt(values, stacked_grads)
    score_low = (probs * (prob_grad - jnp.sum(probs * prob_grad, axis=0, keepdims=True))).astype(LOW)
    query_grad = pick_heads(tn(score_low, keys)) * SCALE
    return query_grad.astype(LOW), nn(score_low, stacked).astype(LOW), nn(probs.astype(LOW), stacked_grads).astype(LOW)


class Stores:
    def __init__(self, sems):
        self.sems = sems
        self.copies = []

    def __call__(self, source, target):
        copy = pltpu.make_async_copy(source, target, self.sems.at[len(self.copies)])
        copy.start()
        self.copies.append(copy)

    def wait(self):
        for copy in self.copies:
            copy.wait()


def partner(axis):
    dp = lax.axis_index("dp")
    side = lax.axis_index("tensor")
    if axis == "y":
        return dp, 1 - side
    if axis == "core":
        return dp + 1 - 2 * (dp % 2), side
    if axis == "z":
        return dp + 4 - 8 * ((dp // 4) % 2), side
    return dp + 2 - 4 * ((dp // 2) % 2), side


def greet(devices):
    barrier = pltpu.get_barrier_semaphore()
    for device in devices:
        pl.semaphore_signal(barrier, inc=1, device_id=device, device_id_type=MESH)
    pl.semaphore_wait(barrier, len(devices))


def remote(source, target, send, recv, device):
    return pltpu.make_async_remote_copy(
        src_ref=source, dst_ref=target, send_sem=send, recv_sem=recv, device_id=device, device_id_type=MESH
    )


class Fetch:
    def __init__(self, items, sent, got):
        self.items, self.sent, self.got = items, sent, got
        dp = lax.axis_index("dp")
        self.y, self.x, self.z, self.core = (partner(axis) for axis in ("y", "x", "z", "core"))
        self.here = dp % 8
        x, z = (dp // 2) % 2, (dp // 4) % 2
        self.from_x = self.here + 2 - 4 * x
        self.from_z = self.here + 4 - 8 * z
        self.from_both = self.from_x + 4 - 8 * z
        self.steps = [0, 0, 0]
        self.clock = 0.0
        greet((self.y, self.x, self.z, self.core))
        for k in range(len(items)):
            self.across(k).start()

    def piece(self, ref, number, part=None):
        size = ref.shape[0] // 8
        start = pl.multiple_of(number * size, size)
        if part is None:
            return ref.at[pl.ds(start, size)]
        cut = (size // 2 + 15) // 16 * 16
        if part == 0:
            return ref.at[pl.ds(start, cut)]
        return ref.at[pl.ds(pl.multiple_of(start + cut, 16), size - cut)]

    def move(self, k, lane, device, number, part=None):
        spot = self.piece(self.items[k][1], number, part)
        return remote(spot, spot, self.sent.at[lane, k], self.got.at[lane, k], device)

    def across(self, k):
        mine, theirs = self.items[k]
        return remote(
            self.piece(mine, self.here), self.piece(theirs, self.here), self.sent.at[0, k], self.got.at[0, k], self.y
        )

    def copy(self, k, lane):
        if lane == 0:
            return self.across(k)
        device = (None, self.x, self.z, self.x, self.z, self.core, self.core, self.core, self.core)[lane]
        number = (None, self.here, self.here, self.from_z, self.from_x, self.here, self.from_x, self.from_z, self.from_both)
        return self.move(k, lane, device, number[lane], {3: 0, 4: 1}.get(lane))

    def stage(self, which):
        k = self.steps[which]
        self.steps[which] += 1
        if which == 0:
            self.copy(k, 0).wait_recv()
            for lane in (1, 2, 5):
                self.copy(k, lane).start()
        elif which == 1:
            self.copy(k, 1).wait_recv()
            self.copy(k, 4).start()
            self.copy(k, 6).start()
            self.copy(k, 2).wait_recv()
            self.copy(k, 3).start()
            self.copy(k, 7).start()
        else:
            self.copy(k, 3).wait_recv()
            self.copy(k, 4).wait_recv()
            self.copy(k, 8).start()

    def tick(self, amount):
        self.clock += amount
        for which, (first, pace) in enumerate(FETCH_PACE):
            limit = len(self.items) if which == 0 else self.steps[which - 1]
            while self.steps[which] < limit and self.clock >= first + pace * self.steps[which]:
                self.stage(which)

    def need(self, *numbers):
        first, pace = FETCH_PACE[2]
        self.clock = max(self.clock, first + pace * max(numbers))
        self.tick(0)
        for which in range(3):
            while self.steps[which] <= max(numbers):
                self.stage(which)
        for k in numbers:
            for lane in range(5, 9):
                self.copy(k, lane).wait_recv()

    def finish(self):
        for k in range(len(self.items)):
            for lane in range(9):
                self.copy(k, lane).wait_send()


def forward(length, tokens, cotangent, source, memory, gains, biases, *refs):
    (w_qkv, w_out, w_kv, w_query, w_mix, w_up, w_down) = refs[:7]
    (x_o, h1_o, s_o, o_o, c_o, qc_o, kv_o, oc_o, cot_o, y_o, dh2_o, gm0, gm1,
     t_qkv_o, t_out_o, t_kv_o, t_query_o, t_mix_o, gain_grad, bias_grad) = refs[7:27]
    (raw, x, cot, mem, h1, h2, s, o, c, qc, kv, oc, low, turned, acc, back, y, bias, z_ref, du_ref, parts,
     m_qkv, m_out, m_kv, m_query, m_mix, m_up, m_down,
     t_qkv, t_out, t_kv, t_query, t_mix, t_up, t_down,
     load_sem, store_sem, part_sem, sent, got) = refs[27:]
    side = lax.axis_index("tensor")
    images = mem.shape[0]
    span = mem.shape[1]
    width = x.shape[1]
    local = m_out.shape[0]
    hidden = m_down.shape[0]
    rows_all = x.shape[0]

    loads = [
        pltpu.make_async_copy(a, b, load_sem.at[i])
        for i, (a, b) in enumerate((
            (tokens, raw.at[0]), (w_qkv, m_qkv), (memory.at[pl.ds(side * images, images)], mem), (w_kv, m_kv),
            (w_out, m_out), (w_query, m_query), (w_mix, m_mix), (cotangent, raw.at[1]), (w_up, m_up), (w_down, m_down),
        ))
    ]
    for copy in loads:
        copy.start()
    blocks = [slice(i, i + local) for i in range(0, hidden, local)]
    items = [(w_qkv.at[j], t_qkv.at[j]) for j in range(3)] + [(w_out, t_out)]
    items += [(w_kv.at[j], t_kv.at[j]) for j in range(2)] + [(w_query, t_query), (w_mix, t_mix)]
    per = width // local
    starts = []
    for first in range(0, len(blocks), per):
        starts.append(len(items))
        items += [(w_up.at[:, b], t_up.at[:, b]) for b in blocks[first : first + per]]
        items += [(w_down.at[b], t_down.at[b]) for b in blocks[first : first + per]]
    fetch = Fetch(items, sent, got)
    store = Stores(store_sem)

    def select(raw_ref):
        column = lax.broadcasted_iota(jnp.int32, (rows_all, raw_ref.shape[0]), 1)
        chosen = jnp.where(source[...] == column, 1.0, 0.0).astype(LOW)
        return nn(chosen, raw_ref[...]).astype(LOW)

    loads[0].wait()
    x[...] = select(raw.at[0])
    store(x, x_o)
    scaled, _ = standardize(x[...].astype(F32))
    low[...] = (scaled * gains[0:1] + biases[0:1]).astype(LOW)
    pair_rows = bias.shape[0]
    bias[...] = caption_bias(pair_rows, length)

    def self_half(half, weight):
        for j in range(3):
            s[half, j] = nn(low[...], weight[j]).astype(LOW)
            fetch.tick(0.35)
        for start in range(0, rows_all, pair_rows):
            rows = slice(start, start + pair_rows)
            for lane in range(0, local, PAIR):
                lanes = slice(lane, lane + PAIR)
                o[half, rows, lanes] = attend(
                    s[half, 0, rows, lanes], s[half, 1, rows, lanes], s[half, 2, rows, lanes], bias
                )
            fetch.tick(0.8)

    def keys_half(half, weight):
        flat = mem[...].reshape(images * span, width)
        for j in range(2):
            kv[half, j] = nn(flat, weight[j]).astype(LOW)
            fetch.tick(0.7)

    def cross_half(half, weight):
        qc[half] = nn(c[...], weight[...]).astype(LOW)
        some = rows_all // images
        fetch.tick(0.35)
        for step in range(images):
            rows = slice(step * some, (step + 1) * some)
            keys = slice(step * span, (step + 1) * span)
            for lane in range(0, local, PAIR):
                lanes = slice(lane, lane + PAIR)
                oc[half, rows, lanes] = attend(
                    qc[half, rows, lanes], kv[half, 0, keys, lanes], kv[half, 1, keys, lanes], None
                )
            fetch.tick(0.45)

    loads[1].wait()
    fetch.tick(2.5)
    self_half(0, m_qkv)
    loads[2].wait()
    loads[3].wait()
    keys_half(0, m_kv)
    loads[7].wait()
    cot[...] = select(raw.at[1])
    store(cot, cot_o)
    fetch.tick(1.0)
    loads[4].wait()
    fetch.need(0, 1, 2)
    store(t_qkv, t_qkv_o)
    self_half(1, t_qkv)
    store(s, s_o)
    store(o, o_o)
    fetch.need(3)
    store(t_out, t_out_o)
    h1[...] = x[...].astype(F32) + (nn(o[0], m_out[...]) + nn(o[1], t_out[...]))
    store(h1, h1_o)
    scaled, _ = standardize(h1[...])
    c[...] = (scaled * gains[1:2] + biases[1:2]).astype(LOW)
    store(c, c_o)
    fetch.tick(1.5)
    loads[5].wait()
    cross_half(0, m_query)
    fetch.need(4, 5)
    store(t_kv, t_kv_o)
    keys_half(1, t_kv)
    store(kv, kv_o)
    fetch.need(6)
    store(t_query, t_query_o)
    cross_half(1, t_query)
    store(qc, qc_o)
    store(oc, oc_o)
    loads[6].wait()
    fetch.need(7)
    store(t_mix, t_mix_o)
    h2[...] = h1[...] + (nn(oc[0], m_mix[...]) + nn(oc[1], t_mix[...]))
    scaled, _ = standardize(h2[...])
    low[...] = (scaled * gains[2:3] + biases[2:3]).astype(LOW)
    turned[...] = low[...].T
    fetch.tick(1.5)
    loads[8].wait()
    loads[9].wait()
    block = min(256, rows_all)
    open_parts = {}
    number = 0
    for half, (up, down, grads) in enumerate(((m_up, m_down, gm0), (t_up, t_down, gm1))):
        for index, start in enumerate(range(0, hidden, width)):
            if half == 1:
                fetch.need(*range(starts[index], starts[index] + 2 * per))
            cols = slice(start, start + width)

            for first in range(0, rows_all, block):
                rows = slice(first, first + block)
                u = nn(low[rows, :], up[:, cols])
                below = 0.5 + 0.5 * lax.erf(u * ROOT_HALF)
                z = (u * below).astype(LOW)
                z_ref[rows, :] = z
                dz = nt(cot[rows, :], down[cols, :])
                du = (dz * (below + u * (PDF_SCALE * jnp.exp(-0.5 * u * u)))).astype(LOW)
                du_ref[rows, :] = du
                more = nn(z, down[cols, :])
                more_back = nt(du, up[:, cols])
                if number == 0:
                    acc[rows, :] = h2[rows, :] + more
                    back[rows, :] = more_back
                else:
                    acc[rows, :] += more
                    back[rows, :] += more_back
                fetch.tick(1.4)
            slot = number % 2
            for copy in open_parts.pop(slot, ()):
                copy.wait()
            parts[slot, 0] = tn(z_ref[...], cot[...]).astype(LOW)
            fetch.tick(0.7)
            parts[slot, 1] = nn(turned[...], du_ref[...]).astype(LOW)
            fetch.tick(0.7)
            copies = [
                pltpu.make_async_copy(parts.at[slot, 0], grads.at[hidden + start : hidden + start + width], part_sem.at[slot, 0]),
                pltpu.make_async_copy(parts.at[slot, 1], grads.at[start : start + width], part_sem.at[slot, 1]),
            ]
            for copy in copies:
                copy.start()
            open_parts[slot] = copies
            number += 1
    y[...] = acc[...].astype(LOW)
    store(y, y_o)
    grad = back[...]
    scaled, inverse = standardize(h2[...])
    gain_grad[...] = column_sum(grad * scaled)
    bias_grad[...] = column_sum(grad)
    acc[...] = cot[...].astype(F32) + standardize_back(grad, scaled, inverse, gains[2:3])
    store(acc, dh2_o)
    for copies in open_parts.values():
        for copy in copies:
            copy.wait()
    store.wait()
    fetch.finish()


def ring_pieces(block):
    step = max(block // 3, 16)
    return [(start, min(step, block - start)) for start in range(0, block, step)]


def ring_shapes(chips, block, width):
    over = block // 3
    count = len(ring_pieces(block))
    dma = pltpu.SemaphoreType.DMA
    cube = pltpu.VMEM((2, chips, block, width), LOW)
    return [
        cube, cube, cube, cube,
        pltpu.VMEM((2, chips, block - over, width), LOW),
        pltpu.VMEM((2, chips - 1, block + over, width), LOW),
        pltpu.VMEM((2, over, width), LOW),
        dma((2, 2, chips)), dma((2, 2, chips)), dma((2, 2, chips)), dma((2, chips)), dma((2, chips)),
        dma((count + 1, 2, chips - 1)), dma((count + 1, 2, chips - 1)), dma((2,)), dma((2,)),
        dma((count, 2, chips - 1)), dma((count, 2, chips - 1)), dma((2, chips)), dma((2, chips)), dma((2,)),
    ]


RING = 21


class Ring:
    def __init__(self, chips, mine, theirs, total, refs):
        (self.own, self.other, self.core_own, self.core_other, self.from_y, self.ring, self.last,
         self.local, self.core_sent, self.core_got, self.y_sent, self.y_got, self.ring_sent, self.ring_got,
         self.last_sent, self.last_got, self.gather_sent, self.gather_got, self.back_sent, self.back_got,
         self.final_sem) = refs
        self.chips, self.mine, self.theirs, self.total = chips, mine, theirs, total
        dp = lax.axis_index("dp")
        side = lax.axis_index("tensor")
        self.core = dp % 2
        line, lane = dp // 4, (dp // 2) % 2
        self.place = line + lane * (chips - 1 - 2 * line)
        long = chips // 2

        def at(position):
            position = (position + chips) % chips
            x = position // long
            z = position + x * (chips - 1 - 2 * position)
            return 4 * z + 2 * x + self.core, side

        self.y, self.mate = partner("y"), partner("core")
        self.toward = (at(self.place + 1), at(self.place - 1))
        self.rows = self.own.shape[2]
        self.cut = self.from_y.shape[2]
        self.pieces = ring_pieces(self.rows)

    def greet(self):
        greet((self.y, self.mate, *self.toward))

    def number(self, d, slot):
        offset = self.chips // 2 - slot // 2 if slot % 2 == 0 else slot // 2 - (self.chips // 2 - 1)
        return (self.place + self.chips + (offset if d == 0 else -offset)) % self.chips

    def way(self, d, slot):
        return self.toward[(slot + d) % 2]

    def held(self, d, turn):
        offset = -(turn // 2) if turn % 2 == 0 else turn // 2
        return (self.place + self.chips + (offset if d == 0 else -offset)) % self.chips

    def spot(self, ref, which, d, number):
        base = (which * 2 + d) * (self.chips * self.rows) + number * self.rows
        return ref.at[pl.ds(pl.multiple_of(base, self.rows), self.rows)]

    def load(self, w, d, s):
        source = (self.mine, self.theirs)[w]
        target = (self.own, self.other)[w]
        return pltpu.make_async_copy(
            self.spot(source, self.core, d, self.number(d, s)), target.at[d, s], self.local.at[w, d, s]
        )

    def to_mate(self, w, d, s):
        source = (self.mine, self.theirs)[w]
        target = (self.core_own, self.core_other)[w]
        return remote(
            self.spot(source, 1 - self.core, d, self.number(d, s)), target.at[d, s],
            self.core_sent.at[w, d, s], self.core_got.at[w, d, s], self.mate,
        )

    def to_y(self, d, s):
        return remote(
            self.other.at[d, s, pl.ds(0, self.cut)], self.from_y.at[d, s], self.y_sent.at[d, s], self.y_got.at[d, s], self.y
        )

    def to_next(self, w, d, s):
        if w < len(self.pieces):
            start, size = self.pieces[w]
            source, target = self.own.at[d, s, pl.ds(start, size)], self.ring.at[d, s, pl.ds(start, size)]
        else:
            over = self.rows - self.cut
            source, target = self.other.at[d, s, pl.ds(self.cut, over)], self.ring.at[d, s, pl.ds(self.rows, over)]
        return remote(source, target, self.ring_sent.at[w, d, s], self.ring_got.at[w, d, s], self.way(d, s))

    def to_y_last(self, d):
        source = self.other.at[d, self.chips - 1, pl.ds(self.cut, self.rows - self.cut)]
        return remote(source, self.last.at[d], self.last_sent.at[d], self.last_got.at[d], self.y)

    def done(self, d, s, start=0, size=None):
        size = self.rows if size is None else size
        k = self.held(d, s)
        base = (self.core * 2 + d) * (self.chips * self.rows) + k * self.rows + start
        spot = self.total.at[pl.ds(pl.multiple_of(base, 8), size)]
        return (self.own.at[d, self.chips - 1, pl.ds(start, size)] if s < 2 else spot), spot

    def gather(self, w, d, s):
        source, spot = self.done(d, s, *self.pieces[w])
        return remote(source, spot, self.gather_sent.at[w, d, s], self.gather_got.at[w, d, s], self.way(d, s))

    def give_back(self, d, s):
        source, spot = self.done(d, s)
        return remote(source, spot, self.back_sent.at[d, s - 1], self.back_got.at[d, s - 1], self.mate)

    def keep(self, d):
        return pltpu.make_async_copy(*self.done(d, 0), self.final_sem.at[d])

    def begin(self):
        for s in range(self.chips):
            for d in range(2):
                for w in (1, 0):
                    self.load(w, d, s).start()
                    self.to_mate(w, d, s).start()

    def first(self, s, d):
        self.load(1, d, s).wait()
        self.to_mate(1, d, s).wait_recv()
        self.other[d, s] = (self.other[d, s].astype(F32) + self.core_other[d, s].astype(F32)).astype(LOW)
        self.to_y(d, s).start()

    def feeds(self, slot):
        if slot == self.chips - 1:
            return [slot - 2, slot - 1]
        return [slot - 2] if slot >= 2 else []

    def second(self, s, w):
        end = s == self.chips - 1
        if w == len(self.pieces):
            high = slice(self.cut, self.rows)
            for d in range(2):
                for k in self.feeds(s):
                    self.to_next(w, d, k).wait_recv()
                    more = self.ring[d, k, self.rows :].astype(F32)
                    self.other[d, s, high] = (self.other[d, s, high].astype(F32) + more).astype(LOW)
                if end:
                    self.to_y_last(d).start()
                else:
                    self.to_next(w, d, s).start()
            return
        start, size = self.pieces[w]
        rows = slice(start, start + size)
        for d in range(2):
            if w == 0:
                self.load(0, d, s).wait()
                self.to_mate(0, d, s).wait_recv()
                self.to_y(d, s).wait_recv()
            total = self.own[d, s, rows].astype(F32) + self.core_own[d, s, rows].astype(F32)
            if start < self.cut:
                total = total + self.from_y[d, s, rows].astype(F32)
            for k in self.feeds(s):
                self.to_next(w, d, k).wait_recv()
                total = total + self.ring[d, k, rows].astype(F32)
            self.own[d, s, rows] = total.astype(LOW)
            if not end:
                self.to_next(w, d, s).start()

    def turn(self, w):
        high = slice(self.cut, self.rows)
        s = self.chips - 1
        for d in range(2):
            if self.pieces[w][0] == self.cut:
                self.to_y_last(d).wait_recv()
                self.own[d, s, high] = (self.own[d, s, high].astype(F32) + self.last[d].astype(F32)).astype(LOW)
            for turn in range(2):
                self.gather(w, d, turn).start()
            if w == len(self.pieces) - 1:
                self.give_back(d, 1).start()
                self.keep(d).start()

    def spread(self, turn, w):
        for d in range(2):
            self.gather(w, d, turn - 2).wait_recv()
            if turn < self.chips - 1:
                self.gather(w, d, turn).start()
            if w == len(self.pieces) - 1:
                self.give_back(d, turn).start()

    def steps(self):
        part = functools.partial
        early = [part(self.first, s, d) for s in range(self.chips) for d in range(2)]
        sums, early = early[:4], early[4:]
        for s in range(self.chips):
            for w in range(len(self.pieces) + 1):
                sums.append(part(self.second, s, w))
                if early and w < 2:
                    sums.append(early.pop(0))
        count = len(self.pieces)
        return sums, [part(self.turn, w) for w in range(count)] + [
            part(self.spread, turn, w) for turn in range(2, self.chips + 1) for w in range(count)
        ]

    def finish(self):
        for d in range(2):
            self.keep(d).wait()
            self.to_y_last(d).wait_send()
            for s in range(self.chips):
                for w in range(2):
                    self.to_mate(w, d, s).wait_send()
                self.to_y(d, s).wait_send()
                self.give_back(d, s + 1).wait()
                if s < self.chips - 1:
                    for w in range(len(self.pieces) + 1):
                        self.to_next(w, d, s).wait_send()
                    for w in range(len(self.pieces)):
                        self.gather(w, d, s).wait_send()


class Share:
    def __init__(self, here, there, whole, sems):
        side = lax.axis_index("tensor")
        size = here.shape[0]
        target = whole.at[pl.ds(pl.multiple_of(side * size, size), size)]
        self.near = pltpu.make_async_copy(here, target, sems[0].at[0])
        self.far = remote(there, target, sems[1].at[0], sems[2].at[0], partner("y"))
        self.near.start()
        self.far.start()

    def finish(self):
        self.near.wait()
        self.far.wait()


def backward(
    length, chips, gm0, gm1, y_half, dh2_h, h1_h, memory, gains, biases, gain2, bias2, c_h, x_h, s_h, o_h, qc_h, kv_h, oc_h,
    w_qkv, w_out, w_kv, w_query, w_mix, t_qkv, t_out, t_kv, t_query, t_mix, *refs
):
    (ga0, ga1, m_sum, out_all, mem_all, x_o, small) = refs[:7]
    ring = Ring(chips, gm0, gm1, m_sum, refs[7 : 7 + RING])
    (dh, h1, mem, c, x, s, o, qc, kv, oc, wx, wo, low, a_ref, turned, dmix, dqkv, dkv, back, mem_acc, mem_half,
     wide_part, thin_part, out_part, bias, result, load_sem, weight_sem, store_sem, *share_sems) = refs[7 + RING :]
    side = lax.axis_index("tensor")
    images, span, width = mem.shape
    local = wo.shape[1]
    rows_all = x.shape[0]

    ring.greet()
    ring.begin()
    loads = {}
    for i, (name, source, target) in enumerate((
        ("dh", dh2_h, dh), ("oc", oc_h, oc), ("qc", qc_h, qc), ("kv", kv_h, kv), ("c", c_h, c),
        ("mem", memory.at[pl.ds(side * images, images)], mem), ("h1", h1_h, h1), ("x", x_h, x), ("s", s_h, s), ("o", o_h, o),
    )):
        loads[name] = pltpu.make_async_copy(source, target, load_sem.at[i])
        loads[name].start()

    def weights(half, cross):
        keys, q, out = ((w_kv, w_query, w_mix), (t_kv, t_query, t_mix))[half]
        big, end = ((w_qkv, w_out), (t_qkv, t_out))[half]
        pairs = ((keys, wx.at[half, 0:2]), (q, wx.at[half, 2]), (out, wo.at[half])) if cross else (
            (big, wx.at[half]), (end, wo.at[half]))
        copies = [
            pltpu.make_async_copy(source, target, weight_sem.at[0 if cross else 1, half, i])
            for i, (source, target) in enumerate(pairs)
        ]
        for copy in copies:
            copy.start()
        return copies

    held = [weights(0, True), weights(1, True)]
    sums, spread = ring.steps()
    shares = []

    def share_out():
        shares.append(Share(y_half, y_half, out_all, share_sems[:3]))

    todo = sums + [share_out] + spread
    clock = [0.0, 0]

    def tick(amount):
        clock[0] += amount
        while clock[1] < len(todo) and clock[0] >= BACK_FIRST + BACK_STEP * clock[1]:
            todo[clock[1]]()
            clock[1] += 1

    open_parts = {}
    count = [0]

    def put(slot, source, target):
        copy = pltpu.make_async_copy(source, target, store_sem.at[count[0]])
        count[0] += 1
        copy.start()
        open_parts.setdefault(slot, []).append(copy)

    def free(slot):
        for copy in open_parts.pop(slot, ()):
            copy.wait()

    def wait(*names):
        for name in names:
            loads[name].wait()

    wait("dh", "oc")
    low[...] = dh[...].astype(LOW)
    some = rows_all // images
    for half, grads in enumerate((ga0, ga1)):
        for copy in held[half]:
            copy.wait()
        out_part[half] = tn(oc[half], low[...]).astype(LOW)
        put(("out", half), out_part.at[half], grads.at[3 * width + local : 4 * width])
        tick(0.6)
        dmix[...] = nt(low[...], wo[half]).astype(LOW)
        tick(0.5)
        if half == 0:
            wait("qc", "kv")
        for step in range(images):
            rows = slice(step * some, (step + 1) * some)
            keys = slice(step * span, (step + 1) * span)
            for lane in range(0, local, PAIR):
                lanes = slice(lane, lane + PAIR)
                dqkv[0, rows, lanes], dkv[0, keys, lanes], dkv[1, keys, lanes] = attend_back(
                    qc[half, rows, lanes], kv[half, 0, keys, lanes], kv[half, 1, keys, lanes], dmix[rows, lanes], None
                )
                tick(0.45)
        if half == 0:
            wait("c", "mem")
        flat = mem[...].reshape(images * span, width)
        thin_part[half] = tn(c[...], dqkv[0]).astype(LOW)
        put(("thin", half), thin_part.at[half], grads.at[width : 2 * width, local:])
        tick(0.6)
        wide_part[half, :, :local] = tn(flat, dkv[0]).astype(LOW)
        tick(0.9)
        wide_part[half, :, local:] = tn(flat, dkv[1]).astype(LOW)
        put(("wide", half), wide_part.at[half], grads.at[2 * width : 3 * width])
        tick(1.0)
        more = nt(dqkv[0], wx[half, 2])
        if half == 0:
            back[...] = more
        else:
            back[...] += more
        tick(0.4)
        more_memory = nt(dkv[0], wx[half, 0]) + nt(dkv[1], wx[half, 1])
        if half == 0:
            mem_acc[...] = more_memory
        else:
            total = (mem_acc[...] + more_memory).astype(LOW)
            mem_half[0] = total[:, :local]
            mem_half[1] = total[:, local:]
            todo.insert(max(clock[1], len(sums) + 1), lambda: shares.append(Share(mem_half.at[side], mem_half.at[1 - side], mem_all, share_sems[3:6])))
        held[half] = weights(half, False)
        tick(1.4)
    wait("h1")
    grad = back[...]
    scaled, inverse = standardize(h1[...])
    small[1:2] = column_sum(grad * scaled)
    small[4:5] = column_sum(grad)
    dh[...] += standardize_back(grad, scaled, inverse, gains[1:2])
    small[2:3] = gain2[...]
    small[5:6] = bias2[...]
    small[6:8] = jnp.zeros((2, width), F32)
    low[...] = dh[...].astype(LOW)
    wait("x")
    scaled, _ = standardize(x[...].astype(F32))
    a_ref[...] = (scaled * gains[0:1] + biases[0:1]).astype(LOW)
    turned[...] = a_ref[...].T
    bias[...] = caption_bias(bias.shape[0], length)
    tick(2.5)
    group = bias.shape[0]
    wait("s", "o")
    for half, grads in enumerate((ga0, ga1)):
        for copy in held[half]:
            copy.wait()
        free(("out", half))
        out_part[half] = tn(o[half], low[...]).astype(LOW)
        put(("out", half), out_part.at[half], grads.at[3 * width : 3 * width + local])
        tick(0.5)
        dmix[...] = nt(low[...], wo[half]).astype(LOW)
        tick(0.5)
        for first in range(0, rows_all, group):
            rows = slice(first, first + group)
            for lane in range(0, local, PAIR):
                lanes = slice(lane, lane + PAIR)
                dqkv[0, rows, lanes], dqkv[1, rows, lanes], dqkv[2, rows, lanes] = attend_back(
                    s[half, 0, rows, lanes], s[half, 1, rows, lanes], s[half, 2, rows, lanes], dmix[rows, lanes], bias
                )
                tick(0.7)
        free(("wide", half))
        wide_part[half, :, :local] = nn(turned[...], dqkv[0]).astype(LOW)
        tick(0.5)
        wide_part[half, :, local:] = nn(turned[...], dqkv[1]).astype(LOW)
        put(("wide", half), wide_part.at[half], grads.at[0:width])
        tick(0.5)
        free(("thin", half))
        thin_part[half] = nn(turned[...], dqkv[2]).astype(LOW)
        put(("thin", half), thin_part.at[half], grads.at[width : 2 * width, :local])
        tick(0.5)
        more = nt(dqkv[0], wx[half, 0]) + nt(dqkv[1], wx[half, 1]) + nt(dqkv[2], wx[half, 2])
        if half == 0:
            back[...] = more
        else:
            back[...] += more
        tick(1.2)
    grad = back[...]
    scaled, inverse = standardize(x[...].astype(F32))
    small[0:1] = column_sum(grad * scaled)
    small[3:4] = column_sum(grad)
    result[...] = (dh[...] + standardize_back(grad, scaled, inverse, gains[0:1])).astype(LOW)
    put("result", result, x_o)
    while clock[1] < len(todo):
        todo[clock[1]]()
        clock[1] += 1
    for slot in list(open_parts):
        free(slot)
    ring.finish()
    for share in shares:
        share.finish()


def reduce_rest(chips, ga0, ga1, in_half, small, *refs):
    a_sum, in_all, small_sum = refs[:3]
    ring = Ring(chips, ga0, ga1, a_sum, refs[3 : 3 + RING])
    (small_core, small_pair, small_y, small_all, small_sent, small_got, round_sent, round_got, *share_sems) = refs[3 + RING :]
    ring.greet()
    ring.begin()
    small_mate = remote(small, small_core, small_sent.at[0], small_got.at[0], ring.mate)
    small_mate.start()
    small_across = remote(small_pair, small_y, small_sent.at[1], small_got.at[1], ring.y)

    def pass_small(s):
        slot = small_all.at[(ring.place + chips - s) % chips]
        return remote(slot, slot, round_sent.at[s], round_got.at[s], ring.toward[0])

    shares = []
    sums, spread = ring.steps()
    every = (len(sums) + len(spread)) // (chips + 1)
    for i, step in enumerate(sums + spread):
        step()
        small_turn, rest = divmod(i, every)
        if rest:
            pass
        elif small_turn == 0:
            small_mate.wait_recv()
            small_pair[...] = small[...] + small_core[...]
            small_across.start()
        elif small_turn == 1:
            small_across.wait_recv()
            small_all[ring.place] = small_pair[...] + small_y[...]
            pass_small(0).start()
        elif 2 <= small_turn < chips:
            pass_small(small_turn - 2).wait_recv()
            pass_small(small_turn - 1).start()
        if i == len(sums) - 1:
            shares.append(Share(in_half, in_half, in_all, share_sems))
    pass_small(chips - 2).wait_recv()
    total = small_all[0]
    for k in range(1, chips):
        total = total + small_all[k]
    small_sum[...] = total
    small_mate.wait_send()
    small_across.wait_send()
    for s in range(chips - 1):
        pass_small(s).wait_send()
    ring.finish()
    for share in shares:
        share.finish()


def unpack(
    length, order, m_sum, a_sum, y_all, x_all, out, inp, qkv, self_out, query, kv, mix, up, down,
    low, wide, acts, read_sems, write_sems, row_sems, act_sems,
):
    width = up.shape[0]
    local = self_out.shape[0]
    blocks = low.shape[0]
    reads = []
    for i in range(blocks):
        source = m_sum if i < blocks // 2 else a_sum
        row = i % (blocks // 2) * width
        copy = pltpu.make_async_copy(source.at[row : row + width], low.at[i], read_sems.at[i])
        copy.start()
        reads.append(copy)
    whole = [pltpu.make_async_copy(a, acts.at[k], act_sems.at[k]) for k, a in enumerate((y_all, x_all))]
    for copy in whole:
        copy.start()
    moves = []
    for k, target in enumerate((out, inp)):
        whole[k].wait()
        for i in range(order.shape[0]):
            rows = pl.ds(pl.multiple_of(order[i] * length, length), length)
            copy = pltpu.make_async_copy(acts.at[k, i * length : (i + 1) * length], target.at[rows], row_sems.at[k, i])
            copy.start()
            moves.append(copy)
    left, right = slice(0, local), slice(local, width)
    hidden = down.shape[0]
    targets = [[(slice(None), up.at[:, i * width : (i + 1) * width])] for i in range(hidden // width)]
    targets += [[(slice(None), down.at[i * width : (i + 1) * width])] for i in range(hidden // width)]
    targets += [
        [((slice(None), left), qkv.at[0]), ((slice(None), right), qkv.at[1])],
        [((slice(None), left), qkv.at[2]), ((slice(None), right), query)],
        [((slice(None), left), kv.at[0]), ((slice(None), right), kv.at[1])],
        [((left, slice(None)), self_out), ((right, slice(None)), mix)],
    ]
    store = Stores(write_sems)
    for i, places in enumerate(targets):
        reads[i].wait()
        wide[i] = low[i].astype(F32)
        for part, target in places:
            store(wide.at[i] if part == slice(None) else wide.at[(i, *part)], target)
    store.wait()
    for copy in moves:
        copy.wait()


def shape(dims, kind=LOW):
    return jax.ShapeDtypeStruct(dims, kind)


def call(body, name, args, outs, scratch, specs=None, out_specs=None, **params):
    return pl.pallas_call(
        body,
        out_shape=outs,
        in_specs=specs if specs is not None else [VMEM] * len(args),
        out_specs=out_specs if out_specs is not None else [VMEM] * len(outs),
        scratch_shapes=scratch,
        input_output_aliases=params.pop("aliases", {}),
        compiler_params=pltpu.CompilerParams(vmem_limit_bytes=VMEM_LIMIT, **params),
        name=name,
    )(*args)


def shards(
    chips, tokens, memory, groups, gains, biases, self_qkv, self_out, cross_query, cross_kv,
    cross_out, mlp_up, mlp_down, cotangent,
):
    captions = groups.shape[0]
    length = tokens.shape[0] // captions
    width = tokens.shape[1]
    images, span = memory.shape[:2]
    local = self_qkv.shape[2]
    hidden = mlp_up.shape[1]
    side = lax.axis_index("tensor")
    some = captions // 2 * length
    rows = images // 2 * span

    picked = groups - lax.axis_index("dp") * images
    same = picked[:, None] == picked[None, :]
    number = lax.broadcasted_iota(jnp.int32, (captions, captions), 0)
    other = lax.broadcasted_iota(jnp.int32, (captions, captions), 1)
    rank = 2 * picked + jnp.sum((same & (other < number)).astype(jnp.int32), axis=1)
    order = jnp.sum(jnp.where(rank[None, :] == number, other, 0), axis=1)
    mine = lax.dynamic_slice_in_dim(order, side * (captions // 2), captions // 2)
    source = (mine[:, None] * length + lax.broadcasted_iota(jnp.int32, (1, length), 1)).reshape(some, 1)

    part = hidden * 2
    row = shape((1, width), F32)
    group = min(some, 4 * length)
    mask = pltpu.VMEM((group, 2 * group), F32)
    dma = pltpu.SemaphoreType.DMA
    vm = pltpu.VMEM
    count = 8 + 2 * (hidden // local)
    weights = (self_qkv, self_out, cross_kv, cross_query, cross_out, mlp_up, mlp_down)
    held = [vm(w.shape, LOW) for w in weights]
    kept = [
        shape((some, width)), shape((some, width), F32), shape((2, 3, some, local)), shape((2, some, local)),
        shape((some, width)), shape((2, some, local)), shape((2, 2, rows, local)), shape((2, some, local)),
        shape((some, width)), shape((some, width)), shape((some, width), F32), shape((part, width)), shape((part, width)),
    ]
    (x, h1, s, o, c, qc, kvs, oc, cot, y_half, dh2, gm0, gm1, t_qkv, t_out, t_kv, t_query, t_mix, gain2, bias2) = call(
        functools.partial(forward, length), "forward",
        (tokens, cotangent, source, memory, gains, biases, *weights),
        kept + [shape(w.shape) for w in weights[:5]] + [row, row],
        [vm((2, *tokens.shape), LOW), vm((some, width), LOW), vm((some, width), LOW), vm((images // 2, span, width), LOW),
         vm((some, width), F32), vm((some, width), F32), vm((2, 3, some, local), LOW), vm((2, some, local), LOW),
         vm((some, width), LOW), vm((2, some, local), LOW), vm((2, 2, rows, local), LOW), vm((2, some, local), LOW),
         vm((some, width), LOW), vm((width, some), LOW), vm((some, width), F32), vm((some, width), F32),
         vm((some, width), LOW), mask, vm((some, width), LOW), vm((some, width), LOW), vm((2, 2, width, width), LOW)]
        + held + held
        + [dma((10,)), dma((16,)), dma((2, 2)), dma((9, count)), dma((9, count))],
        [ANY, ANY, VMEM, ANY, VMEM, VMEM] + [ANY] * 7, [ANY] * 18 + [VMEM] * 2,
        collective_id=0, has_side_effects=True,
    )
    attn_rows = 4 * width
    block = part // (4 * chips)
    ring = ring_shapes(chips, block, width)
    one = [dma((1,))] * 3
    ga0, ga1, m_sum, y_all, mem_all, x_half, small = call(
        functools.partial(backward, length, chips), "backward",
        (gm0, gm1, y_half, dh2, h1, memory, gains, biases, gain2, bias2, c, x, s, o, qc, kvs, oc, *weights[:5],
         t_qkv, t_out, t_kv, t_query, t_mix),
        [shape((attn_rows, width)), shape((attn_rows, width)), shape((part, width)), shape((2 * some, width)),
         shape((2 * rows, local)), shape((some, width)), shape((8, width), F32)],
        ring
        + [vm((some, width), F32), vm((some, width), F32), vm((images // 2, span, width), LOW), vm((some, width), LOW),
           vm((some, width), LOW), vm((2, 3, some, local), LOW), vm((2, some, local), LOW), vm((2, some, local), LOW),
           vm((2, 2, rows, local), LOW), vm((2, some, local), LOW), vm((2, 3, width, local), LOW), vm((2, local, width), LOW),
           vm((some, width), LOW), vm((some, width), LOW), vm((width, some), LOW), vm((some, local), LOW),
           vm((3, some, local), LOW), vm((2, rows, local), LOW), vm((some, width), F32), vm((rows, width), F32),
           vm((2, rows, local), LOW), vm((2, width, width), LOW), vm((2, width, local), LOW), vm((2, local, width), LOW),
           mask, vm((some, width), LOW), dma((10,)), dma((2, 2, 3)), dma((16,))]
        + one + one,
        [ANY] * 6 + [VMEM] * 4 + [ANY] * 17, [ANY] * 6 + [VMEM],
        collective_id=1, has_side_effects=True,
    )
    a_sum, x_all, small_sum = call(
        functools.partial(reduce_rest, chips), "reduce_rest", (ga0, ga1, x_half, small),
        [shape((attn_rows, width)), shape((2 * some, width)), shape((8, width), F32)],
        ring + [vm((8, width), F32)] * 3 + [vm((chips, 8, width), F32)] + [dma((2,))] * 2 + [dma((chips - 1,))] * 2 + one,
        [ANY] * 3 + [VMEM], [ANY, ANY, VMEM], collective_id=2, has_side_effects=True,
    )
    blocks = 2 * hidden // width + 4
    smem = pl.BlockSpec(memory_space=pltpu.SMEM)
    (output, input_grad, qkv_grad, out_grad, query_grad, kv_grad, mix_grad, up_grad, down_grad) = call(
        functools.partial(unpack, length), "unpack", (order, m_sum, a_sum, y_all, x_all),
        [shape(tokens.shape), shape(tokens.shape), shape(self_qkv.shape, F32), shape(self_out.shape, F32),
         shape(cross_query.shape, F32), shape(cross_kv.shape, F32), shape(cross_out.shape, F32),
         shape(mlp_up.shape, F32), shape(mlp_down.shape, F32)],
        [pltpu.VMEM((blocks, width, width), LOW), pltpu.VMEM((blocks, width, width), F32), pltpu.VMEM((2, *tokens.shape), LOW),
         dma((blocks,)),         dma((2 * blocks,)), dma((2, captions)), dma((2,))],
        [smem] + [ANY] * 4, [ANY] * 9,
    )
    return (
        output, input_grad, mem_all.reshape(images, span, local), small_sum[:3], small_sum[3:6], qkv_grad, out_grad,
        query_grad, kv_grad, mix_grad, up_grad, down_grad,
    )


def solution(mesh):
    rows = P("dp", None)
    columns = P(None, "tensor")
    stacked = P(None, None, "tensor")
    halves = P("tensor", None)
    return jax.shard_map(
        functools.partial(shards, mesh.shape["dp"] // 2),
        mesh=mesh,
        in_specs=(rows, P("dp", None, None), P("dp"), P(), P(), stacked, halves, columns, stacked, halves, columns, halves, rows),
        out_specs=(
            rows, rows, P("dp", None, "tensor"), P(), P(), stacked, halves, columns, stacked, halves, columns, halves,
        ),
        check_vma=False,
    )
```

```python
import functools

import jax
import jax.numpy as jnp
from jax import lax
from jax.experimental import pallas as pl
from jax.experimental.pallas import tpu as pltpu
from jax.sharding import PartitionSpec as P

HEAD_DIM = 64
SCALE = HEAD_DIM**-0.5
PAIR = 2 * HEAD_DIM
EPSILON = 1e-05
ROOT_HALF = 0.7071067811865476
PDF_SCALE = 0.3989422804014327
MESH = pl.DeviceIdType.MESH
LOW = jnp.bfloat16
F32 = jnp.float32
BACK_FIRST = 2.0
BACK_STEP = 0.45
FETCH_PACE = ((4.0, 1.7), (6.5, 2.4), (9.0, 2.4))
VMEM_LIMIT = 60 * 1024 * 1024
ANY = pl.BlockSpec(memory_space=pl.ANY)
VMEM = pl.BlockSpec(memory_space=pltpu.VMEM)


def nn(left, right):
    return lax.dot_general(left, right, (((1,), (0,)), ((), ())), preferred_element_type=F32)


def nt(left, right):
    return lax.dot_general(left, right, (((1,), (1,)), ((), ())), preferred_element_type=F32)


def tn(left, right):
    return lax.dot_general(left, right, (((0,), (0,)), ((), ())), preferred_element_type=F32)


def standardize(values):
    average = jnp.mean(values, axis=-1, keepdims=True)
    centred = values - average
    inverse = lax.rsqrt(jnp.mean(centred * centred, axis=-1, keepdims=True) + EPSILON)
    return centred * inverse, inverse


def standardize_back(grad_out, scaled, inverse, gain_row):
    weighted = grad_out * gain_row
    return inverse * (
        weighted
        - jnp.mean(weighted, axis=-1, keepdims=True)
        - scaled * jnp.mean(weighted * scaled, axis=-1, keepdims=True)
    )


def column_sum(values):
    return jnp.sum(values, axis=0, keepdims=True)


def softmax_down(scores):
    weights = jnp.exp(scores - jnp.max(scores, axis=0, keepdims=True))
    return weights * (1.0 / jnp.sum(weights, axis=0, keepdims=True))


def first_lanes():
    return lax.broadcasted_iota(jnp.int32, (1, PAIR), 1) < HEAD_DIM


def stack_heads(values):
    zeros = jnp.zeros_like(values)
    first = first_lanes()
    return jnp.concatenate([jnp.where(first, values, zeros), jnp.where(first, zeros, values)], axis=0)


def pick_heads(stacked):
    rows = stacked.shape[0] // 2
    return jnp.where(first_lanes(), stacked[:rows], stacked[rows:])


def caption_bias(rows, length):
    key = lax.broadcasted_iota(jnp.int32, (rows, rows), 0)
    query = lax.broadcasted_iota(jnp.int32, (rows, rows), 1)
    allowed = query >= key
    for edge in range(length, rows, length):
        allowed = allowed & ((query < edge) | (key >= edge))
    bias = jnp.where(allowed, 0.0, -1e30)
    return jnp.concatenate([bias, bias], axis=1)


def attend(queries, keys, values, bias):
    scores = nt(keys, stack_heads(queries * jnp.asarray(SCALE, LOW)))
    if bias is not None:
        scores = scores + bias[...]
    return pick_heads(tn(softmax_down(scores).astype(LOW), values)).astype(LOW)


def attend_back(queries, keys, values, grads, bias):
    stacked = stack_heads(queries * jnp.asarray(SCALE, LOW))
    stacked_grads = stack_heads(grads)
    scores = nt(keys, stacked)
    if bias is not None:
        scores = scores + bias[...]
    probs = softmax_down(scores)
    prob_grad = nt(values, stacked_grads)
    score_low = (probs * (prob_grad - jnp.sum(probs * prob_grad, axis=0, keepdims=True))).astype(LOW)
    query_grad = pick_heads(tn(score_low, keys)) * SCALE
    return query_grad.astype(LOW), nn(score_low, stacked).astype(LOW), nn(probs.astype(LOW), stacked_grads).astype(LOW)


class Stores:
    def __init__(self, sems):
        self.sems = sems
        self.copies = []

    def __call__(self, source, target):
        copy = pltpu.make_async_copy(source, target, self.sems.at[len(self.copies)])
        copy.start()
        self.copies.append(copy)

    def wait(self):
        for copy in self.copies:
            copy.wait()


def partner(axis):
    dp = lax.axis_index("dp")
    side = lax.axis_index("tensor")
    if axis == "y":
        return dp, 1 - side
    if axis == "core":
        return dp + 1 - 2 * (dp % 2), side
    if axis == "z":
        return dp + 4 - 8 * ((dp // 4) % 2), side
    return dp + 2 - 4 * ((dp // 2) % 2), side


def greet(devices):
    barrier = pltpu.get_barrier_semaphore()
    for device in devices:
        pl.semaphore_signal(barrier, inc=1, device_id=device, device_id_type=MESH)
    pl.semaphore_wait(barrier, len(devices))


def remote(source, target, send, recv, device):
    return pltpu.make_async_remote_copy(
        src_ref=source, dst_ref=target, send_sem=send, recv_sem=recv, device_id=device, device_id_type=MESH
    )


class Fetch:
    def __init__(self, items, sent, got):
        self.items, self.sent, self.got = items, sent, got
        dp = lax.axis_index("dp")
        self.y, self.x, self.z, self.core = (partner(axis) for axis in ("y", "x", "z", "core"))
        self.here = dp % 8
        x, z = (dp // 2) % 2, (dp // 4) % 2
        self.from_x = self.here + 2 - 4 * x
        self.from_z = self.here + 4 - 8 * z
        self.from_both = self.from_x + 4 - 8 * z
        self.steps = [0, 0, 0]
        self.clock = 0.0
        greet((self.y, self.x, self.z, self.core))
        for k in range(len(items)):
            self.across(k).start()

    def piece(self, ref, number, part=None):
        size = ref.shape[0] // 8
        start = pl.multiple_of(number * size, size)
        if part is None:
            return ref.at[pl.ds(start, size)]
        cut = (size // 2 + 15) // 16 * 16
        if part == 0:
            return ref.at[pl.ds(start, cut)]
        return ref.at[pl.ds(pl.multiple_of(start + cut, 16), size - cut)]

    def move(self, k, lane, device, number, part=None):
        spot = self.piece(self.items[k][1], number, part)
        return remote(spot, spot, self.sent.at[lane, k], self.got.at[lane, k], device)

    def across(self, k):
        mine, theirs = self.items[k]
        return remote(
            self.piece(mine, self.here), self.piece(theirs, self.here), self.sent.at[0, k], self.got.at[0, k], self.y
        )

    def copy(self, k, lane):
        if lane == 0:
            return self.across(k)
        device = (None, self.x, self.z, self.x, self.z, self.core, self.core, self.core, self.core)[lane]
        number = (None, self.here, self.here, self.from_z, self.from_x, self.here, self.from_x, self.from_z, self.from_both)
        return self.move(k, lane, device, number[lane], {3: 0, 4: 1}.get(lane))

    def stage(self, which):
        k = self.steps[which]
        self.steps[which] += 1
        if which == 0:
            self.copy(k, 0).wait_recv()
            for lane in (1, 2, 5):
                self.copy(k, lane).start()
        elif which == 1:
            self.copy(k, 1).wait_recv()
            self.copy(k, 4).start()
            self.copy(k, 6).start()
            self.copy(k, 2).wait_recv()
            self.copy(k, 3).start()
            self.copy(k, 7).start()
        else:
            self.copy(k, 3).wait_recv()
            self.copy(k, 4).wait_recv()
            self.copy(k, 8).start()

    def tick(self, amount):
        self.clock += amount
        for which, (first, pace) in enumerate(FETCH_PACE):
            limit = len(self.items) if which == 0 else self.steps[which - 1]
            while self.steps[which] < limit and self.clock >= first + pace * self.steps[which]:
                self.stage(which)

    def need(self, *numbers):
        first, pace = FETCH_PACE[2]
        self.clock = max(self.clock, first + pace * max(numbers))
        self.tick(0)
        for which in range(3):
            while self.steps[which] <= max(numbers):
                self.stage(which)
        for k in numbers:
            for lane in range(5, 9):
                self.copy(k, lane).wait_recv()

    def finish(self):
        for k in range(len(self.items)):
            for lane in range(9):
                self.copy(k, lane).wait_send()


def forward(length, tokens, cotangent, source, memory, gains, biases, *refs):
    (w_qkv, w_out, w_kv, w_query, w_mix, w_up, w_down) = refs[:7]
    (x_o, h1_o, s_o, o_o, c_o, qc_o, kv_o, oc_o, cot_o, y_o, dh2_o, gm0, gm1,
     t_qkv_o, t_out_o, t_kv_o, t_query_o, t_mix_o, gain_grad, bias_grad) = refs[7:27]
    (raw, x, cot, mem, h1, h2, s, o, c, qc, kv, oc, low, turned, acc, back, y, bias, z_ref, du_ref, parts,
     m_qkv, m_out, m_kv, m_query, m_mix, m_up, m_down,
     t_qkv, t_out, t_kv, t_query, t_mix, t_up, t_down,
     load_sem, store_sem, part_sem, sent, got) = refs[27:]
    side = lax.axis_index("tensor")
    images = mem.shape[0]
    span = mem.shape[1]
    width = x.shape[1]
    local = m_out.shape[0]
    hidden = m_down.shape[0]
    rows_all = x.shape[0]

    loads = [
        pltpu.make_async_copy(a, b, load_sem.at[i])
        for i, (a, b) in enumerate((
            (tokens, raw.at[0]), (w_qkv, m_qkv), (memory.at[pl.ds(side * images, images)], mem), (w_kv, m_kv),
            (w_out, m_out), (w_query, m_query), (w_mix, m_mix), (cotangent, raw.at[1]), (w_up, m_up), (w_down, m_down),
        ))
    ]
    for copy in loads:
        copy.start()
    blocks = [slice(i, i + local) for i in range(0, hidden, local)]
    items = [(w_qkv.at[j], t_qkv.at[j]) for j in range(3)] + [(w_out, t_out)]
    items += [(w_kv.at[j], t_kv.at[j]) for j in range(2)] + [(w_query, t_query), (w_mix, t_mix)]
    per = width // local
    starts = []
    for first in range(0, len(blocks), per):
        starts.append(len(items))
        items += [(w_up.at[:, b], t_up.at[:, b]) for b in blocks[first : first + per]]
        items += [(w_down.at[b], t_down.at[b]) for b in blocks[first : first + per]]
    fetch = Fetch(items, sent, got)
    store = Stores(store_sem)

    def select(raw_ref):
        column = lax.broadcasted_iota(jnp.int32, (rows_all, raw_ref.shape[0]), 1)
        chosen = jnp.where(source[...] == column, 1.0, 0.0).astype(LOW)
        return nn(chosen, raw_ref[...]).astype(LOW)

    loads[0].wait()
    x[...] = select(raw.at[0])
    store(x, x_o)
    scaled, _ = standardize(x[...].astype(F32))
    low[...] = (scaled * gains[0:1] + biases[0:1]).astype(LOW)
    pair_rows = bias.shape[0]
    bias[...] = caption_bias(pair_rows, length)

    def self_half(half, weight):
        for j in range(3):
            s[half, j] = nn(low[...], weight[j]).astype(LOW)
            fetch.tick(0.35)
        for start in range(0, rows_all, pair_rows):
            rows = slice(start, start + pair_rows)
            for lane in range(0, local, PAIR):
                lanes = slice(lane, lane + PAIR)
                o[half, rows, lanes] = attend(
                    s[half, 0, rows, lanes], s[half, 1, rows, lanes], s[half, 2, rows, lanes], bias
                )
            fetch.tick(0.8)

    def keys_half(half, weight):
        flat = mem[...].reshape(images * span, width)
        for j in range(2):
            kv[half, j] = nn(flat, weight[j]).astype(LOW)
            fetch.tick(0.7)

    def cross_half(half, weight):
        qc[half] = nn(c[...], weight[...]).astype(LOW)
        some = rows_all // images
        fetch.tick(0.35)
        for step in range(images):
            rows = slice(step * some, (step + 1) * some)
            keys = slice(step * span, (step + 1) * span)
            for lane in range(0, local, PAIR):
                lanes = slice(lane, lane + PAIR)
                oc[half, rows, lanes] = attend(
                    qc[half, rows, lanes], kv[half, 0, keys, lanes], kv[half, 1, keys, lanes], None
                )
            fetch.tick(0.45)

    loads[1].wait()
    fetch.tick(2.5)
    self_half(0, m_qkv)
    loads[2].wait()
    loads[3].wait()
    keys_half(0, m_kv)
    loads[7].wait()
    cot[...] = select(raw.at[1])
    store(cot, cot_o)
    fetch.tick(1.0)
    loads[4].wait()
    fetch.need(0, 1, 2)
    store(t_qkv, t_qkv_o)
    self_half(1, t_qkv)
    store(s, s_o)
    store(o, o_o)
    fetch.need(3)
    store(t_out, t_out_o)
    h1[...] = x[...].astype(F32) + (nn(o[0], m_out[...]) + nn(o[1], t_out[...]))
    store(h1, h1_o)
    scaled, _ = standardize(h1[...])
    c[...] = (scaled * gains[1:2] + biases[1:2]).astype(LOW)
    store(c, c_o)
    fetch.tick(1.5)
    loads[5].wait()
    cross_half(0, m_query)
    fetch.need(4, 5)
    store(t_kv, t_kv_o)
    keys_half(1, t_kv)
    store(kv, kv_o)
    fetch.need(6)
    store(t_query, t_query_o)
    cross_half(1, t_query)
    store(qc, qc_o)
    store(oc, oc_o)
    loads[6].wait()
    fetch.need(7)
    store(t_mix, t_mix_o)
    h2[...] = h1[...] + (nn(oc[0], m_mix[...]) + nn(oc[1], t_mix[...]))
    scaled, _ = standardize(h2[...])
    low[...] = (scaled * gains[2:3] + biases[2:3]).astype(LOW)
    turned[...] = low[...].T
    fetch.tick(1.5)
    loads[8].wait()
    loads[9].wait()
    block = min(256, rows_all)
    open_parts = {}
    number = 0
    for half, (up, down, grads) in enumerate(((m_up, m_down, gm0), (t_up, t_down, gm1))):
        for index, start in enumerate(range(0, hidden, width)):
            if half == 1:
                fetch.need(*range(starts[index], starts[index] + 2 * per))
            cols = slice(start, start + width)

            for first in range(0, rows_all, block):
                rows = slice(first, first + block)
                u = nn(low[rows, :], up[:, cols])
                below = 0.5 + 0.5 * lax.erf(u * ROOT_HALF)
                z = (u * below).astype(LOW)
                z_ref[rows, :] = z
                dz = nt(cot[rows, :], down[cols, :])
                du = (dz * (below + u * (PDF_SCALE * jnp.exp(-0.5 * u * u)))).astype(LOW)
                du_ref[rows, :] = du
                more = nn(z, down[cols, :])
                more_back = nt(du, up[:, cols])
                if number == 0:
                    acc[rows, :] = h2[rows, :] + more
                    back[rows, :] = more_back
                else:
                    acc[rows, :] += more
                    back[rows, :] += more_back
                fetch.tick(1.4)
            slot = number % 2
            for copy in open_parts.pop(slot, ()):
                copy.wait()
            parts[slot, 0] = tn(z_ref[...], cot[...]).astype(LOW)
            fetch.tick(0.7)
            parts[slot, 1] = nn(turned[...], du_ref[...]).astype(LOW)
            fetch.tick(0.7)
            copies = [
                pltpu.make_async_copy(parts.at[slot, 0], grads.at[hidden + start : hidden + start + width], part_sem.at[slot, 0]),
                pltpu.make_async_copy(parts.at[slot, 1], grads.at[start : start + width], part_sem.at[slot, 1]),
            ]
            for copy in copies:
                copy.start()
            open_parts[slot] = copies
            number += 1
    y[...] = acc[...].astype(LOW)
    store(y, y_o)
    grad = back[...]
    scaled, inverse = standardize(h2[...])
    gain_grad[...] = column_sum(grad * scaled)
    bias_grad[...] = column_sum(grad)
    acc[...] = cot[...].astype(F32) + standardize_back(grad, scaled, inverse, gains[2:3])
    store(acc, dh2_o)
    for copies in open_parts.values():
        for copy in copies:
            copy.wait()
    store.wait()
    fetch.finish()


def ring_pieces(block):
    step = max(block // 3, 16)
    return [(start, min(step, block - start)) for start in range(0, block, step)]


def ring_shapes(chips, block, width):
    over = block // 3
    count = len(ring_pieces(block))
    dma = pltpu.SemaphoreType.DMA
    cube = pltpu.VMEM((2, chips, block, width), LOW)
    return [
        cube, cube, cube, cube,
        pltpu.VMEM((2, chips, block - over, width), LOW),
        pltpu.VMEM((2, chips - 1, block + over, width), LOW),
        pltpu.VMEM((2, over, width), LOW),
        dma((2, 2, chips)), dma((2, 2, chips)), dma((2, 2, chips)), dma((2, chips)), dma((2, chips)),
        dma((count + 1, 2, chips - 1)), dma((count + 1, 2, chips - 1)), dma((2,)), dma((2,)),
        dma((count, 2, chips - 1)), dma((count, 2, chips - 1)), dma((2, chips)), dma((2, chips)), dma((2,)),
    ]


RING = 21


class Ring:
    def __init__(self, chips, mine, theirs, total, refs):
        (self.own, self.other, self.core_own, self.core_other, self.from_y, self.ring, self.last,
         self.local, self.core_sent, self.core_got, self.y_sent, self.y_got, self.ring_sent, self.ring_got,
         self.last_sent, self.last_got, self.gather_sent, self.gather_got, self.back_sent, self.back_got,
         self.final_sem) = refs
        self.chips, self.mine, self.theirs, self.total = chips, mine, theirs, total
        dp = lax.axis_index("dp")
        side = lax.axis_index("tensor")
        self.core = dp % 2
        line, lane = dp // 4, (dp // 2) % 2
        self.place = line + lane * (chips - 1 - 2 * line)
        long = chips // 2

        def at(position):
            position = (position + chips) % chips
            x = position // long
            z = position + x * (chips - 1 - 2 * position)
            return 4 * z + 2 * x + self.core, side

        self.y, self.mate = partner("y"), partner("core")
        self.toward = (at(self.place + 1), at(self.place - 1))
        self.rows = self.own.shape[2]
        self.cut = self.from_y.shape[2]
        self.pieces = ring_pieces(self.rows)

    def greet(self):
        greet((self.y, self.mate, *self.toward))

    def number(self, d, slot):
        offset = self.chips // 2 - slot // 2 if slot % 2 == 0 else slot // 2 - (self.chips // 2 - 1)
        return (self.place + self.chips + (offset if d == 0 else -offset)) % self.chips

    def way(self, d, slot):
        return self.toward[(slot + d) % 2]

    def held(self, d, turn):
        offset = -(turn // 2) if turn % 2 == 0 else turn // 2
        return (self.place + self.chips + (offset if d == 0 else -offset)) % self.chips

    def spot(self, ref, which, d, number):
        base = (which * 2 + d) * (self.chips * self.rows) + number * self.rows
        return ref.at[pl.ds(pl.multiple_of(base, self.rows), self.rows)]

    def load(self, w, d, s):
        source = (self.mine, self.theirs)[w]
        target = (self.own, self.other)[w]
        return pltpu.make_async_copy(
            self.spot(source, self.core, d, self.number(d, s)), target.at[d, s], self.local.at[w, d, s]
        )

    def to_mate(self, w, d, s):
        source = (self.mine, self.theirs)[w]
        target = (self.core_own, self.core_other)[w]
        return remote(
            self.spot(source, 1 - self.core, d, self.number(d, s)), target.at[d, s],
            self.core_sent.at[w, d, s], self.core_got.at[w, d, s], self.mate,
        )

    def to_y(self, d, s):
        return remote(
            self.other.at[d, s, pl.ds(0, self.cut)], self.from_y.at[d, s], self.y_sent.at[d, s], self.y_got.at[d, s], self.y
        )

    def to_next(self, w, d, s):
        if w < len(self.pieces):
            start, size = self.pieces[w]
            source, target = self.own.at[d, s, pl.ds(start, size)], self.ring.at[d, s, pl.ds(start, size)]
        else:
            over = self.rows - self.cut
            source, target = self.other.at[d, s, pl.ds(self.cut, over)], self.ring.at[d, s, pl.ds(self.rows, over)]
        return remote(source, target, self.ring_sent.at[w, d, s], self.ring_got.at[w, d, s], self.way(d, s))

    def to_y_last(self, d):
        source = self.other.at[d, self.chips - 1, pl.ds(self.cut, self.rows - self.cut)]
        return remote(source, self.last.at[d], self.last_sent.at[d], self.last_got.at[d], self.y)

    def done(self, d, s, start=0, size=None):
        size = self.rows if size is None else size
        k = self.held(d, s)
        base = (self.core * 2 + d) * (self.chips * self.rows) + k * self.rows + start
        spot = self.total.at[pl.ds(pl.multiple_of(base, 8), size)]
        return (self.own.at[d, self.chips - 1, pl.ds(start, size)] if s < 2 else spot), spot

    def gather(self, w, d, s):
        source, spot = self.done(d, s, *self.pieces[w])
        return remote(source, spot, self.gather_sent.at[w, d, s], self.gather_got.at[w, d, s], self.way(d, s))

    def give_back(self, d, s):
        source, spot = self.done(d, s)
        return remote(source, spot, self.back_sent.at[d, s - 1], self.back_got.at[d, s - 1], self.mate)

    def keep(self, d):
        return pltpu.make_async_copy(*self.done(d, 0), self.final_sem.at[d])

    def begin(self):
        for s in range(self.chips):
            for d in range(2):
                for w in (1, 0):
                    self.load(w, d, s).start()
                    self.to_mate(w, d, s).start()

    def first(self, s, d):
        self.load(1, d, s).wait()
        self.to_mate(1, d, s).wait_recv()
        self.other[d, s] = (self.other[d, s].astype(F32) + self.core_other[d, s].astype(F32)).astype(LOW)
        self.to_y(d, s).start()

    def feeds(self, slot):
        if slot == self.chips - 1:
            return [slot - 2, slot - 1]
        return [slot - 2] if slot >= 2 else []

    def second(self, s, w):
        end = s == self.chips - 1
        if w == len(self.pieces):
            high = slice(self.cut, self.rows)
            for d in range(2):
                for k in self.feeds(s):
                    self.to_next(w, d, k).wait_recv()
                    more = self.ring[d, k, self.rows :].astype(F32)
                    self.other[d, s, high] = (self.other[d, s, high].astype(F32) + more).astype(LOW)
                if end:
                    self.to_y_last(d).start()
                else:
                    self.to_next(w, d, s).start()
            return
        start, size = self.pieces[w]
        rows = slice(start, start + size)
        for d in range(2):
            if w == 0:
                self.load(0, d, s).wait()
                self.to_mate(0, d, s).wait_recv()
                self.to_y(d, s).wait_recv()
            total = self.own[d, s, rows].astype(F32) + self.core_own[d, s, rows].astype(F32)
            if start < self.cut:
                total = total + self.from_y[d, s, rows].astype(F32)
            for k in self.feeds(s):
                self.to_next(w, d, k).wait_recv()
                total = total + self.ring[d, k, rows].astype(F32)
            self.own[d, s, rows] = total.astype(LOW)
            if not end:
                self.to_next(w, d, s).start()

    def turn(self, w):
        high = slice(self.cut, self.rows)
        s = self.chips - 1
        for d in range(2):
            if self.pieces[w][0] == self.cut:
                self.to_y_last(d).wait_recv()
                self.own[d, s, high] = (self.own[d, s, high].astype(F32) + self.last[d].astype(F32)).astype(LOW)
            for turn in range(2):
                self.gather(w, d, turn).start()
            if w == len(self.pieces) - 1:
                self.give_back(d, 1).start()
                self.keep(d).start()

    def spread(self, turn, w):
        for d in range(2):
            self.gather(w, d, turn - 2).wait_recv()
            if turn < self.chips - 1:
                self.gather(w, d, turn).start()
            if w == len(self.pieces) - 1:
                self.give_back(d, turn).start()

    def steps(self):
        part = functools.partial
        early = [part(self.first, s, d) for s in range(self.chips) for d in range(2)]
        sums, early = early[:8], early[8:]
        for s in range(self.chips):
            for w in range(len(self.pieces) + 1):
                sums.append(part(self.second, s, w))
                if early and w < 2:
                    sums.append(early.pop(0))
        count = len(self.pieces)
        return sums, [part(self.turn, w) for w in range(count)] + [
            part(self.spread, turn, w) for turn in range(2, self.chips + 1) for w in range(count)
        ]

    def finish(self):
        for d in range(2):
            self.keep(d).wait()
            self.to_y_last(d).wait_send()
            for s in range(self.chips):
                for w in range(2):
                    self.to_mate(w, d, s).wait_send()
                self.to_y(d, s).wait_send()
                self.give_back(d, s + 1).wait()
                if s < self.chips - 1:
                    for w in range(len(self.pieces) + 1):
                        self.to_next(w, d, s).wait_send()
                    for w in range(len(self.pieces)):
                        self.gather(w, d, s).wait_send()


class Share:
    def __init__(self, here, there, whole, sems):
        side = lax.axis_index("tensor")
        size = here.shape[0]
        target = whole.at[pl.ds(pl.multiple_of(side * size, size), size)]
        self.near = pltpu.make_async_copy(here, target, sems[0].at[0])
        self.far = remote(there, target, sems[1].at[0], sems[2].at[0], partner("y"))
        self.near.start()
        self.far.start()

    def finish(self):
        self.near.wait()
        self.far.wait()


def backward(
    length, chips, gm0, gm1, y_half, dh2_h, h1_h, memory, gains, biases, gain2, bias2, c_h, x_h, s_h, o_h, qc_h, kv_h, oc_h,
    w_qkv, w_out, w_kv, w_query, w_mix, t_qkv, t_out, t_kv, t_query, t_mix, *refs
):
    (ga0, ga1, m_sum, out_all, mem_all, x_o, small) = refs[:7]
    ring = Ring(chips, gm0, gm1, m_sum, refs[7 : 7 + RING])
    (dh, h1, mem, c, x, s, o, qc, kv, oc, wx, wo, low, a_ref, turned, dmix, dqkv, dkv, back, mem_acc, mem_half,
     wide_part, thin_part, out_part, bias, result, load_sem, weight_sem, store_sem, *share_sems) = refs[7 + RING :]
    side = lax.axis_index("tensor")
    images, span, width = mem.shape
    local = wo.shape[1]
    rows_all = x.shape[0]

    ring.greet()
    ring.begin()
    loads = {}
    for i, (name, source, target) in enumerate((
        ("dh", dh2_h, dh), ("oc", oc_h, oc), ("qc", qc_h, qc), ("kv", kv_h, kv), ("c", c_h, c),
        ("mem", memory.at[pl.ds(side * images, images)], mem), ("h1", h1_h, h1), ("x", x_h, x), ("s", s_h, s), ("o", o_h, o),
    )):
        loads[name] = pltpu.make_async_copy(source, target, load_sem.at[i])
        loads[name].start()

    def weights(half, cross):
        keys, q, out = ((w_kv, w_query, w_mix), (t_kv, t_query, t_mix))[half]
        big, end = ((w_qkv, w_out), (t_qkv, t_out))[half]
        pairs = ((keys, wx.at[half, 0:2]), (q, wx.at[half, 2]), (out, wo.at[half])) if cross else (
            (big, wx.at[half]), (end, wo.at[half]))
        copies = [
            pltpu.make_async_copy(source, target, weight_sem.at[0 if cross else 1, half, i])
            for i, (source, target) in enumerate(pairs)
        ]
        for copy in copies:
            copy.start()
        return copies

    held = [weights(0, True), weights(1, True)]
    sums, spread = ring.steps()
    shares = []

    def share_out():
        shares.append(Share(y_half, y_half, out_all, share_sems[:3]))

    todo = sums + [share_out] + spread
    clock = [0.0, 0]

    def tick(amount):
        clock[0] += amount
        while clock[1] < len(todo) and clock[0] >= BACK_FIRST + BACK_STEP * clock[1]:
            todo[clock[1]]()
            clock[1] += 1

    open_parts = {}
    count = [0]

    def put(slot, source, target):
        copy = pltpu.make_async_copy(source, target, store_sem.at[count[0]])
        count[0] += 1
        copy.start()
        open_parts.setdefault(slot, []).append(copy)

    def free(slot):
        for copy in open_parts.pop(slot, ()):
            copy.wait()

    def wait(*names):
        for name in names:
            loads[name].wait()

    wait("dh", "oc")
    low[...] = dh[...].astype(LOW)
    some = rows_all // images
    for half, grads in enumerate((ga0, ga1)):
        for copy in held[half]:
            copy.wait()
        out_part[half] = tn(oc[half], low[...]).astype(LOW)
        put(("out", half), out_part.at[half], grads.at[3 * width + local : 4 * width])
        tick(0.6)
        dmix[...] = nt(low[...], wo[half]).astype(LOW)
        tick(0.5)
        if half == 0:
            wait("qc", "kv")
        for step in range(images):
            rows = slice(step * some, (step + 1) * some)
            keys = slice(step * span, (step + 1) * span)
            for lane in range(0, local, PAIR):
                lanes = slice(lane, lane + PAIR)
                dqkv[0, rows, lanes], dkv[0, keys, lanes], dkv[1, keys, lanes] = attend_back(
                    qc[half, rows, lanes], kv[half, 0, keys, lanes], kv[half, 1, keys, lanes], dmix[rows, lanes], None
                )
                tick(0.45)
        if half == 0:
            wait("c", "mem")
        flat = mem[...].reshape(images * span, width)
        thin_part[half] = tn(c[...], dqkv[0]).astype(LOW)
        put(("thin", half), thin_part.at[half], grads.at[width : 2 * width, local:])
        tick(0.6)
        wide_part[half, :, :local] = tn(flat, dkv[0]).astype(LOW)
        tick(0.9)
        wide_part[half, :, local:] = tn(flat, dkv[1]).astype(LOW)
        put(("wide", half), wide_part.at[half], grads.at[2 * width : 3 * width])
        tick(1.0)
        more = nt(dqkv[0], wx[half, 2])
        if half == 0:
            back[...] = more
        else:
            back[...] += more
        tick(0.4)
        more_memory = nt(dkv[0], wx[half, 0]) + nt(dkv[1], wx[half, 1])
        if half == 0:
            mem_acc[...] = more_memory
        else:
            total = (mem_acc[...] + more_memory).astype(LOW)
            mem_half[0] = total[:, :local]
            mem_half[1] = total[:, local:]
            todo.insert(max(clock[1], len(sums) + 1), lambda: shares.append(Share(mem_half.at[side], mem_half.at[1 - side], mem_all, share_sems[3:6])))
        held[half] = weights(half, False)
        tick(1.4)
    wait("h1")
    grad = back[...]
    scaled, inverse = standardize(h1[...])
    small[1:2] = column_sum(grad * scaled)
    small[4:5] = column_sum(grad)
    dh[...] += standardize_back(grad, scaled, inverse, gains[1:2])
    small[2:3] = gain2[...]
    small[5:6] = bias2[...]
    small[6:8] = jnp.zeros((2, width), F32)
    low[...] = dh[...].astype(LOW)
    wait("x")
    scaled, _ = standardize(x[...].astype(F32))
    a_ref[...] = (scaled * gains[0:1] + biases[0:1]).astype(LOW)
    turned[...] = a_ref[...].T
    bias[...] = caption_bias(bias.shape[0], length)
    tick(2.5)
    group = bias.shape[0]
    wait("s", "o")
    for half, grads in enumerate((ga0, ga1)):
        for copy in held[half]:
            copy.wait()
        free(("out", half))
        out_part[half] = tn(o[half], low[...]).astype(LOW)
        put(("out", half), out_part.at[half], grads.at[3 * width : 3 * width + local])
        tick(0.5)
        dmix[...] = nt(low[...], wo[half]).astype(LOW)
        tick(0.5)
        for first in range(0, rows_all, group):
            rows = slice(first, first + group)
            for lane in range(0, local, PAIR):
                lanes = slice(lane, lane + PAIR)
                dqkv[0, rows, lanes], dqkv[1, rows, lanes], dqkv[2, rows, lanes] = attend_back(
                    s[half, 0, rows, lanes], s[half, 1, rows, lanes], s[half, 2, rows, lanes], dmix[rows, lanes], bias
                )
                tick(0.7)
        free(("wide", half))
        wide_part[half, :, :local] = nn(turned[...], dqkv[0]).astype(LOW)
        tick(0.5)
        wide_part[half, :, local:] = nn(turned[...], dqkv[1]).astype(LOW)
        put(("wide", half), wide_part.at[half], grads.at[0:width])
        tick(0.5)
        free(("thin", half))
        thin_part[half] = nn(turned[...], dqkv[2]).astype(LOW)
        put(("thin", half), thin_part.at[half], grads.at[width : 2 * width, :local])
        tick(0.5)
        more = nt(dqkv[0], wx[half, 0]) + nt(dqkv[1], wx[half, 1]) + nt(dqkv[2], wx[half, 2])
        if half == 0:
            back[...] = more
        else:
            back[...] += more
        tick(1.2)
    grad = back[...]
    scaled, inverse = standardize(x[...].astype(F32))
    small[0:1] = column_sum(grad * scaled)
    small[3:4] = column_sum(grad)
    result[...] = (dh[...] + standardize_back(grad, scaled, inverse, gains[0:1])).astype(LOW)
    put("result", result, x_o)
    while clock[1] < len(todo):
        todo[clock[1]]()
        clock[1] += 1
    for slot in list(open_parts):
        free(slot)
    ring.finish()
    for share in shares:
        share.finish()


def reduce_rest(chips, ga0, ga1, in_half, small, *refs):
    a_sum, in_all, small_sum = refs[:3]
    ring = Ring(chips, ga0, ga1, a_sum, refs[3 : 3 + RING])
    (small_core, small_pair, small_y, small_all, small_sent, small_got, round_sent, round_got, *share_sems) = refs[3 + RING :]
    ring.greet()
    ring.begin()
    small_mate = remote(small, small_core, small_sent.at[0], small_got.at[0], ring.mate)
    small_mate.start()
    small_across = remote(small_pair, small_y, small_sent.at[1], small_got.at[1], ring.y)

    def pass_small(s):
        slot = small_all.at[(ring.place + chips - s) % chips]
        return remote(slot, slot, round_sent.at[s], round_got.at[s], ring.toward[0])

    shares = []
    sums, spread = ring.steps()
    every = (len(sums) + len(spread)) // (chips + 1)
    for i, step in enumerate(sums + spread):
        step()
        small_turn, rest = divmod(i, every)
        if rest:
            pass
        elif small_turn == 0:
            small_mate.wait_recv()
            small_pair[...] = small[...] + small_core[...]
            small_across.start()
        elif small_turn == 1:
            small_across.wait_recv()
            small_all[ring.place] = small_pair[...] + small_y[...]
            pass_small(0).start()
        elif 2 <= small_turn < chips:
            pass_small(small_turn - 2).wait_recv()
            pass_small(small_turn - 1).start()
        if i == len(sums) - 1:
            shares.append(Share(in_half, in_half, in_all, share_sems))
    pass_small(chips - 2).wait_recv()
    total = small_all[0]
    for k in range(1, chips):
        total = total + small_all[k]
    small_sum[...] = total
    small_mate.wait_send()
    small_across.wait_send()
    for s in range(chips - 1):
        pass_small(s).wait_send()
    ring.finish()
    for share in shares:
        share.finish()


def unpack(
    length, order, m_sum, a_sum, y_all, x_all, out, inp, qkv, self_out, query, kv, mix, up, down,
    low, wide, acts, read_sems, write_sems, row_sems, act_sems,
):
    width = up.shape[0]
    local = self_out.shape[0]
    blocks = low.shape[0]
    reads = []
    for i in range(blocks):
        source = m_sum if i < blocks // 2 else a_sum
        row = i % (blocks // 2) * width
        copy = pltpu.make_async_copy(source.at[row : row + width], low.at[i], read_sems.at[i])
        copy.start()
        reads.append(copy)
    whole = [pltpu.make_async_copy(a, acts.at[k], act_sems.at[k]) for k, a in enumerate((y_all, x_all))]
    for copy in whole:
        copy.start()
    moves = []
    for k, target in enumerate((out, inp)):
        whole[k].wait()
        for i in range(order.shape[0]):
            rows = pl.ds(pl.multiple_of(order[i] * length, length), length)
            copy = pltpu.make_async_copy(acts.at[k, i * length : (i + 1) * length], target.at[rows], row_sems.at[k, i])
            copy.start()
            moves.append(copy)
    left, right = slice(0, local), slice(local, width)
    hidden = down.shape[0]
    targets = [[(slice(None), up.at[:, i * width : (i + 1) * width])] for i in range(hidden // width)]
    targets += [[(slice(None), down.at[i * width : (i + 1) * width])] for i in range(hidden // width)]
    targets += [
        [((slice(None), left), qkv.at[0]), ((slice(None), right), qkv.at[1])],
        [((slice(None), left), qkv.at[2]), ((slice(None), right), query)],
        [((slice(None), left), kv.at[0]), ((slice(None), right), kv.at[1])],
        [((left, slice(None)), self_out), ((right, slice(None)), mix)],
    ]
    store = Stores(write_sems)
    for i, places in enumerate(targets):
        reads[i].wait()
        wide[i] = low[i].astype(F32)
        for part, target in places:
            store(wide.at[i] if part == slice(None) else wide.at[(i, *part)], target)
    store.wait()
    for copy in moves:
        copy.wait()


def shape(dims, kind=LOW):
    return jax.ShapeDtypeStruct(dims, kind)


def call(body, name, args, outs, scratch, specs=None, out_specs=None, **params):
    return pl.pallas_call(
        body,
        out_shape=outs,
        in_specs=specs if specs is not None else [VMEM] * len(args),
        out_specs=out_specs if out_specs is not None else [VMEM] * len(outs),
        scratch_shapes=scratch,
        input_output_aliases=params.pop("aliases", {}),
        compiler_params=pltpu.CompilerParams(vmem_limit_bytes=VMEM_LIMIT, **params),
        name=name,
    )(*args)


def shards(
    chips, tokens, memory, groups, gains, biases, self_qkv, self_out, cross_query, cross_kv,
    cross_out, mlp_up, mlp_down, cotangent,
):
    captions = groups.shape[0]
    length = tokens.shape[0] // captions
    width = tokens.shape[1]
    images, span = memory.shape[:2]
    local = self_qkv.shape[2]
    hidden = mlp_up.shape[1]
    side = lax.axis_index("tensor")
    some = captions // 2 * length
    rows = images // 2 * span

    picked = groups - lax.axis_index("dp") * images
    same = picked[:, None] == picked[None, :]
    number = lax.broadcasted_iota(jnp.int32, (captions, captions), 0)
    other = lax.broadcasted_iota(jnp.int32, (captions, captions), 1)
    rank = 2 * picked + jnp.sum((same & (other < number)).astype(jnp.int32), axis=1)
    order = jnp.sum(jnp.where(rank[None, :] == number, other, 0), axis=1)
    mine = lax.dynamic_slice_in_dim(order, side * (captions // 2), captions // 2)
    source = (mine[:, None] * length + lax.broadcasted_iota(jnp.int32, (1, length), 1)).reshape(some, 1)

    part = hidden * 2
    row = shape((1, width), F32)
    group = min(some, 4 * length)
    mask = pltpu.VMEM((group, 2 * group), F32)
    dma = pltpu.SemaphoreType.DMA
    vm = pltpu.VMEM
    count = 8 + 2 * (hidden // local)
    weights = (self_qkv, self_out, cross_kv, cross_query, cross_out, mlp_up, mlp_down)
    held = [vm(w.shape, LOW) for w in weights]
    kept = [
        shape((some, width)), shape((some, width), F32), shape((2, 3, some, local)), shape((2, some, local)),
        shape((some, width)), shape((2, some, local)), shape((2, 2, rows, local)), shape((2, some, local)),
        shape((some, width)), shape((some, width)), shape((some, width), F32), shape((part, width)), shape((part, width)),
    ]
    (x, h1, s, o, c, qc, kvs, oc, cot, y_half, dh2, gm0, gm1, t_qkv, t_out, t_kv, t_query, t_mix, gain2, bias2) = call(
        functools.partial(forward, length), "forward",
        (tokens, cotangent, source, memory, gains, biases, *weights),
        kept + [shape(w.shape) for w in weights[:5]] + [row, row],
        [vm((2, *tokens.shape), LOW), vm((some, width), LOW), vm((some, width), LOW), vm((images // 2, span, width), LOW),
         vm((some, width), F32), vm((some, width), F32), vm((2, 3, some, local), LOW), vm((2, some, local), LOW),
         vm((some, width), LOW), vm((2, some, local), LOW), vm((2, 2, rows, local), LOW), vm((2, some, local), LOW),
         vm((some, width), LOW), vm((width, some), LOW), vm((some, width), F32), vm((some, width), F32),
         vm((some, width), LOW), mask, vm((some, width), LOW), vm((some, width), LOW), vm((2, 2, width, width), LOW)]
        + held + held
        + [dma((10,)), dma((16,)), dma((2, 2)), dma((9, count)), dma((9, count))],
        [ANY, ANY, VMEM, ANY, VMEM, VMEM] + [ANY] * 7, [ANY] * 18 + [VMEM] * 2,
        collective_id=0, has_side_effects=True,
    )
    attn_rows = 4 * width
    block = part // (4 * chips)
    ring = ring_shapes(chips, block, width)
    one = [dma((1,))] * 3
    ga0, ga1, m_sum, y_all, mem_all, x_half, small = call(
        functools.partial(backward, length, chips), "backward",
        (gm0, gm1, y_half, dh2, h1, memory, gains, biases, gain2, bias2, c, x, s, o, qc, kvs, oc, *weights[:5],
         t_qkv, t_out, t_kv, t_query, t_mix),
        [shape((attn_rows, width)), shape((attn_rows, width)), shape((part, width)), shape((2 * some, width)),
         shape((2 * rows, local)), shape((some, width)), shape((8, width), F32)],
        ring
        + [vm((some, width), F32), vm((some, width), F32), vm((images // 2, span, width), LOW), vm((some, width), LOW),
           vm((some, width), LOW), vm((2, 3, some, local), LOW), vm((2, some, local), LOW), vm((2, some, local), LOW),
           vm((2, 2, rows, local), LOW), vm((2, some, local), LOW), vm((2, 3, width, local), LOW), vm((2, local, width), LOW),
           vm((some, width), LOW), vm((some, width), LOW), vm((width, some), LOW), vm((some, local), LOW),
           vm((3, some, local), LOW), vm((2, rows, local), LOW), vm((some, width), F32), vm((rows, width), F32),
           vm((2, rows, local), LOW), vm((2, width, width), LOW), vm((2, width, local), LOW), vm((2, local, width), LOW),
           mask, vm((some, width), LOW), dma((10,)), dma((2, 2, 3)), dma((16,))]
        + one + one,
        [ANY] * 6 + [VMEM] * 4 + [ANY] * 17, [ANY] * 6 + [VMEM],
        collective_id=1, has_side_effects=True,
    )
    a_sum, x_all, small_sum = call(
        functools.partial(reduce_rest, chips), "reduce_rest", (ga0, ga1, x_half, small),
        [shape((attn_rows, width)), shape((2 * some, width)), shape((8, width), F32)],
        ring + [vm((8, width), F32)] * 3 + [vm((chips, 8, width), F32)] + [dma((2,))] * 2 + [dma((chips - 1,))] * 2 + one,
        [ANY] * 3 + [VMEM], [ANY, ANY, VMEM], collective_id=2, has_side_effects=True,
    )
    blocks = 2 * hidden // width + 4
    smem = pl.BlockSpec(memory_space=pltpu.SMEM)
    (output, input_grad, qkv_grad, out_grad, query_grad, kv_grad, mix_grad, up_grad, down_grad) = call(
        functools.partial(unpack, length), "unpack", (order, m_sum, a_sum, y_all, x_all),
        [shape(tokens.shape), shape(tokens.shape), shape(self_qkv.shape, F32), shape(self_out.shape, F32),
         shape(cross_query.shape, F32), shape(cross_kv.shape, F32), shape(cross_out.shape, F32),
         shape(mlp_up.shape, F32), shape(mlp_down.shape, F32)],
        [pltpu.VMEM((blocks, width, width), LOW), pltpu.VMEM((blocks, width, width), F32), pltpu.VMEM((2, *tokens.shape), LOW),
         dma((blocks,)),         dma((2 * blocks,)), dma((2, captions)), dma((2,))],
        [smem] + [ANY] * 4, [ANY] * 9,
    )
    return (
        output, input_grad, mem_all.reshape(images, span, local), small_sum[:3], small_sum[3:6], qkv_grad, out_grad,
        query_grad, kv_grad, mix_grad, up_grad, down_grad,
    )


def solution(mesh):
    rows = P("dp", None)
    columns = P(None, "tensor")
    stacked = P(None, None, "tensor")
    halves = P("tensor", None)
    return jax.shard_map(
        functools.partial(shards, mesh.shape["dp"] // 2),
        mesh=mesh,
        in_specs=(rows, P("dp", None, None), P("dp"), P(), P(), stacked, halves, columns, stacked, halves, columns, halves, rows),
        out_specs=(
            rows, rows, P("dp", None, "tensor"), P(), P(), stacked, halves, columns, stacked, halves, columns, halves,
        ),
        check_vma=False,
    )
```
